32 devices in a mesh: scen: 2 (over y), tile: 4 (over z), col: 2 (over x), sub: 2 (over core).
Axes of the slice: x: 2, y: 2, z: 4, core: 2. Of those that a mesh axis runs over, the one named last changes fastest.
Arguments:
- green: bfloat16 [4096, 512], P(('tile', 'col', 'sub')), may hold values from -5 to 5
- row_owner: int32 [4096, 1], P(('tile', 'col', 'sub')), may hold values from 0 to 15; in each aligned block of 256 rows (0 to 255, 256 to 511, ...) at most 32 rows name the same one
- row_index: int32 [4096], P(('tile', 'col', 'sub')), may hold values from 0 to 63
- row_fault: int32 [4096], P(('tile', 'col', 'sub')), may hold values from 0 to 15
- slip: float32 [512], P(('scen', 'tile', 'col', 'sub')), parts along dimension 0, may hold values from 0.3 to 3
- depth: float32 [256, 2048], P('tile', ('col', 'sub')), may hold values from 0.2 to 1.6
- wet: int32 [256, 2048], P('tile', ('col', 'sub')), may hold values 0 or 1
- coarse_depth: float32 [256, 512], P('tile', ('col', 'sub')), may hold values from 0.5 to 3
- coarse_start: float32 [512, 512], P(('scen', 'tile'), ('col', 'sub')), parts along dimension 0, may hold values from -6 to 6
Outputs:
- peak_level: float32 [512, 2048], P(('scen', 'tile'), ('col', 'sub')), parts along dimension 0
- surface: float32 [512, 2048], P(('scen', 'tile'), ('col', 'sub')), parts along dimension 0
- coarse_surface: float32 [512, 512], P(('scen', 'tile'), ('col', 'sub')), parts along dimension 0
The draws below stay inside these ranges and needn't reach their ends.
There are 2 independent parts, one for each index of `scen`. The reference program is written for one: setup_inputs(seed, part) draws one part's arguments, and reference() takes and returns one part's arrays. A program takes and returns all parts, laid end to end along the dimension named above; an argument that names none is the same for every part. Nothing has to cross between parts.
Inputs may be any that keep to these rules, and one draw needn't show every extreme that they name: `row_owner`: in the rows of one device no fine tile is named more than 32 times; in some device's rows a tile is named exactly 32 times.
All inputs are finite; a program needn't handle non-finite values. No bound on the sum of `wet` on one device may be relied on, other than what follows from the above.
Results may differ from the reference program's by a relative error of at most 0.0075.
Values may be sent and summed in bfloat16 or wider, within the bound.
A program may use at most 64 MiB of HBM per device.

```python
import math
import jax
import jax.numpy as jnp
import numpy as np

FR = 64
FC = 512
E_DEV = 256
S_DEV = 16
RATIO = 4
STEPS = 6
SIDES = 4
FTILES = 16
CAP = 32
NFR = 256
NFC = 2048
NCR = 256
NCC = 512
NB = 64
SUBROWS = 4096
SUBFAULTS = 256


def place_ends(drawn, stream_key, low, top_value):
    spot = [jax.random.randint(jax.random.fold_in(stream_key, axis), (), 0, length) for axis, length in enumerate(drawn.shape)]
    longest = drawn.shape.index(max(drawn.shape))
    beside = spot[:longest] + [(spot[longest] + 1) % drawn.shape[longest]] + spot[longest + 1:]
    return drawn.at[tuple(spot)].set(low).at[tuple(beside)].set(top_value)


def block_scale(own_key, shape, pieces, low, high):
    level, own = 1.0, jax.random.fold_in(own_key, 6)
    for dim, shards_of in pieces:
        draws = jnp.exp(jax.random.uniform(jax.random.fold_in(own, dim), (shards_of,), jnp.float32, low / len(pieces), high / len(pieces)))
        level = level * jnp.repeat(draws, shape[dim] // shards_of).reshape([-1 if axis == dim else 1 for axis in range(len(shape))])
    return level


def assign_block(rng, own, number, rows, count, top, reach, lean):
    sequence = jax.random.permutation(rng, count)
    packed, usual = shares(count, rows * top, reach, lean, True), shares(count, rows * top, reach, lean, False)
    places = jnp.arange(count)

    def named(lengths, rotation):
        used = int((lengths > 0).sum())
        fixed = max(1, used // 4)
        passed = fixed + (places - fixed + rotation * (used - fixed)) % max(1, count - fixed)
        return jnp.zeros((count,), jnp.int32).at[sequence[jnp.where(places < fixed, places, passed)]].set(jnp.asarray(lengths, jnp.int32))

    lengths = jnp.where(number % 4 == 0, named(packed, number // 4), named(usual, number - number // 4 - 1))
    mixed = jax.random.permutation(jax.random.fold_in(own, 3), count)
    source_of, taker = mixed[0:count // 2 * 2:2], mixed[1:count // 2 * 2:2]
    room = jnp.minimum(lengths[source_of] - 1, reach - lengths[taker]) // 2
    room = jnp.where((source_of == sequence[0]) | (taker == sequence[0]) | (lengths[taker] == 0), 0, jnp.maximum(room, 0))
    passed = jax.random.randint(jax.random.fold_in(own, 4), (count // 2,), 0, 1 << 20) % (room + 1)
    lengths = lengths.at[source_of].add(-passed).at[taker].add(passed)
    items = jnp.searchsorted(jnp.cumsum(lengths), jnp.arange(rows * top), side="right").astype(jnp.int32)
    listing = items.reshape(top, rows).T
    listing = listing[jax.random.permutation(jax.random.fold_in(own, 1), rows)]
    rotation = jax.random.randint(jax.random.fold_in(own, 2), (rows, 1), 0, top)
    return jnp.take_along_axis(listing, (jnp.arange(top)[None, :] + rotation) % top, axis=1)


def shares(count, total, bound, skew, full):
    portions = [(1 << 20) // math.isqrt(rank ** skew) + 1 for rank in range(1, count + 1)]
    largest = bound if full else min(bound, max(-(-total // count), total * portions[0] // sum(portions)))
    least = 1 if total - largest >= count - 1 else 0
    counts, surplus = [largest] + [least] * (count - 1), total - largest - least * (count - 1)
    while surplus > 0:
        candidates = [i for i in range(1, count) if counts[i] < largest] or [i for i in range(1, count) if counts[i] < bound]
        mass, left = sum([portions[i] for i in candidates]), surplus
        for i in candidates:
            more = min(bound - counts[i], max(1, left * portions[i] // mass), surplus)
            counts[i] = counts[i] + more
            surplus = surplus - more
    return np.array(counts)


def scatter_about(rng, dims, scale, bound, cuts=(), kind=jnp.bfloat16):
    drawn = jax.random.normal(rng, dims, jnp.float32) * scale
    if len(cuts) > 0:
        drawn = block_scale(rng, dims, cuts, -0.22, 0.18) * drawn
    return jnp.clip(drawn, min=-bound, max=bound).astype(kind)


def setup_inputs(seed: int = 0, part: int = 0) -> dict:
    arg_keys = jax.random.split(jax.random.key(seed), 10)
    part_splits = jax.random.split(jax.random.fold_in(arg_keys[9], part), 10)
    green = scatter_about(arg_keys[0], (SUBROWS, FC), 0.35, 5.0, ((0, 16),))
    row_owner_keys = jax.random.split(jax.random.fold_in(arg_keys[1], 1), SUBROWS // E_DEV)
    row_owner_turns = jax.random.permutation(jax.random.fold_in(arg_keys[1], 3), SUBROWS // E_DEV)
    row_owner = jax.vmap(lambda own, number: assign_block(jax.random.fold_in(arg_keys[1], 2), own, number, E_DEV, FTILES, 1, CAP, 1))(row_owner_keys, row_owner_turns).reshape((SUBROWS, 1))
    row_index = place_ends(jax.random.randint(arg_keys[2], (SUBROWS,), 0, FR), jax.random.fold_in(arg_keys[2], 1), 0, FR - 1).astype(jnp.int32)
    row_fault = place_ends(jax.random.randint(arg_keys[3], (SUBROWS,), 0, S_DEV), jax.random.fold_in(arg_keys[3], 1), 0, S_DEV - 1).astype(jnp.int32)
    slip = jnp.clip(jnp.exp(math.log(3.0) - 2.3025851 * jax.random.uniform(part_splits[4], (SUBFAULTS,), jnp.float32) ** block_scale(part_splits[4], (SUBFAULTS,), ((0, 16),), -0.2, 0.2)), 0.3, 3.0)
    depth = jnp.clip(jnp.exp(math.log(1.6) - 2.0794415 * jax.random.uniform(arg_keys[5], (NFR, NFC), jnp.float32) ** block_scale(arg_keys[5], (NFR, NFC), ((0, 4), (1, 4)), -0.2, 0.2)), 0.2, 1.6)
    wet = place_ends((jax.random.randint(arg_keys[6], (NFR, NFC), 0, 5) < 4).astype(jnp.int32), jax.random.fold_in(arg_keys[6], 1), 0, 1)
    coarse_depth = jnp.clip(jnp.exp(math.log(3.0) - 1.7917595 * jax.random.uniform(arg_keys[7], (NCR, NCC), jnp.float32) ** block_scale(arg_keys[7], (NCR, NCC), ((0, 4), (1, 4)), -0.2, 0.2)), 0.5, 3.0)
    coarse_start = scatter_about(part_splits[8], (NCR, NCC), 1.0, 6.0, ((0, 4), (1, 4)), jnp.float32)
    return dict(green=green, row_owner=row_owner, row_index=row_index, row_fault=row_fault, slip=slip, depth=depth, wet=wet, coarse_depth=coarse_depth, coarse_start=coarse_start)


flux_coef = 0.5
level_coef = 0.5


def face_depths(padded):
    west_cells = padded[1:-1, :-1]
    east_cells = padded[1:-1, 1:]
    depth_cols = jnp.where((west_cells > 0.0) & (east_cells > 0.0), 0.5 * (west_cells + east_cells), 0.0)
    north_cells = padded[:-1, 1:-1]
    south_cells = padded[1:, 1:-1]
    depth_rows = jnp.where((north_cells > 0.0) & (south_cells > 0.0), 0.5 * (north_cells + south_cells), 0.0)
    return depth_cols, depth_rows


def advance(level_pad, flow_cols_ext, flow_rows_ext, level, depth_cols, depth_rows, flux_step, level_step):
    flow_cols = flow_cols_ext - flux_step * depth_cols * (level_pad[1:-1, 1:] - level_pad[1:-1, :-1])
    flow_rows = flow_rows_ext - flux_step * depth_rows * (level_pad[1:, 1:-1] - level_pad[:-1, 1:-1])
    level = level - level_step * ((flow_cols[:, 1:] - flow_cols[:, :-1]) + (flow_rows[1:] - flow_rows[:-1]))
    return level, flow_cols[:, :-1], flow_rows[:-1]


def reference(green, row_owner, row_index, row_fault, slip, depth, wet, coarse_depth, coarse_start):
    destination = row_owner[:, 0]
    source_device = jnp.arange(SUBROWS, dtype=jnp.int32) // E_DEV
    fault_index = source_device * S_DEV + row_fault
    factor = slip[fault_index]
    uplift_rows = green.astype(jnp.float32) * factor[:, None]
    global_rows = (destination // SIDES) * FR + row_index
    global_tiles = destination % SIDES
    uplift = jnp.zeros((NFR, SIDES, FC), jnp.float32).at[global_rows, global_tiles].add(uplift_rows)
    surface = uplift.reshape(NFR, NFC)

    effective = jnp.where(wet > 0, depth, 0.0)
    bordered = jnp.concatenate([depth[0:1], effective, jnp.zeros((1, NFC), jnp.float32)], axis=0)
    bordered = jnp.pad(bordered, ((0, 0), (1, 1)))
    depth_cols, depth_rows = face_depths(bordered)
    coarse_cols, coarse_rows = face_depths(jnp.pad(coarse_depth, 1))

    peak_level = surface
    flow_cols = jnp.zeros((NFR, NFC), jnp.float32)
    flow_rows = jnp.zeros((NFR, NFC), jnp.float32)
    coarse_surface = coarse_start
    coarse_east = jnp.zeros((NCR, NCC), jnp.float32)
    coarse_south = jnp.zeros((NCR, NCC), jnp.float32)
    for step_index in range(STEPS):
        averages = surface.reshape(NB, RATIO, NCC, RATIO).mean(axis=(1, 3))
        coarse_surface = jnp.concatenate([coarse_surface[0:1], averages, coarse_surface[NB + 1:]], axis=0)
        ghost_row = jnp.repeat(coarse_surface[0], RATIO)
        level_pad = jnp.pad(surface, 1).at[0, 1:-1].set(ghost_row)
        cols_ext = jnp.pad(flow_cols, ((0, 0), (0, 1)))
        rows_ext = jnp.pad(flow_rows, ((0, 1), (0, 0)))
        surface, flow_cols, flow_rows = advance(level_pad, cols_ext, rows_ext, surface, depth_cols, depth_rows, flux_coef, level_coef)
        peak_level = jnp.maximum(peak_level, surface)
        coarse_pad = jnp.pad(coarse_surface, 1)
        east_ext = jnp.pad(coarse_east, ((0, 0), (0, 1)))
        south_ext = jnp.pad(coarse_south, ((0, 1), (0, 0)))
        coarse_surface, coarse_east, coarse_south = advance(coarse_pad, east_ext, south_ext, coarse_surface, coarse_cols, coarse_rows, flux_coef / RATIO, level_coef / RATIO)
    return (peak_level, surface, coarse_surface)
```

```python
import functools
import jax
import jax.numpy as jnp
from jax import lax
from jax.experimental import pallas as pl
from jax.experimental.pallas import tpu as pltpu
from jax.sharding import PartitionSpec as P

RATIO = 4
STEPS = 6
HALO = 8
LEAD = 16
F32 = jnp.float32
BF16 = jnp.bfloat16
MESH = pl.DeviceIdType.MESH


def split2(x):
    high = x.astype(BF16).astype(F32)
    return high, (x - high).astype(BF16).astype(F32)


def iota(shape, dim):
    return lax.broadcasted_iota(jnp.int32, shape, dim)


def kernel(
    dims,
    green_h, owner_h, index_h, fault_h, slip_h, depth_h, wet_h, cdep_h, cstart_h,
    peak_o, surf_o, coarse_o,
    green, owner, index, fault, slip, depth, wet, chosen_r,
    place, send, recv, msend, mrecv, slip_s, slip_r, acc,
    zs, zside, zvert, zcorn,
    half, hcore, hside, hvert, hcorn,
    lev, held, gc, gr, kc, kr,
    clev, cheld, cgc, cgr, ckc, ckr,
    amat, rmat, work, total, avgs, avgr, esum, edges, edger,
    i_s, a_ss, a_rs, m_ss, m_rs, sl_s, z_ss, z_rs, h_ss, h_rs, v_ss, v_rs,
):
    planes, tiles, cols_n, subs_n = dims
    sides = cols_n * subs_n
    owners = tiles * sides
    plane = lax.axis_index("scen")
    tile = lax.axis_index("tile")
    side = lax.axis_index("col") * subs_n + lax.axis_index("sub")
    me = tile * sides + side
    rows, cols = depth.shape
    crows, ccols = cdep_h.shape
    entries, hw = green.shape
    capp = send.shape[1]
    pack = 128 // capp
    packs = owners // pack
    fw = cols + 128
    cw = ccols + 128
    top = LEAD + rows

    def dev(p, t, c):
        return {"scen": p, "tile": t, "col": c // subs_n, "sub": c % subs_n}

    def fetch(i):
        lanes = pl.ds(pl.multiple_of(plane * hw, 128), hw)
        far = 256 + cols
        src, dst = [
            (owner_h, owner), (green_h.at[:, lanes], green), (index_h, index), (fault_h, fault),
            (slip_h, slip), (depth_h, depth), (wet_h, wet),
            (cdep_h, zs.at[0:rows, 0:ccols]), (cstart_h, zs.at[0:rows, 128 : 128 + ccols]),
            (cdep_h, zs.at[0:rows, far : far + ccols]),
            (cstart_h, zs.at[0:rows, far + 128 : far + 128 + ccols]),
        ][i]
        return pltpu.make_async_copy(src, dst, i_s.at[i])

    for i in range(11):
        fetch(i).start()

    barrier = pltpu.get_barrier_semaphore()

    def greet(i, carry):
        d = lax.rem(me + i, owners)
        pl.semaphore_signal(
            barrier, inc=1, device_id=dev(plane, d // sides, lax.rem(d, sides)),
            device_id_type=MESH,
        )
        return carry

    lax.fori_loop(1, owners, greet, 0)
    beside = side + 2 * plane - 1
    at_side = jnp.logical_and(beside >= 0, beside < sides)
    at_up, at_down = tile > 0, tile < tiles - 1
    cross = [(0, side, True), (-1, side, at_up), (1, side, at_down), (0, beside, at_side)] + [
        (dy, beside, jnp.logical_and(ok, at_side)) for dy, ok in ((-1, at_up), (1, at_down))
    ]
    greeted = owners - 1
    for dy, c, ok in cross:
        greeted = greeted + jnp.where(ok, 1, 0)
        pl.when(ok)(
            lambda dy=dy, c=c: pl.semaphore_signal(
                barrier, inc=1, device_id=dev(planes - 1 - plane, tile + dy, c),
                device_id_type=MESH,
            )
        )

    fetch(0).wait()
    dest = owner[...]
    hit = iota((owners, entries), 0) == dest
    before = (iota((entries, entries), 0) < iota((entries, entries), 1)).astype(F32).astype(BF16)
    rank = jnp.dot(hit.astype(F32).astype(BF16), before, preferred_element_type=F32)
    place[...] = jnp.where(hit, rank, -1.0)
    group = min(owners, 512 // capp)
    groups = owners // group
    fetch(1).wait()
    gh = green[...]
    slots = iota((group, capp, entries), 1).astype(F32)

    def select(g):
        rows_of = place[pl.ds(pl.multiple_of(g * group, group), group), :]
        chosen = jnp.where(rows_of[:, None, :] == slots, 1.0, 0.0)
        chosen = chosen.reshape(group * capp, entries).astype(BF16)
        chosen_r[pl.ds(g * group * capp, group * capp), :] = chosen
        return chosen

    def fill(g, carry):
        picked = jnp.dot(select(g), gh, preferred_element_type=F32).astype(BF16)
        send[pl.ds(g * group, group)] = picked.reshape(group, capp, hw)
        return carry

    fill(0, 0) if groups == 1 else lax.fori_loop(0, groups, fill, 0)

    for i in range(2, 11):
        fetch(i).wait()
    slip_s[...] = jnp.zeros_like(slip_s)
    slip_s[0:1, 0 : slip.shape[1]] = slip[...]
    raw = depth[...]
    zs[0:rows, 256 : 256 + cols] = jnp.where(wet[...] > 0, raw, 0.0)
    zs[rows : rows + 8, 256 : 256 + cols] = jnp.broadcast_to(raw[0:1], (8, cols))
    for off in (0, 256 + cols):
        zs[rows : rows + 8, off : off + 256] = jnp.zeros((8, 256), F32)

    pl.semaphore_wait(barrier, greeted)

    other = planes - 1 - plane
    slip_copy = pltpu.make_async_remote_copy(
        src_ref=slip_s, dst_ref=slip_r, send_sem=sl_s.at[0], recv_sem=sl_s.at[1],
        device_id=dev(other, tile, side), device_id_type=MESH,
    )
    slip_copy.start()

    def pair_copy(src, dst, s_sem, r_sem, d):
        return pltpu.make_async_remote_copy(
            src_ref=src, dst_ref=dst, send_sem=s_sem, recv_sem=r_sem,
            device_id=dev(plane, d // sides, lax.rem(d, sides)), device_id_type=MESH,
        )

    def a2a(d):
        return pair_copy(send.at[d], recv.at[me], a_ss.at[0], a_rs.at[me // pack], d)

    def a2a_meta(d):
        return pair_copy(msend.at[d // pack], mrecv.at[me], m_ss.at[0], m_rs.at[me // pack], d)

    def a2a_wait(g, n):
        first = pl.ds(g * pack, n)
        pair_copy(recv.at[first], recv.at[first], a_ss.at[0], a_rs.at[g], me).wait_recv()
        pair_copy(mrecv.at[first], mrecv.at[first], m_ss.at[0], m_rs.at[g], me).wait_recv()

    def turn(i):
        return lax.rem(me + lax.rem(i + owners // 2 - 1, owners - 1) + 1, owners)

    def launch(i, carry):
        a2a(turn(i)).start()
        return carry

    lax.fori_loop(0, owners - 1, launch, 0)

    moves = [(0, -1), (0, 1), (-1, 0), (1, 0), (-1, -1), (-1, 1), (1, -1), (1, 1)]

    def static_copy(i):
        dy, dx = moves[i]
        lanes = (
            slice(0, 512 - 128) if dx == -1
            else slice(cols + 128, cols + 512) if dx == 1 else slice(0, 256 + cols)
        )
        sel = slice(0, rows + 8) if dy == 0 else slice(0, 8) if dy == -1 else slice(rows - 8, rows)
        bi = 0 if dy == -1 else 1
        bj = 0 if dx == -1 else 1
        dst = zside.at[bj] if dy == 0 else zvert.at[bi] if dx == 0 else zcorn.at[bi, bj]
        return pltpu.make_async_remote_copy(
            src_ref=zs.at[sel, lanes], dst_ref=dst, send_sem=z_ss.at[i], recv_sem=z_rs.at[i],
            device_id=dev(plane, tile + dy, side + dx), device_id_type=MESH,
        )

    def inside(dy, dx):
        ok = True
        for at, by, size in ((tile, dy, tiles), (side, dx, sides)):
            if by == -1:
                ok = jnp.logical_and(ok, at > 0)
            if by == 1:
                ok = jnp.logical_and(ok, at < size - 1)
        return ok

    for i, (dy, dx) in enumerate(moves):
        pl.when(inside(dy, dx))(lambda i=i: static_copy(i).start())

    slip_copy.wait()

    mrow = iota((8, slip.shape[1]), 0)
    own_h, own_l = split2(slip[...])
    oth_h, oth_l = split2(slip_r[0:1, 0 : slip.shape[1]])
    parts = jnp.where(mrow == 1, own_h, 0.0)
    for i, part in ((2, own_l), (3, oth_h), (4, oth_l)):
        parts = jnp.where(mrow == i, part, parts)
    picks = (iota((slip.shape[1], entries), 0) == fault[...]).astype(F32).astype(BF16)
    meta = jnp.dot(parts.astype(BF16), picks, preferred_element_type=F32)
    meta = jnp.where(iota((8, entries), 0) == 0, index[...].astype(F32), meta).astype(BF16)

    def describe(g, carry):
        told = lax.dot_general(
            meta, chosen_r[pl.ds(g * group * capp, group * capp), :], (((1,), (1,)), ((), ())), preferred_element_type=F32
        )
        for i in range(group // pack):
            msend[g * (group // pack) + i] = told[:, i * 128 : (i + 1) * 128].astype(BF16)
        return carry

    describe(0, 0) if groups == 1 else lax.fori_loop(0, groups, describe, 0)

    def launch_meta(i, carry):
        a2a_meta(turn(i)).start()
        return carry

    lax.fori_loop(0, owners - 1, launch_meta, 0)


    fl = iota((fw, cw), 0)
    fmap = jnp.where(fl < cols + 64, fl // RATIO, fl // RATIO + (cw - fw // RATIO))
    amat[...] = jnp.where(fmap == iota((fw, cw), 1), 1.0 / (RATIO * RATIO), 0.0).astype(BF16)
    rl = iota((cw, fw), 1)
    rmap = jnp.where(rl < cols + 64, rl // RATIO, rl // RATIO + (cw - fw // RATIO))
    rmat[...] = jnp.where(rmap == iota((cw, fw), 0), 1.0, 0.0).astype(BF16)
    for ref in (lev, held, gc, gr, clev, cheld, cgc, cgr):
        ref[...] = jnp.zeros_like(ref)
    acc[...] = jnp.zeros_like(acc)

    for bj in range(2):
        dx = 1 if bj == 0 else -1
        @pl.when(jnp.logical_not(inside(0, dx)))
        def _(bj=bj):
            zside[bj] = jnp.zeros(zside.shape[1:], F32)
        for bi in range(2):
            dy = 1 if bi == 0 else -1
            @pl.when(jnp.logical_not(inside(dy, dx)))
            def _(bi=bi, bj=bj):
                zcorn[bi, bj] = jnp.zeros(zcorn.shape[2:], F32)
    for bi in range(2):
        dy = 1 if bi == 0 else -1
        @pl.when(jnp.logical_not(inside(dy, 0)))
        def _(bi=bi):
            zvert[bi] = jnp.zeros(zvert.shape[1:], F32)
    wrow = iota((4 * rows, 128), 0)
    in_tile = lax.rem(wrow, rows).astype(F32)
    mlane = iota((8, 128), 1)
    recv[me] = send[me]
    mrecv[me] = msend[me // pack]

    def put(g):
        told = jnp.zeros((8, 128), F32)
        for j in range(pack):
            moved = pltpu.roll(
                mrecv[g * pack + j].astype(F32), lax.rem(j + pack - lax.rem(me, pack), pack) * capp, 1
            )
            told = jnp.where((mlane >= j * capp) & (mlane < (j + 1) * capp), moved, told)
        weight = jnp.where(
            wrow < rows, told[1:2],
            jnp.where(wrow < 2 * rows, told[3:4], jnp.where(wrow < 3 * rows, told[2:3], told[4:5])),
        )
        weight = jnp.where(in_tile == told[0:1], weight, 0.0).astype(BF16)
        block = recv[pl.ds(g * pack, pack)].reshape(128, hw)
        acc[...] += jnp.dot(weight, block, preferred_element_type=F32)

    mine = me // pack

    def take(i, carry):
        g = lax.rem(mine + i, packs)
        a2a_wait(g, pack)
        put(g)
        return carry

    a2a_wait(mine, pack - 1)
    put(mine)
    lax.fori_loop(1, packs, take, 0, unroll=packs == 4)
    half[...] = acc[0 : 2 * rows, :] + acc[2 * rows : 4 * rows, :]

    toward = 2 * plane - 1

    def core_copy():
        return pltpu.make_async_remote_copy(
            src_ref=half.at[rows : 2 * rows, :], dst_ref=hcore, send_sem=h_ss.at[0],
            recv_sem=h_rs.at[0], device_id=dev(other, tile, side), device_id_type=MESH,
        )

    edge = pl.ds(pl.multiple_of(plane * (hw - 128), 128), 128)

    def halo_copy(s, kind, v, q):
        to_plane = plane if s == 0 else other
        dy = 0 if kind == 0 else (-1 if v == 0 else 1)
        r0 = s * rows + (0 if v == 0 else rows - 8)
        if kind == 0:
            src, dst, n = half.at[s * rows : (s + 1) * rows, edge], hside.at[q], 0
        elif kind == 1:
            src, dst, n = half.at[r0 : r0 + 8, :], hvert.at[v, q], 1 + v
        else:
            src, dst, n = half.at[r0 : r0 + 8, edge], hcorn.at[v, q], 3 + v
        return pltpu.make_async_remote_copy(
            src_ref=src, dst_ref=dst, send_sem=h_ss.at[1 + 5 * s + n], recv_sem=h_rs.at[1 + n + 5 * q],
            device_id=dev(to_plane, tile + dy, side if kind == 1 else side + toward),
            device_id_type=MESH,
        )

    kinds = [(1, 0), (1, 1), (0, 0), (2, 0), (2, 1)]

    def goes(kind, v, sign):
        dy = 0 if kind == 0 else (-1 if v == 0 else 1) * sign
        ok = inside(dy, 0)
        if kind != 1:
            to = side + toward
            ok = jnp.logical_and(ok, jnp.logical_and(to >= 0, to < sides))
        return ok

    core_copy().start()
    for s in (1, 0):
        for kind, v in kinds:
            pl.when(goes(kind, v, 1))(
                lambda s=s, kind=kind, v=v: halo_copy(s, kind, v, plane).start()
            )

    def comes(kind, v, q):
        dy = 0 if kind == 0 else (1 if v == 0 else -1)
        dx = 0 if kind == 1 else (1 if q == 0 else -1)
        return inside(dy, dx)

    for i, (dy, dx) in enumerate(moves):
        pl.when(inside(-dy, -dx))(lambda i=i: static_copy(i).wait_recv())

    def merge(right, left):
        return jnp.where(iota(right.shape, right.ndim - 1) < 64, right, left)

    def place_static(r0, n, z, zr, zl, sr):
        held[r0 : r0 + n, 0:cols] = z[sr, 256 : 256 + cols]
        held[r0 : r0 + n, cols:fw] = merge(zr[sr, 256:384], zl[sr, 0:128])
        cheld[r0 : r0 + n, 0:ccols] = z[sr, 0:128]
        cheld[r0 : r0 + n, ccols:cw] = merge(zr[sr, 0:128], zl[sr, 128:256])
        clev[r0 : r0 + n, 0:ccols] = z[sr, 128:256]
        clev[r0 : r0 + n, ccols:cw] = merge(zr[sr, 128:256], zl[sr, 256:384])

    place_static(LEAD, rows, zs, zside.at[0], zside.at[1], slice(0, rows))
    place_static(top, 8, zvert.at[0], zcorn.at[0, 0], zcorn.at[0, 1], slice(0, 8))
    place_static(8, 8, zvert.at[1], zcorn.at[1, 0], zcorn.at[1, 1], slice(0, 8))

    @pl.when(tile == 0)
    def _():
        held[LEAD - 1 : LEAD, 0:cols] = depth[0:1, :]
        held[LEAD - 1 : LEAD, cols:fw] = merge(
            zside[0, rows : rows + 1, 256:384], zside[1, rows : rows + 1, 0:128]
        )

    strips = [8 + 8 * i for i in range((rows + 16) // 8)]
    cstrips = [8 + 8 * i for i in range((crows + 16) // 8)]

    def faces(h, k_c, k_r, scale, which):
        width = h.shape[1]
        for b in which:
            here, up = h[b : b + 8, :], h[b - 1 : b + 7, :]
            west = pltpu.roll(here, 1, 1)
            k_c[b : b + 8, :] = jnp.where((here > 0.0) & (west > 0.0), scale * (here + west), 0.0)
            k_r[b : b + 8, :] = jnp.where((here > 0.0) & (up > 0.0), scale * (here + up), 0.0)

    faces(held, kc, kr, 0.5 * 0.5 * 0.5, strips)
    faces(cheld, ckc, ckr, 0.5 * 0.125 * 0.125, cstrips)

    for q in range(2):
        for kind, v in kinds:
            dst = hside.at[q] if kind == 0 else hvert.at[v, q] if kind == 1 else hcorn.at[v, q]
            @pl.when(jnp.logical_not(comes(kind, v, q)))
            def _(dst=dst):
                dst[...] = jnp.zeros(dst.shape, F32)
            pl.when(comes(kind, v, q))(
                lambda kind=kind, v=v, q=q: halo_copy(0, kind, v, q).wait_recv()
            )
    core_copy().wait_recv()

    lev[LEAD:top, pl.ds(pl.multiple_of(plane * hw, 128), hw)] = half[0:rows, :]
    lev[LEAD:top, pl.ds(pl.multiple_of(other * hw, 128), hw)] = hcore[...]
    lev[LEAD:top, cols:fw] = merge(hside[0], hside[1])
    for v, r0 in ((0, top), (1, 8)):
        lev[r0 : r0 + 8, 0:hw] = hvert[v, 0]
        lev[r0 : r0 + 8, hw:cols] = hvert[v, 1]
        lev[r0 : r0 + 8, cols:fw] = merge(hcorn[v, 0], hcorn[v, 1])
    peak_o[...] = lev[LEAD:top, 0:cols]
    total[...] = lev[LEAD:top, :]

    brows = rows // RATIO
    per = crows * RATIO // rows
    nest = brows * tiles
    nested = nest // crows
    ct = tile // per
    cm = lax.rem(tile, per)

    def avg_copy(k, kind):
        if kind == 0:
            src, to = avgs.at[k], ct
            dst = avgr.at[k, pl.ds(pl.multiple_of(LEAD + cm * brows, 8), brows), :]
        elif kind == 1:
            src, to = avgs.at[k, brows - 8 : brows, :], ct + 1
            dst = avgr.at[k, 8:16, :]
        else:
            src, to = avgs.at[k, 0:8, :], ct - 1
            dst = avgr.at[k, LEAD + crows : LEAD + crows + 8, :]
        return pltpu.make_async_remote_copy(
            src_ref=src, dst_ref=dst, send_sem=v_ss.at[k, kind], recv_sem=v_rs.at[k, kind],
            device_id=dev(plane, to, side), device_id_type=MESH,
        )

    def avg_goes(kind):
        if kind == 0:
            return tile > 0
        if kind == 1:
            return jnp.logical_and(cm == per - 1, ct + 1 < nested)
        return jnp.logical_and(cm == 0, ct > 0)

    def avg_send(k):
        for kind in range(3):
            pl.when(avg_goes(kind))(lambda kind=kind: avg_copy(k, kind).start())

    def avg_wait(k):
        def wait(kind, dst):
            pltpu.make_async_remote_copy(
                src_ref=dst, dst_ref=dst, send_sem=v_ss.at[k, kind], recv_sem=v_rs.at[k, kind],
                device_id=dev(plane, tile, side), device_id_type=MESH,
            ).wait_recv()

        pl.when(tile == 0)(lambda: wait(0, avgr.at[k, LEAD + brows : LEAD + per * brows, :]))
        pl.when(tile > 0)(lambda: wait(0, avgr.at[k, LEAD : LEAD + per * brows, :]))
        pl.when(tile > 0)(lambda: wait(1, avgr.at[k, 8:16, :]))
        pl.when(tile < nested - 1)(lambda: wait(2, avgr.at[k, LEAD + crows : LEAD + crows + 8, :]))

    def edge_copy():
        return pltpu.make_async_remote_copy(
            src_ref=edges, dst_ref=edger, send_sem=v_ss.at[2, 0], recv_sem=v_rs.at[2, 0],
            device_id=dev(plane, nested, side), device_id_type=MESH,
        )

    ends = nested < tiles
    is_last = tile == tiles - 1

    def push(s_ref, g_c, g_r, k_c, k_r, which):
        for b in which:
            here, up = s_ref[b : b + 8, :], s_ref[b - 1 : b + 7, :]
            g_c[b : b + 8, :] -= k_c[b : b + 8, :] * (here - pltpu.roll(here, 1, 1))
            g_r[b : b + 8, :] -= k_r[b : b + 8, :] * (here - up)

    def spread(g_c, g_r, b):
        east = g_c[b : b + 8, :]
        return (pltpu.roll(east, east.shape[1] - 1, 1) - east) + (
            g_r[b + 1 : b + 9, :] - g_r[b : b + 8, :]
        )

    def means(x):
        high, low = split2(x)
        return jnp.dot(high.astype(BF16), amat[...], preferred_element_type=F32) + jnp.dot(
            low.astype(BF16), amat[...], preferred_element_type=F32
        )

    def block_means(k, x):
        sums = means(x)
        for j in range(cw // 128):
            work[j] = sums[:, j * 128 : (j + 1) * 128]
            avgs[k, :, j * 128 : (j + 1) * 128] = sum(
                work[j, pl.ds(i, brows, stride=RATIO), :] for i in range(RATIO)
            )
        avg_send(k)

        @pl.when(tile == 0)
        def _():
            avgr[k, LEAD : LEAD + brows, :] = avgs[k]

    def stack3(values):
        rows_of = iota((16, values[0].shape[1]), 0)
        out = jnp.zeros(rows_of.shape, F32)
        for i, v in enumerate(values):
            first, rest = split2(v)
            second, third = split2(v - first)
            for j, part in enumerate((first, second, third)):
                out = jnp.where(rows_of == 3 * i + j, part, out)
        return out.astype(BF16)

    def join3(wide, i):
        return wide[3 * i : 3 * i + 1] + wide[3 * i + 1 : 3 * i + 2] + wide[3 * i + 2 : 3 * i + 3]

    wide = jnp.dot(
        stack3([clev[LEAD : LEAD + 1, :], ckc[LEAD : LEAD + 1, :], ckr[LEAD + 1 : LEAD + 2, :]]),
        rmat[...], preferred_element_type=F32,
    )
    kc0, kr1 = join3(wide, 1), join3(wide, 2)
    lane = iota((1, fw), 1)
    odd, upper = lane % 2 == 1, lane % 4 >= 2

    def lane_means(x):
        x = x + jnp.where(odd, pltpu.roll(x, 1, 1), pltpu.roll(x, fw - 1, 1))
        x = x + jnp.where(upper, pltpu.roll(x, 2, 1), pltpu.roll(x, fw - 2, 1))
        return x * (1.0 / (RATIO * RATIO))

    erow = iota((16, fw), 0)

    def step(k, carry, keep=False):
        c0, g0, h1 = carry

        @pl.when(tile == 0)
        def _():
            lev[LEAD - 1 : LEAD, :] = c0

        if ends:
            @pl.when(is_last)
            def _():
                above = jnp.sum(lev[top - 8 : top - 4, :], axis=0, keepdims=True)
                below = jnp.sum(lev[top - 4 : top, :], axis=0, keepdims=True)
                esum[...] = jnp.where(
                    erow == 2 * k, above, jnp.where(erow == 2 * k + 1, below, esum[...])
                )

        mean = lane_means(jnp.sum(lev[LEAD : LEAD + RATIO, :], axis=0, keepdims=True))
        g0 = g0 - kc0 * (c0 - pltpu.roll(c0, RATIO, 1))
        h1 = h1 - kr1 * (mean - c0)
        c0 = c0 - ((pltpu.roll(g0, fw - RATIO, 1) - g0) + h1)
        push(lev, gc, gr, kc, kr, strips)
        for b in strips:
            new = lev[b : b + 8, :] - spread(gc, gr, b)
            lev[b : b + 8, :] = new
            if LEAD <= b < top:
                r = slice(b - LEAD, b - LEAD + 8)
                peak_o[r, :] = jnp.maximum(peak_o[r, :], new[:, 0:cols])
                if keep:
                    total[r, :] += new
        return c0, g0, h1

    zero = jnp.zeros((1, fw), F32)
    carry = lax.fori_loop(
        0, STEPS - 2, functools.partial(step, keep=True), (join3(wide, 0), zero, zero)
    )
    block_means(0, total[...])
    carry = step(STEPS - 2, carry)
    block_means(1, lev[LEAD:top, :])
    carry = step(STEPS - 1, carry)
    if ends:
        @pl.when(is_last)
        def _():
            edges[...] = means(esum[...])
            edge_copy().start()
    surf_o[...] = lev[LEAD:top, 0:cols]

    @pl.when(tile >= nested)
    def _():
        if ends:
            pl.when(tile == nested)(lambda: edge_copy().wait_recv())
        erows = iota((16, cw), 0)
        crow = iota((8, cw), 0)

        def cstep(k, carry):
            def edge(i):
                return jnp.sum(jnp.where(erows == 2 * k + i, edger[...], 0.0), axis=0, keepdims=True)

            @pl.when(tile == nested)
            def _():
                clev[LEAD - 8 : LEAD, :] = jnp.where(crow == 7, edge(0), clev[LEAD - 8 : LEAD, :])
                clev[LEAD : LEAD + 8, :] = jnp.where(crow == 0, edge(1), clev[LEAD : LEAD + 8, :])

            push(clev, cgc, cgr, ckc, ckr, cstrips)
            for b in cstrips:
                clev[b : b + 8, :] -= spread(cgc, cgr, b)
            return carry

        lax.fori_loop(0, STEPS, cstep, 0)
        coarse_o[...] = clev[LEAD : LEAD + crows, 0:ccols]

    @pl.when(tile < nested)
    def _():
        c0, g0, h1 = carry
        narrow = RATIO * jnp.dot(stack3([c0, h1]), amat[...], preferred_element_type=F32)
        avg_wait(0)
        avg_wait(1)
        for b in range(LEAD, LEAD + crows + 8, 8):
            clev[b : b + 8, :] = avgr[0, b - 1 : b + 7, :] + avgr[1, b - 1 : b + 7, :]
        clev[LEAD - 1 : LEAD, :] = avgr[0, LEAD - 2 : LEAD - 1, :] + avgr[1, LEAD - 2 : LEAD - 1, :]
        inner = range(LEAD, LEAD + crows + 8, 8)
        push(clev, cgc, cgr, ckc, ckr, inner)

        @pl.when(tile == 0)
        def _():
            cgr[LEAD + 1 : LEAD + 2, :] = join3(narrow, 1)

        for b in range(LEAD, LEAD + crows, 8):
            new = avgr[1, b - 1 : b + 7, :] - spread(cgc, cgr, b)
            coarse_o[b - LEAD : b - LEAD + 8, :] = new[:, 0:ccols]

        @pl.when(tile == 0)
        def _():
            coarse_o[0:1, :] = join3(narrow, 0)[:, 0:ccols]

    rest = pl.ds(0, owners - 1)
    pair_copy(send.at[rest], recv.at[rest], a_ss.at[0], a_rs.at[0], me).wait_send()
    pair_copy(mrecv.at[rest], mrecv.at[rest], m_ss.at[0], m_rs.at[0], me).wait_send()
    for i, (dy, dx) in enumerate(moves):
        pl.when(inside(dy, dx))(lambda i=i: static_copy(i).wait_send())
    core_copy().wait_send()
    for s in (1, 0):
        for kind, v in kinds:
            pl.when(goes(kind, v, 1))(
                lambda s=s, kind=kind, v=v: halo_copy(s, kind, v, plane).wait_send()
            )

    for k in range(2):
        for kind in range(3):
            pl.when(avg_goes(kind))(lambda k=k, kind=kind: avg_copy(k, kind).wait_send())
    if ends:
        pl.when(is_last)(lambda: edge_copy().wait_send())


def shards(dims, green, row_owner, row_index, row_fault, slip, depth, wet, coarse_depth, coarse_start):
    planes, tiles, cols_n, subs_n = dims
    owners = tiles * cols_n * subs_n
    entries, cols = green.shape
    rows = depth.shape[0]
    crows, ccols = coarse_depth.shape
    capacity = max(2, (2 * entries + owners - 1) // owners)
    capp = (capacity + 15) // 16 * 16
    packs = owners // (128 // capp)
    hw = cols // planes
    i32 = lambda *shape: pltpu.VMEM(shape, jnp.int32)
    fw, cw = cols + 128, ccols + 128
    high, chigh = rows + 32, crows + 32
    vmem = lambda *shape: pltpu.VMEM(shape, F32)
    dma = pltpu.SemaphoreType.DMA
    keep = lambda x: pltpu.with_memory_space_constraint(x, pltpu.HBM)
    return pl.pallas_call(
        functools.partial(kernel, dims),
        out_shape=(
            jax.ShapeDtypeStruct((rows, cols), F32),
            jax.ShapeDtypeStruct((rows, cols), F32),
            jax.ShapeDtypeStruct((crows, ccols), F32),
        ),
        in_specs=[pl.BlockSpec(memory_space=pltpu.HBM)] * 9,
        out_specs=(pl.BlockSpec(memory_space=pltpu.VMEM),) * 3,
        scratch_shapes=[
            pltpu.VMEM((entries, hw), BF16), i32(1, entries), i32(1, entries), i32(1, entries),
            vmem(1, slip.shape[0]), vmem(rows, cols), i32(rows, cols),
            pltpu.VMEM((owners * capp, entries), BF16), vmem(owners, entries),
            pltpu.VMEM((owners, capp, hw), BF16),
            pltpu.VMEM((owners, capp, hw), BF16),
            pltpu.VMEM((packs, 8, 128), BF16), pltpu.VMEM((owners, 8, 128), BF16),
            vmem(8, 128), vmem(8, 128), vmem(4 * rows, hw),
            vmem(rows + 8, cols + 512), vmem(2, rows + 8, 384), vmem(2, 8, cols + 256),
            vmem(2, 2, 8, 384),
            vmem(2 * rows, hw), vmem(rows, hw), vmem(2, rows, 128), vmem(2, 2, 8, hw),
            vmem(2, 2, 8, 128),
        ]
        + [vmem(high, fw)] * 6
        + [vmem(chigh, cw)] * 6
        + [
            pltpu.VMEM((fw, cw), BF16), pltpu.VMEM((cw, fw), BF16),
            vmem(cw // 128, rows, 128),
            vmem(rows, fw), vmem(2, rows // RATIO, cw), vmem(2, chigh, cw),
            vmem(16, fw), vmem(16, cw), vmem(16, cw),
            dma((11,)), dma((1,)), dma((packs,)), dma((1,)), dma((packs,)), dma((2,)), dma((8,)), dma((8,)), dma((11,)),
            dma((11,)), dma((3, 3)), dma((3, 3)),
        ],
        compiler_params=pltpu.CompilerParams(
            collective_id=0, has_side_effects=True, vmem_limit_bytes=48 * 1024 * 1024
        ),
    )(
        keep(green), keep(row_owner.reshape(1, entries)), keep(row_index.reshape(1, entries)),
        keep(row_fault.reshape(1, entries)), keep(slip.reshape(1, -1)), keep(depth), keep(wet), keep(coarse_depth), keep(coarse_start),
    )


def solution(mesh):
    dims = tuple(mesh.shape[a] for a in ("scen", "tile", "col", "sub"))
    return jax.shard_map(
        functools.partial(shards, dims),
        mesh=mesh,
        in_specs=(
            P(("tile", "col", "sub"), None),
            P(("tile", "col", "sub"), None),
            P(("tile", "col", "sub")),
            P(("tile", "col", "sub")),
            P(("scen", "tile", "col", "sub")),
            P("tile", ("col", "sub")),
            P("tile", ("col", "sub")),
            P("tile", ("col", "sub")),
            P(("scen", "tile"), ("col", "sub")),
        ),
        out_specs=(
            P(("scen", "tile"), ("col", "sub")),
            P(("scen", "tile"), ("col", "sub")),
            P(("scen", "tile"), ("col", "sub")),
        ),
        check_vma=False,
    )
```

```python
import functools
import jax
import jax.numpy as jnp
from jax import lax
from jax.experimental import pallas as pl
from jax.experimental.pallas import tpu as pltpu
from jax.sharding import PartitionSpec as P

RATIO = 4
STEPS = 6
HALO = 8
LEAD = 16
F32 = jnp.float32
BF16 = jnp.bfloat16
MESH = pl.DeviceIdType.MESH


def split2(x):
    high = x.astype(BF16).astype(F32)
    return high, (x - high).astype(BF16).astype(F32)


def iota(shape, dim):
    return lax.broadcasted_iota(jnp.int32, shape, dim)


def kernel(
    dims,
    green_h, owner_h, index_h, fault_h, slip_h, depth_h, wet_h, cdep_h, cstart_h,
    peak_o, surf_o, coarse_o,
    green, owner, index, fault, slip, depth, wet, chosen_r,
    place, send, recv, msend, mrecv, slip_s, slip_r, acc,
    zs, zside, zvert, zcorn,
    half, hcore, hside, hvert, hcorn,
    lev, held, gc, gr, kc, kr,
    clev, cheld, cgc, cgr, ckc, ckr,
    amat, rmat, work, total, avgs, avgr, esum, edges, edger,
    i_s, a_ss, a_rs, m_ss, m_rs, sl_s, z_ss, z_rs, h_ss, h_rs, v_ss, v_rs, alive,
):
    planes, tiles, cols_n, subs_n = dims
    sides = cols_n * subs_n
    owners = tiles * sides
    plane = lax.axis_index("scen")
    tile = lax.axis_index("tile")
    side = lax.axis_index("col") * subs_n + lax.axis_index("sub")
    me = tile * sides + side
    rows, cols = depth.shape
    crows, ccols = cdep_h.shape
    entries, hw = green.shape
    capp = send.shape[1]
    pack = 128 // capp
    packs = owners // pack
    fw = cols + 128
    cw = ccols + 128
    top = LEAD + rows

    def dev(p, t, c):
        return {"scen": p, "tile": t, "col": c // subs_n, "sub": c % subs_n}

    def fetch(i):
        lanes = pl.ds(pl.multiple_of(plane * hw, 128), hw)
        far = 256 + cols
        src, dst = [
            (owner_h, owner), (green_h.at[:, lanes], green), (index_h, index), (fault_h, fault),
            (slip_h, slip), (depth_h, depth), (wet_h, wet),
            (cdep_h, zs.at[0:rows, 0:ccols]), (cstart_h, zs.at[0:rows, 128 : 128 + ccols]),
            (cdep_h, zs.at[0:rows, far : far + ccols]),
            (cstart_h, zs.at[0:rows, far + 128 : far + 128 + ccols]),
        ][i]
        return pltpu.make_async_copy(src, dst, i_s.at[i])

    for i in range(11):
        fetch(i).start()

    barrier = pltpu.get_barrier_semaphore()

    other = planes - 1 - plane
    base = tile * sides
    later = owners - base

    def greet(i, carry):
        d = base + lax.rem(side + i, later)
        pl.semaphore_signal(
            barrier, inc=1, device_id=dev(plane, d // sides, lax.rem(d, sides)),
            device_id_type=MESH,
        )
        return carry

    lax.fori_loop(1, later, greet, 0)
    pl.semaphore_signal(barrier, inc=1, device_id=dev(other, tile, side), device_id_type=MESH)

    fetch(0).wait()
    dest = owner[...]
    hit = iota((owners, entries), 0) == dest
    before = (iota((entries, entries), 0) < iota((entries, entries), 1)).astype(F32).astype(BF16)
    rank = jnp.dot(hit.astype(F32).astype(BF16), before, preferred_element_type=F32)
    place[...] = jnp.where(hit, rank, -1.0)
    group = min(owners, 512 // capp)
    groups = owners // group
    fetch(1).wait()
    gh = green[...]
    slots = iota((group, capp, entries), 1).astype(F32)

    def select(g):
        rows_of = place[pl.ds(pl.multiple_of(g * group, group), group), :]
        chosen = jnp.where(rows_of[:, None, :] == slots, 1.0, 0.0)
        chosen = chosen.reshape(group * capp, entries).astype(BF16)
        chosen_r[pl.ds(g * group * capp, group * capp), :] = chosen
        return chosen

    def fill(g, carry):
        picked = jnp.dot(select(g), gh, preferred_element_type=F32).astype(BF16)
        send[pl.ds(g * group, group)] = picked.reshape(group, capp, hw)
        return carry

    fill(0, 0) if groups == 1 else lax.fori_loop(0, groups, fill, 0)

    for i in range(2, 11):
        fetch(i).wait()
    slip_s[...] = jnp.zeros_like(slip_s)
    slip_s[0:1, 0 : slip.shape[1]] = slip[...]
    raw = depth[...]
    zs[0:rows, 256 : 256 + cols] = jnp.where(wet[...] > 0, raw, 0.0)
    zs[rows : rows + 8, 256 : 256 + cols] = jnp.broadcast_to(raw[0:1], (8, cols))
    for off in (0, 256 + cols):
        zs[rows : rows + 8, off : off + 256] = jnp.zeros((8, 256), F32)

    pl.semaphore_wait(barrier, base + sides)

    def tell(i, carry):
        pl.semaphore_signal(
            alive.at[tile], inc=1, device_id=dev(plane, i // sides, lax.rem(i, sides)),
            device_id_type=MESH,
        )
        return carry

    lax.fori_loop(0, base, tell, 0)

    slip_copy = pltpu.make_async_remote_copy(
        src_ref=slip_s, dst_ref=slip_r, send_sem=sl_s.at[0], recv_sem=sl_s.at[1],
        device_id=dev(other, tile, side), device_id_type=MESH,
    )
    slip_copy.start()

    def pair_copy(src, dst, s_sem, r_sem, d):
        return pltpu.make_async_remote_copy(
            src_ref=src, dst_ref=dst, send_sem=s_sem, recv_sem=r_sem,
            device_id=dev(plane, d // sides, lax.rem(d, sides)), device_id_type=MESH,
        )

    def a2a(d):
        return pair_copy(send.at[d], recv.at[me], a_ss.at[0], a_rs.at[me // pack], d)

    def a2a_meta(d):
        return pair_copy(msend.at[d // pack], mrecv.at[me], m_ss.at[0], m_rs.at[me // pack], d)

    def a2a_wait(g, n):
        first = pl.ds(g * pack, n)
        pair_copy(recv.at[first], recv.at[first], a_ss.at[0], a_rs.at[g], me).wait_recv()
        pair_copy(mrecv.at[first], mrecv.at[first], m_ss.at[0], m_rs.at[g], me).wait_recv()

    middle = tiles // 2
    low = tile < middle

    def launch_tile(t, start):
        first = t * sides

        def own(i, carry):
            start(first + lax.rem(side + i, sides)).start()
            return carry

        lax.fori_loop(jnp.where(t == tile, 1, 0), sides, own, 0)

    def launch_span(begin, end, start):
        lax.fori_loop(begin, end, lambda t, c: (launch_tile(t, start), c)[1], 0)

    def launch_met(begin, end, start):
        def met(t, carry):
            pl.semaphore_wait(alive.at[t], sides)
            launch_tile(t, start)
            return carry

        lax.fori_loop(begin, end, met, 0)

    @pl.when(low)
    def _():
        launch_span(0, tile + 1, a2a)
        launch_met(middle, tiles, a2a)

    @pl.when(jnp.logical_not(low))
    def _():
        launch_span(0, middle, a2a)

    moves = [(0, -1), (0, 1), (-1, 0), (1, 0), (-1, -1), (-1, 1), (1, -1), (1, 1)]

    def static_copy(i):
        dy, dx = moves[i]
        lanes = (
            slice(0, 512 - 128) if dx == -1
            else slice(cols + 128, cols + 512) if dx == 1 else slice(0, 256 + cols)
        )
        sel = slice(0, rows + 8) if dy == 0 else slice(0, 8) if dy == -1 else slice(rows - 8, rows)
        bi = 0 if dy == -1 else 1
        bj = 0 if dx == -1 else 1
        dst = zside.at[bj] if dy == 0 else zvert.at[bi] if dx == 0 else zcorn.at[bi, bj]
        return pltpu.make_async_remote_copy(
            src_ref=zs.at[sel, lanes], dst_ref=dst, send_sem=z_ss.at[i], recv_sem=z_rs.at[i],
            device_id=dev(plane, tile + dy, side + dx), device_id_type=MESH,
        )

    def inside(dy, dx):
        ok = True
        for at, by, size in ((tile, dy, tiles), (side, dx, sides)):
            if by == -1:
                ok = jnp.logical_and(ok, at > 0)
            if by == 1:
                ok = jnp.logical_and(ok, at < size - 1)
        return ok

    slip_copy.wait()

    mrow = iota((8, slip.shape[1]), 0)
    own_h, own_l = split2(slip[...])
    oth_h, oth_l = split2(slip_r[0:1, 0 : slip.shape[1]])
    parts = jnp.where(mrow == 1, own_h, 0.0)
    for i, part in ((2, own_l), (3, oth_h), (4, oth_l)):
        parts = jnp.where(mrow == i, part, parts)
    picks = (iota((slip.shape[1], entries), 0) == fault[...]).astype(F32).astype(BF16)
    meta = jnp.dot(parts.astype(BF16), picks, preferred_element_type=F32)
    meta = jnp.where(iota((8, entries), 0) == 0, index[...].astype(F32), meta).astype(BF16)

    def describe(g, carry):
        told = lax.dot_general(
            meta, chosen_r[pl.ds(g * group * capp, group * capp), :], (((1,), (1,)), ((), ())), preferred_element_type=F32
        )
        for i in range(group // pack):
            msend[g * (group // pack) + i] = told[:, i * 128 : (i + 1) * 128].astype(BF16)
        return carry

    describe(0, 0) if groups == 1 else lax.fori_loop(0, groups, describe, 0)

    @pl.when(low)
    def _():
        launch_span(middle, tiles, a2a_meta)
        launch_span(0, tile + 1, a2a_meta)
        launch_met(tile + 1, middle, a2a)
        launch_span(tile + 1, middle, a2a_meta)

    @pl.when(jnp.logical_not(low))
    def _():
        launch_span(0, middle, a2a_meta)
        launch_span(middle, tile + 1, a2a_meta)
        launch_span(middle, tile + 1, a2a)
        launch_met(tile + 1, tiles, a2a)
        launch_span(tile + 1, tiles, a2a_meta)

    fl = iota((fw, cw), 0)
    fmap = jnp.where(fl < cols + 64, fl // RATIO, fl // RATIO + (cw - fw // RATIO))
    amat[...] = jnp.where(fmap == iota((fw, cw), 1), 1.0 / (RATIO * RATIO), 0.0).astype(BF16)
    rl = iota((cw, fw), 1)
    rmap = jnp.where(rl < cols + 64, rl // RATIO, rl // RATIO + (cw - fw // RATIO))
    rmat[...] = jnp.where(rmap == iota((cw, fw), 0), 1.0, 0.0).astype(BF16)
    for ref in (lev, held, gc, gr, clev, cheld, cgc, cgr):
        ref[...] = jnp.zeros_like(ref)
    acc[...] = jnp.zeros_like(acc)

    for bj in range(2):
        dx = 1 if bj == 0 else -1
        @pl.when(jnp.logical_not(inside(0, dx)))
        def _(bj=bj):
            zside[bj] = jnp.zeros(zside.shape[1:], F32)
        for bi in range(2):
            dy = 1 if bi == 0 else -1
            @pl.when(jnp.logical_not(inside(dy, dx)))
            def _(bi=bi, bj=bj):
                zcorn[bi, bj] = jnp.zeros(zcorn.shape[2:], F32)
    for bi in range(2):
        dy = 1 if bi == 0 else -1
        @pl.when(jnp.logical_not(inside(dy, 0)))
        def _(bi=bi):
            zvert[bi] = jnp.zeros(zvert.shape[1:], F32)
    wrow = iota((4 * rows, 128), 0)
    in_tile = lax.rem(wrow, rows).astype(F32)
    mlane = iota((8, 128), 1)
    recv[me] = send[me]
    mrecv[me] = msend[me // pack]

    def put(g):
        told = jnp.zeros((8, 128), F32)
        for j in range(pack):
            moved = pltpu.roll(
                mrecv[g * pack + j].astype(F32), lax.rem(j + pack - lax.rem(me, pack), pack) * capp, 1
            )
            told = jnp.where((mlane >= j * capp) & (mlane < (j + 1) * capp), moved, told)
        weight = jnp.where(
            wrow < rows, told[1:2],
            jnp.where(wrow < 2 * rows, told[3:4], jnp.where(wrow < 3 * rows, told[2:3], told[4:5])),
        )
        weight = jnp.where(in_tile == told[0:1], weight, 0.0).astype(BF16)
        block = recv[pl.ds(g * pack, pack)].reshape(128, hw)
        acc[...] += jnp.dot(weight, block, preferred_element_type=F32)

    mine = me // pack

    def take(i, carry):
        g = lax.rem(mine + i, packs)
        a2a_wait(g, pack)
        put(g)
        return carry

    a2a_wait(mine, pack - 1)
    put(mine)
    lax.fori_loop(1, packs - 1, take, 0, unroll=packs == 4)
    for i, (dy, dx) in enumerate(moves):
        pl.when(inside(dy, dx))(lambda i=i: static_copy(i).start())

    take(packs - 1, 0)
    half[...] = acc[0 : 2 * rows, :] + acc[2 * rows : 4 * rows, :]

    toward = 2 * plane - 1

    def core_copy():
        return pltpu.make_async_remote_copy(
            src_ref=half.at[rows : 2 * rows, :], dst_ref=hcore, send_sem=h_ss.at[0],
            recv_sem=h_rs.at[0], device_id=dev(other, tile, side), device_id_type=MESH,
        )

    edge = pl.ds(pl.multiple_of(plane * (hw - 128), 128), 128)

    def halo_copy(s, kind, v, q):
        to_plane = plane if s == 0 else other
        dy = 0 if kind == 0 else (-1 if v == 0 else 1)
        r0 = s * rows + (0 if v == 0 else rows - 8)
        if kind == 0:
            src, dst, n = half.at[s * rows : (s + 1) * rows, edge], hside.at[q], 0
        elif kind == 1:
            src, dst, n = half.at[r0 : r0 + 8, :], hvert.at[v, q], 1 + v
        else:
            src, dst, n = half.at[r0 : r0 + 8, edge], hcorn.at[v, q], 3 + v
        return pltpu.make_async_remote_copy(
            src_ref=src, dst_ref=dst, send_sem=h_ss.at[1 + 5 * s + n], recv_sem=h_rs.at[1 + n + 5 * q],
            device_id=dev(to_plane, tile + dy, side if kind == 1 else side + toward),
            device_id_type=MESH,
        )

    kinds = [(1, 0), (1, 1), (0, 0), (2, 0), (2, 1)]

    def goes(kind, v, sign):
        dy = 0 if kind == 0 else (-1 if v == 0 else 1) * sign
        ok = inside(dy, 0)
        if kind != 1:
            to = side + toward
            ok = jnp.logical_and(ok, jnp.logical_and(to >= 0, to < sides))
        return ok

    core_copy().start()
    for s in (1, 0):
        for kind, v in kinds:
            pl.when(goes(kind, v, 1))(
                lambda s=s, kind=kind, v=v: halo_copy(s, kind, v, plane).start()
            )

    def comes(kind, v, q):
        dy = 0 if kind == 0 else (1 if v == 0 else -1)
        dx = 0 if kind == 1 else (1 if q == 0 else -1)
        return inside(dy, dx)

    for i, (dy, dx) in enumerate(moves):
        pl.when(inside(-dy, -dx))(lambda i=i: static_copy(i).wait_recv())

    def merge(right, left):
        return jnp.where(iota(right.shape, right.ndim - 1) < 64, right, left)

    def place_static(r0, n, z, zr, zl, sr):
        held[r0 : r0 + n, 0:cols] = z[sr, 256 : 256 + cols]
        held[r0 : r0 + n, cols:fw] = merge(zr[sr, 256:384], zl[sr, 0:128])
        cheld[r0 : r0 + n, 0:ccols] = z[sr, 0:128]
        cheld[r0 : r0 + n, ccols:cw] = merge(zr[sr, 0:128], zl[sr, 128:256])
        clev[r0 : r0 + n, 0:ccols] = z[sr, 128:256]
        clev[r0 : r0 + n, ccols:cw] = merge(zr[sr, 128:256], zl[sr, 256:384])

    place_static(LEAD, rows, zs, zside.at[0], zside.at[1], slice(0, rows))
    place_static(top, 8, zvert.at[0], zcorn.at[0, 0], zcorn.at[0, 1], slice(0, 8))
    place_static(8, 8, zvert.at[1], zcorn.at[1, 0], zcorn.at[1, 1], slice(0, 8))

    @pl.when(tile == 0)
    def _():
        held[LEAD - 1 : LEAD, 0:cols] = depth[0:1, :]
        held[LEAD - 1 : LEAD, cols:fw] = merge(
            zside[0, rows : rows + 1, 256:384], zside[1, rows : rows + 1, 0:128]
        )

    strips = [8 + 8 * i for i in range((rows + 16) // 8)]
    cstrips = [8 + 8 * i for i in range((crows + 16) // 8)]

    def faces(h, k_c, k_r, scale, which):
        width = h.shape[1]
        for b in which:
            here, up = h[b : b + 8, :], h[b - 1 : b + 7, :]
            west = pltpu.roll(here, 1, 1)
            k_c[b : b + 8, :] = jnp.where((here > 0.0) & (west > 0.0), scale * (here + west), 0.0)
            k_r[b : b + 8, :] = jnp.where((here > 0.0) & (up > 0.0), scale * (here + up), 0.0)

    faces(held, kc, kr, 0.5 * 0.5 * 0.5, strips)
    faces(cheld, ckc, ckr, 0.5 * 0.125 * 0.125, cstrips)

    for q in range(2):
        for kind, v in kinds:
            dst = hside.at[q] if kind == 0 else hvert.at[v, q] if kind == 1 else hcorn.at[v, q]
            @pl.when(jnp.logical_not(comes(kind, v, q)))
            def _(dst=dst):
                dst[...] = jnp.zeros(dst.shape, F32)
            pl.when(comes(kind, v, q))(
                lambda kind=kind, v=v, q=q: halo_copy(0, kind, v, q).wait_recv()
            )
    core_copy().wait_recv()

    lev[LEAD:top, pl.ds(pl.multiple_of(plane * hw, 128), hw)] = half[0:rows, :]
    lev[LEAD:top, pl.ds(pl.multiple_of(other * hw, 128), hw)] = hcore[...]
    lev[LEAD:top, cols:fw] = merge(hside[0], hside[1])
    for v, r0 in ((0, top), (1, 8)):
        lev[r0 : r0 + 8, 0:hw] = hvert[v, 0]
        lev[r0 : r0 + 8, hw:cols] = hvert[v, 1]
        lev[r0 : r0 + 8, cols:fw] = merge(hcorn[v, 0], hcorn[v, 1])
    peak_o[...] = lev[LEAD:top, 0:cols]
    total[...] = lev[LEAD:top, :]

    brows = rows // RATIO
    per = crows * RATIO // rows
    nest = brows * tiles
    nested = nest // crows
    ct = tile // per
    cm = lax.rem(tile, per)

    def avg_copy(k, kind):
        if kind == 0:
            src, to = avgs.at[k], ct
            dst = avgr.at[k, pl.ds(pl.multiple_of(LEAD + cm * brows, 8), brows), :]
        elif kind == 1:
            src, to = avgs.at[k, brows - 8 : brows, :], ct + 1
            dst = avgr.at[k, 8:16, :]
        else:
            src, to = avgs.at[k, 0:8, :], ct - 1
            dst = avgr.at[k, LEAD + crows : LEAD + crows + 8, :]
        return pltpu.make_async_remote_copy(
            src_ref=src, dst_ref=dst, send_sem=v_ss.at[k, kind], recv_sem=v_rs.at[k, kind],
            device_id=dev(plane, to, side), device_id_type=MESH,
        )

    def avg_goes(kind):
        if kind == 0:
            return tile > 0
        if kind == 1:
            return jnp.logical_and(cm == per - 1, ct + 1 < nested)
        return jnp.logical_and(cm == 0, ct > 0)

    def avg_send(k):
        for kind in range(3):
            pl.when(avg_goes(kind))(lambda kind=kind: avg_copy(k, kind).start())

    def avg_wait(k):
        def wait(kind, dst):
            pltpu.make_async_remote_copy(
                src_ref=dst, dst_ref=dst, send_sem=v_ss.at[k, kind], recv_sem=v_rs.at[k, kind],
                device_id=dev(plane, tile, side), device_id_type=MESH,
            ).wait_recv()

        pl.when(tile == 0)(lambda: wait(0, avgr.at[k, LEAD + brows : LEAD + per * brows, :]))
        pl.when(tile > 0)(lambda: wait(0, avgr.at[k, LEAD : LEAD + per * brows, :]))
        pl.when(tile > 0)(lambda: wait(1, avgr.at[k, 8:16, :]))
        pl.when(tile < nested - 1)(lambda: wait(2, avgr.at[k, LEAD + crows : LEAD + crows + 8, :]))

    def edge_copy():
        return pltpu.make_async_remote_copy(
            src_ref=edges, dst_ref=edger, send_sem=v_ss.at[2, 0], recv_sem=v_rs.at[2, 0],
            device_id=dev(plane, nested, side), device_id_type=MESH,
        )

    ends = nested < tiles
    is_last = tile == tiles - 1

    def push(s_ref, g_c, g_r, k_c, k_r, which):
        for b in which:
            here, up = s_ref[b : b + 8, :], s_ref[b - 1 : b + 7, :]
            g_c[b : b + 8, :] -= k_c[b : b + 8, :] * (here - pltpu.roll(here, 1, 1))
            g_r[b : b + 8, :] -= k_r[b : b + 8, :] * (here - up)

    def spread(g_c, g_r, b):
        east = g_c[b : b + 8, :]
        return (pltpu.roll(east, east.shape[1] - 1, 1) - east) + (
            g_r[b + 1 : b + 9, :] - g_r[b : b + 8, :]
        )

    def means(x):
        high, low = split2(x)
        return jnp.dot(high.astype(BF16), amat[...], preferred_element_type=F32) + jnp.dot(
            low.astype(BF16), amat[...], preferred_element_type=F32
        )

    def block_means(k, x):
        sums = means(x)
        for j in range(cw // 128):
            work[j] = sums[:, j * 128 : (j + 1) * 128]
            avgs[k, :, j * 128 : (j + 1) * 128] = sum(
                work[j, pl.ds(i, brows, stride=RATIO), :] for i in range(RATIO)
            )
        avg_send(k)

        @pl.when(tile == 0)
        def _():
            avgr[k, LEAD : LEAD + brows, :] = avgs[k]

    def stack3(values):
        rows_of = iota((16, values[0].shape[1]), 0)
        out = jnp.zeros(rows_of.shape, F32)
        for i, v in enumerate(values):
            first, rest = split2(v)
            second, third = split2(v - first)
            for j, part in enumerate((first, second, third)):
                out = jnp.where(rows_of == 3 * i + j, part, out)
        return out.astype(BF16)

    def join3(wide, i):
        return wide[3 * i : 3 * i + 1] + wide[3 * i + 1 : 3 * i + 2] + wide[3 * i + 2 : 3 * i + 3]

    wide = jnp.dot(
        stack3([clev[LEAD : LEAD + 1, :], ckc[LEAD : LEAD + 1, :], ckr[LEAD + 1 : LEAD + 2, :]]),
        rmat[...], preferred_element_type=F32,
    )
    kc0, kr1 = join3(wide, 1), join3(wide, 2)
    lane = iota((1, fw), 1)
    odd, upper = lane % 2 == 1, lane % 4 >= 2

    def lane_means(x):
        x = x + jnp.where(odd, pltpu.roll(x, 1, 1), pltpu.roll(x, fw - 1, 1))
        x = x + jnp.where(upper, pltpu.roll(x, 2, 1), pltpu.roll(x, fw - 2, 1))
        return x * (1.0 / (RATIO * RATIO))

    erow = iota((16, fw), 0)

    def step(k, carry, keep=False):
        c0, g0, h1 = carry

        @pl.when(tile == 0)
        def _():
            lev[LEAD - 1 : LEAD, :] = c0

        if ends:
            @pl.when(is_last)
            def _():
                above = jnp.sum(lev[top - 8 : top - 4, :], axis=0, keepdims=True)
                below = jnp.sum(lev[top - 4 : top, :], axis=0, keepdims=True)
                esum[...] = jnp.where(
                    erow == 2 * k, above, jnp.where(erow == 2 * k + 1, below, esum[...])
                )

        mean = lane_means(jnp.sum(lev[LEAD : LEAD + RATIO, :], axis=0, keepdims=True))
        g0 = g0 - kc0 * (c0 - pltpu.roll(c0, RATIO, 1))
        h1 = h1 - kr1 * (mean - c0)
        c0 = c0 - ((pltpu.roll(g0, fw - RATIO, 1) - g0) + h1)
        push(lev, gc, gr, kc, kr, strips)
        for b in strips:
            new = lev[b : b + 8, :] - spread(gc, gr, b)
            lev[b : b + 8, :] = new
            if LEAD <= b < top:
                r = slice(b - LEAD, b - LEAD + 8)
                peak_o[r, :] = jnp.maximum(peak_o[r, :], new[:, 0:cols])
                if keep:
                    total[r, :] += new
        return c0, g0, h1

    zero = jnp.zeros((1, fw), F32)
    carry = lax.fori_loop(
        0, STEPS - 2, functools.partial(step, keep=True), (join3(wide, 0), zero, zero)
    )
    block_means(0, total[...])
    carry = step(STEPS - 2, carry)
    block_means(1, lev[LEAD:top, :])
    carry = step(STEPS - 1, carry)
    if ends:
        @pl.when(is_last)
        def _():
            edges[...] = means(esum[...])
            edge_copy().start()
    surf_o[...] = lev[LEAD:top, 0:cols]

    @pl.when(tile >= nested)
    def _():
        if ends:
            pl.when(tile == nested)(lambda: edge_copy().wait_recv())
        erows = iota((16, cw), 0)
        crow = iota((8, cw), 0)

        def cstep(k, carry):
            def edge(i):
                return jnp.sum(jnp.where(erows == 2 * k + i, edger[...], 0.0), axis=0, keepdims=True)

            @pl.when(tile == nested)
            def _():
                clev[LEAD - 8 : LEAD, :] = jnp.where(crow == 7, edge(0), clev[LEAD - 8 : LEAD, :])
                clev[LEAD : LEAD + 8, :] = jnp.where(crow == 0, edge(1), clev[LEAD : LEAD + 8, :])

            push(clev, cgc, cgr, ckc, ckr, cstrips)
            for b in cstrips:
                clev[b : b + 8, :] -= spread(cgc, cgr, b)
            return carry

        lax.fori_loop(0, STEPS, cstep, 0)
        coarse_o[...] = clev[LEAD : LEAD + crows, 0:ccols]

    @pl.when(tile < nested)
    def _():
        c0, g0, h1 = carry
        narrow = RATIO * jnp.dot(stack3([c0, h1]), amat[...], preferred_element_type=F32)
        avg_wait(0)
        avg_wait(1)
        for b in range(LEAD, LEAD + crows + 8, 8):
            clev[b : b + 8, :] = avgr[0, b - 1 : b + 7, :] + avgr[1, b - 1 : b + 7, :]
        clev[LEAD - 1 : LEAD, :] = avgr[0, LEAD - 2 : LEAD - 1, :] + avgr[1, LEAD - 2 : LEAD - 1, :]
        inner = range(LEAD, LEAD + crows + 8, 8)
        push(clev, cgc, cgr, ckc, ckr, inner)

        @pl.when(tile == 0)
        def _():
            cgr[LEAD + 1 : LEAD + 2, :] = join3(narrow, 1)

        for b in range(LEAD, LEAD + crows, 8):
            new = avgr[1, b - 1 : b + 7, :] - spread(cgc, cgr, b)
            coarse_o[b - LEAD : b - LEAD + 8, :] = new[:, 0:ccols]

        @pl.when(tile == 0)
        def _():
            coarse_o[0:1, :] = join3(narrow, 0)[:, 0:ccols]

    rest = pl.ds(0, owners - 1)
    pair_copy(send.at[rest], recv.at[rest], a_ss.at[0], a_rs.at[0], me).wait_send()
    pair_copy(mrecv.at[rest], mrecv.at[rest], m_ss.at[0], m_rs.at[0], me).wait_send()
    for i, (dy, dx) in enumerate(moves):
        pl.when(inside(dy, dx))(lambda i=i: static_copy(i).wait_send())
    core_copy().wait_send()
    for s in (1, 0):
        for kind, v in kinds:
            pl.when(goes(kind, v, 1))(
                lambda s=s, kind=kind, v=v: halo_copy(s, kind, v, plane).wait_send()
            )

    for k in range(2):
        for kind in range(3):
            pl.when(avg_goes(kind))(lambda k=k, kind=kind: avg_copy(k, kind).wait_send())
    if ends:
        pl.when(is_last)(lambda: edge_copy().wait_send())


def shards(dims, green, row_owner, row_index, row_fault, slip, depth, wet, coarse_depth, coarse_start):
    planes, tiles, cols_n, subs_n = dims
    owners = tiles * cols_n * subs_n
    entries, cols = green.shape
    rows = depth.shape[0]
    crows, ccols = coarse_depth.shape
    capacity = max(2, (2 * entries + owners - 1) // owners)
    capp = (capacity + 15) // 16 * 16
    packs = owners // (128 // capp)
    hw = cols // planes
    i32 = lambda *shape: pltpu.VMEM(shape, jnp.int32)
    fw, cw = cols + 128, ccols + 128
    high, chigh = rows + 32, crows + 32
    vmem = lambda *shape: pltpu.VMEM(shape, F32)
    dma = pltpu.SemaphoreType.DMA
    keep = lambda x: pltpu.with_memory_space_constraint(x, pltpu.HBM)
    return pl.pallas_call(
        functools.partial(kernel, dims),
        out_shape=(
            jax.ShapeDtypeStruct((rows, cols), F32),
            jax.ShapeDtypeStruct((rows, cols), F32),
            jax.ShapeDtypeStruct((crows, ccols), F32),
        ),
        in_specs=[pl.BlockSpec(memory_space=pltpu.HBM)] * 9,
        out_specs=(pl.BlockSpec(memory_space=pltpu.VMEM),) * 3,
        scratch_shapes=[
            pltpu.VMEM((entries, hw), BF16), i32(1, entries), i32(1, entries), i32(1, entries),
            vmem(1, slip.shape[0]), vmem(rows, cols), i32(rows, cols),
            pltpu.VMEM((owners * capp, entries), BF16), vmem(owners, entries),
            pltpu.VMEM((owners, capp, hw), BF16),
            pltpu.VMEM((owners, capp, hw), BF16),
            pltpu.VMEM((packs, 8, 128), BF16), pltpu.VMEM((owners, 8, 128), BF16),
            vmem(8, 128), vmem(8, 128), vmem(4 * rows, hw),
            vmem(rows + 8, cols + 512), vmem(2, rows + 8, 384), vmem(2, 8, cols + 256),
            vmem(2, 2, 8, 384),
            vmem(2 * rows, hw), vmem(rows, hw), vmem(2, rows, 128), vmem(2, 2, 8, hw),
            vmem(2, 2, 8, 128),
        ]
        + [vmem(high, fw)] * 6
        + [vmem(chigh, cw)] * 6
        + [
            pltpu.VMEM((fw, cw), BF16), pltpu.VMEM((cw, fw), BF16),
            vmem(cw // 128, rows, 128),
            vmem(rows, fw), vmem(2, rows // RATIO, cw), vmem(2, chigh, cw),
            vmem(16, fw), vmem(16, cw), vmem(16, cw),
            dma((11,)), dma((1,)), dma((packs,)), dma((1,)), dma((packs,)), dma((2,)), dma((8,)), dma((8,)), dma((11,)),
            dma((11,)), dma((3, 3)), dma((3, 3)), pltpu.SemaphoreType.REGULAR((tiles,)),
        ],
        compiler_params=pltpu.CompilerParams(
            collective_id=0, has_side_effects=True, vmem_limit_bytes=48 * 1024 * 1024
        ),
    )(
        keep(green), keep(row_owner.reshape(1, entries)), keep(row_index.reshape(1, entries)),
        keep(row_fault.reshape(1, entries)), keep(slip.reshape(1, -1)), keep(depth), keep(wet), keep(coarse_depth), keep(coarse_start),
    )


def solution(mesh):
    dims = tuple(mesh.shape[a] for a in ("scen", "tile", "col", "sub"))
    return jax.shard_map(
        functools.partial(shards, dims),
        mesh=mesh,
        in_specs=(
            P(("tile", "col", "sub"), None),
            P(("tile", "col", "sub"), None),
            P(("tile", "col", "sub")),
            P(("tile", "col", "sub")),
            P(("scen", "tile", "col", "sub")),
            P("tile", ("col", "sub")),
            P("tile", ("col", "sub")),
            P("tile", ("col", "sub")),
            P(("scen", "tile"), ("col", "sub")),
        ),
        out_specs=(
            P(("scen", "tile"), ("col", "sub")),
            P(("scen", "tile"), ("col", "sub")),
            P(("scen", "tile"), ("col", "sub")),
        ),
        check_vma=False,
    )
```

```python
import functools
import jax
import jax.numpy as jnp
from jax import lax
from jax.experimental import pallas as pl
from jax.experimental.pallas import tpu as pltpu
from jax.sharding import PartitionSpec as P

RATIO = 4
STEPS = 6
HALO = 8
LEAD = 16
F32 = jnp.float32
BF16 = jnp.bfloat16
MESH = pl.DeviceIdType.MESH


def split2(x):
    high = x.astype(BF16).astype(F32)
    return high, (x - high).astype(BF16).astype(F32)


def iota(shape, dim):
    return lax.broadcasted_iota(jnp.int32, shape, dim)


def kernel(
    dims,
    green_h, owner_h, index_h, fault_h, slip_h, depth_h, wet_h, cdep_h, cstart_h,
    peak_o, surf_o, coarse_o,
    green, owner, index, fault, slip, depth, wet, chosen_r,
    place, send, recv, msend, mrecv, slip_s, slip_r, acc, weights,
    zs, zside, zvert, zcorn,
    half, hcore, hside, hvert, hcorn,
    lev, held, gc, gr, kc, kr,
    clev, cheld, cgc, cgr, ckc, ckr,
    amat, rmat, work, total, avgs, avgr, esum, edges, edger,
    i_s, a_ss, a_rs, m_ss, m_rs, sl_s, z_rs, h_ss, h_rs, v_rs, alive,
):
    planes, tiles, cols_n, subs_n = dims
    sides = cols_n * subs_n
    owners = tiles * sides
    plane = lax.axis_index("scen")
    tile = lax.axis_index("tile")
    side = lax.axis_index("col") * subs_n + lax.axis_index("sub")
    me = tile * sides + side
    rows, cols = depth.shape
    crows, ccols = cdep_h.shape
    entries, hw = green.shape
    capp = send.shape[2]
    pack = 128 // capp
    packs = owners // pack
    fw = cols + 128
    cw = ccols + 128
    top = LEAD + rows

    def dev(p, t, c):
        return {"scen": p, "tile": t, "col": c // subs_n, "sub": c % subs_n}

    def fetch(i):
        edge_lanes = pl.ds(pl.multiple_of(plane * (hw + 128), 128), 128)
        inner_lanes = pl.ds(pl.multiple_of(128 + plane * 128, 128), 128)
        far = 256 + cols
        src, dst = [
            (owner_h, owner), (green_h.at[:, edge_lanes], green.at[:, 0:128]), (index_h, index), (fault_h, fault),
            (slip_h, slip), (depth_h, depth), (wet_h, wet),
            (cdep_h, zs.at[0:rows, 0:ccols]), (cstart_h, zs.at[0:rows, 128 : 128 + ccols]),
            (cdep_h, zs.at[0:rows, far : far + ccols]),
            (cstart_h, zs.at[0:rows, far + 128 : far + 128 + ccols]),
            (green_h.at[:, inner_lanes], green.at[:, 128:256]),
        ][i]
        return pltpu.make_async_copy(src, dst, i_s.at[i])

    barrier = pltpu.get_barrier_semaphore()

    other = planes - 1 - plane

    def hail(sem):
        def start(i, carry):
            pl.semaphore_signal(
                sem, inc=1, device_id=dev(plane, i // sides, lax.rem(i, sides)), device_id_type=MESH
            )
            return carry

        return start

    def hail_other(sem):
        pl.semaphore_signal(sem, inc=1, device_id=dev(other, tile, side), device_id_type=MESH)

    lax.fori_loop(me + 1, owners, hail(barrier), 0)
    pl.when(plane == 0)(lambda: hail_other(barrier))
    for i in (4, 0, 1, 11, 2, 3, 5, 6, 7, 8, 9, 10):
        fetch(i).start()

    slip_copy = pltpu.make_async_remote_copy(
        src_ref=slip_s, dst_ref=slip_r, send_sem=sl_s.at[0], recv_sem=sl_s.at[1],
        device_id=dev(other, tile, side), device_id_type=MESH,
    )
    fetch(4).wait()
    slip_s[...] = jnp.zeros_like(slip_s)
    slip_s[0:1, 0 : slip.shape[1]] = slip[...]
    pl.when(me + plane > 0)(lambda: pl.semaphore_wait(barrier, me + plane))

    @pl.when(plane > 0)
    def _():
        hail_other(alive.at[tiles])
        slip_copy.start()

    lax.fori_loop(0, me, hail(alive.at[tile]), 0)

    fetch(0).wait()
    dest = owner[...]
    hit = iota((owners, entries), 0) == dest
    before = (iota((entries, entries), 0) < iota((entries, entries), 1)).astype(F32).astype(BF16)
    rank = jnp.dot(hit.astype(F32).astype(BF16), before, preferred_element_type=F32)
    place[...] = jnp.where(hit, rank, -1.0)
    group = min(owners, 512 // capp)
    groups = owners // group
    fetch(1).wait()
    fetch(11).wait()
    gh = green[...]
    slots = iota((group, capp, entries), 1).astype(F32)

    def select(g):
        rows_of = place[pl.ds(pl.multiple_of(g * group, group), group), :]
        chosen = jnp.where(rows_of[:, None, :] == slots, 1.0, 0.0)
        chosen = chosen.reshape(group * capp, entries).astype(BF16)
        chosen_r[pl.ds(g * group * capp, group * capp), :] = chosen
        return chosen

    def fill(g, carry):
        picked = jnp.dot(select(g), gh, preferred_element_type=F32).astype(BF16)
        for h in range(2):
            send[h, pl.ds(g * group, group)] = picked[:, h * 128 : (h + 1) * 128].reshape(group, capp, 128)
        return carry

    fill(0, 0) if groups == 1 else lax.fori_loop(0, groups, fill, 0)

    for i in (2, 3, 5, 6, 7, 8, 9, 10):
        fetch(i).wait()
    raw = depth[...]
    zs[0:rows, 256 : 256 + cols] = jnp.where(wet[...] > 0, raw, 0.0)
    zs[rows : rows + 8, 256 : 256 + cols] = jnp.broadcast_to(raw[0:1], (8, cols))
    for off in (0, 256 + cols):
        zs[rows : rows + 8, off : off + 256] = jnp.zeros((8, 256), F32)

    def pair_copy(src, dst, s_sem, r_sem, d):
        return pltpu.make_async_remote_copy(
            src_ref=src, dst_ref=dst, send_sem=s_sem, recv_sem=r_sem,
            device_id=dev(plane, d // sides, lax.rem(d, sides)), device_id_type=MESH,
        )

    def a2a(h, d):
        return pair_copy(send.at[h, d], recv.at[h, me], a_ss.at[h], a_rs.at[h, me // pack], d)

    def a2a_meta(d):
        return pair_copy(msend.at[d // pack], mrecv.at[me], m_ss.at[0], m_rs.at[me // pack], d)

    def a2a_wait(h, g, n):
        got = recv.at[h, pl.ds(g * pack, n)]
        pair_copy(got, got, a_ss.at[h], a_rs.at[h, g], me).wait_recv()

    def meta_wait(g, n):
        got = mrecv.at[pl.ds(g * pack, n)]
        pair_copy(got, got, m_ss.at[0], m_rs.at[g], me).wait_recv()

    middle = tiles // 2
    cut = jnp.where(tile < middle, middle, 0)

    def launch_tile(t, start):
        first = t * sides

        def own(i, carry):
            start(first + lax.rem(side + i, sides)).start()
            return carry

        lax.fori_loop(jnp.where(t == tile, 1, 0), sides, own, 0)

    def launch_across(start):
        lax.fori_loop(
            0, tiles, lambda i, c: (launch_tile(lax.rem(cut + i, tiles), start), c)[1], 0
        )

    def launch_one(d, carry):
        a2a(0, d).start()
        return carry

    def launch_met(t, carry):
        pl.semaphore_wait(alive.at[t], sides)
        launch_tile(t, functools.partial(a2a, 0))
        return carry

    lax.fori_loop(0, me, launch_one, 0)
    @pl.when(plane == 0)
    def _():
        pl.semaphore_wait(alive.at[tiles], 1)
        slip_copy.start()

    pl.when(side < sides - 1)(lambda: pl.semaphore_wait(alive.at[tile], sides - 1 - side))
    lax.fori_loop(me + 1, (tile + 1) * sides, launch_one, 0)
    lax.fori_loop(tile + 1, tiles, launch_met, 0)

    moves = [(0, -1), (0, 1), (-1, 0), (1, 0), (-1, -1), (-1, 1), (1, -1), (1, 1)]

    def static_copy(i):
        dy, dx = moves[i]
        lanes = (
            slice(0, 512 - 128) if dx == -1
            else slice(cols + 128, cols + 512) if dx == 1 else slice(0, 256 + cols)
        )
        sel = slice(0, rows + 8) if dy == 0 else slice(0, 8) if dy == -1 else slice(rows - 8, rows)
        bi = 0 if dy == -1 else 1
        bj = 0 if dx == -1 else 1
        dst = zside.at[bj] if dy == 0 else zvert.at[bi] if dx == 0 else zcorn.at[bi, bj]
        return pltpu.make_async_remote_copy(
            src_ref=zs.at[sel, lanes], dst_ref=dst, send_sem=i_s.at[i], recv_sem=z_rs.at[i],
            device_id=dev(plane, tile + dy, side + dx), device_id_type=MESH,
        )

    def inside(dy, dx):
        ok = True
        for at, by, size in ((tile, dy, tiles), (side, dx, sides)):
            if by == -1:
                ok = jnp.logical_and(ok, at > 0)
            if by == 1:
                ok = jnp.logical_and(ok, at < size - 1)
        return ok

    slip_copy.wait_recv()

    mrow = iota((8, slip.shape[1]), 0)
    own_h, own_l = split2(slip[...])
    oth_h, oth_l = split2(slip_r[0:1, 0 : slip.shape[1]])
    parts = jnp.where(mrow == 1, own_h, 0.0)
    for i, part in ((2, own_l), (3, oth_h), (4, oth_l)):
        parts = jnp.where(mrow == i, part, parts)
    picks = (iota((slip.shape[1], entries), 0) == fault[...]).astype(F32).astype(BF16)
    meta = jnp.dot(parts.astype(BF16), picks, preferred_element_type=F32)
    meta = jnp.where(iota((8, entries), 0) == 0, index[...].astype(F32), meta).astype(BF16)

    def describe(g, carry):
        told = lax.dot_general(
            meta, chosen_r[pl.ds(g * group * capp, group * capp), :], (((1,), (1,)), ((), ())), preferred_element_type=F32
        )
        for i in range(group // pack):
            msend[g * (group // pack) + i] = told[:, i * 128 : (i + 1) * 128].astype(BF16)
        return carry

    describe(0, 0) if groups == 1 else lax.fori_loop(0, groups, describe, 0)

    launch_across(a2a_meta)
    launch_across(functools.partial(a2a, 1))

    fl = iota((fw, cw), 0)
    fmap = jnp.where(fl < cols + 64, fl // RATIO, fl // RATIO + (cw - fw // RATIO))
    amat[...] = jnp.where(fmap == iota((fw, cw), 1), 1.0 / (RATIO * RATIO), 0.0).astype(BF16)
    rl = iota((cw, fw), 1)
    rmap = jnp.where(rl < cols + 64, rl // RATIO, rl // RATIO + (cw - fw // RATIO))
    rmat[...] = jnp.where(rmap == iota((cw, fw), 0), 1.0, 0.0).astype(BF16)
    for ref in (lev, held, gc, gr, clev, cheld, cgc, cgr):
        ref[...] = jnp.zeros_like(ref)

    for bj in range(2):
        dx = 1 if bj == 0 else -1
        @pl.when(jnp.logical_not(inside(0, dx)))
        def _(bj=bj):
            zside[bj] = jnp.zeros(zside.shape[1:], F32)
        for bi in range(2):
            dy = 1 if bi == 0 else -1
            @pl.when(jnp.logical_not(inside(dy, dx)))
            def _(bi=bi, bj=bj):
                zcorn[bi, bj] = jnp.zeros(zcorn.shape[2:], F32)
    for bi in range(2):
        dy = 1 if bi == 0 else -1
        @pl.when(jnp.logical_not(inside(dy, 0)))
        def _(bi=bi):
            zvert[bi] = jnp.zeros(zvert.shape[1:], F32)
    wrow = iota((4 * rows, 128), 0)
    in_tile = lax.rem(wrow, rows).astype(F32)
    mlane = iota((8, 128), 1)
    recv[0, me] = send[0, me]
    recv[1, me] = send[1, me]
    mrecv[me] = msend[me // pack]

    def product(h, g, weight):
        block = recv[h, pl.ds(g * pack, pack)].reshape(128, 128)
        return jnp.dot(weight, block, preferred_element_type=F32)

    def put(g):
        told = jnp.zeros((8, 128), F32)
        for j in range(pack):
            moved = pltpu.roll(
                mrecv[g * pack + j].astype(F32), lax.rem(j + pack - lax.rem(me, pack), pack) * capp, 1
            )
            told = jnp.where((mlane >= j * capp) & (mlane < (j + 1) * capp), moved, told)
        weight = jnp.where(
            wrow < rows, told[1:2],
            jnp.where(wrow < 2 * rows, told[3:4], jnp.where(wrow < 3 * rows, told[2:3], told[4:5])),
        )
        weight = jnp.where(in_tile == told[0:1], weight, 0.0).astype(BF16)
        weights[g] = weight
        return product(0, g, weight)

    mine = me // pack

    def take(i, carry):
        g = lax.rem(mine + i, packs)
        a2a_wait(0, g, pack)
        meta_wait(g, pack)
        acc[...] += put(g)
        return carry

    def fold():
        return acc[0 : 2 * rows, :] + acc[2 * rows : 4 * rows, :]

    a2a_wait(0, mine, pack - 1)
    meta_wait(mine, pack - 1)
    acc[...] = put(mine)
    lax.fori_loop(1, packs - 1, take, 0, unroll=packs == 4)
    for i, (dy, dx) in enumerate(moves):
        pl.when(inside(dy, dx))(lambda i=i: static_copy(i).start())

    take(packs - 1, 0)
    half[0] = fold()

    toward = 2 * plane - 1

    def core_copy(h):
        return pltpu.make_async_remote_copy(
            src_ref=half.at[h, rows : 2 * rows, :], dst_ref=hcore.at[h], send_sem=h_ss.at[14 + h],
            recv_sem=h_rs.at[14 + h], device_id=dev(other, tile, side), device_id_type=MESH,
        )

    def halo_copy(h, s, kind, v, q):
        to_plane = plane if s == 0 else other
        dy = 0 if kind == 0 else (-1 if v == 0 else 1)
        r0 = s * rows + (0 if v == 0 else rows - 8)
        if kind == 0:
            src, dst, n = half.at[h, s * rows : (s + 1) * rows, :], hside.at[q], 0
        elif kind == 1:
            src, dst, n = half.at[h, r0 : r0 + 8, :], hvert.at[v, q, h], 1 + v + 4 * h
        else:
            src, dst, n = half.at[h, r0 : r0 + 8, :], hcorn.at[v, q], 3 + v
        return pltpu.make_async_remote_copy(
            src_ref=src, dst_ref=dst, send_sem=h_ss.at[7 * s + n], recv_sem=h_rs.at[n + 7 * q],
            device_id=dev(to_plane, tile + dy, side if kind == 1 else side + toward),
            device_id_type=MESH,
        )

    kinds = [(0, 1, 0), (0, 1, 1), (0, 0, 0), (0, 2, 0), (0, 2, 1), (1, 1, 0), (1, 1, 1)]

    def goes(kind, v, sign):
        dy = 0 if kind == 0 else (-1 if v == 0 else 1) * sign
        ok = inside(dy, 0)
        if kind != 1:
            to = side + toward
            ok = jnp.logical_and(ok, jnp.logical_and(to >= 0, to < sides))
        return ok

    def send_half(half_of):
        core_copy(half_of).start()
        for s in (1, 0):
            for h, kind, v in kinds:
                if h == half_of:
                    pl.when(goes(kind, v, 1))(
                        lambda s=s, h=h, kind=kind, v=v: halo_copy(h, s, kind, v, plane).start()
                    )

    send_half(0)

    def take_inner(i, carry):
        g = lax.rem(mine + i, packs)
        a2a_wait(1, g, pack)
        acc[...] += product(1, g, weights[g])
        return carry

    a2a_wait(1, mine, pack - 1)
    acc[...] = product(1, mine, weights[mine])
    lax.fori_loop(1, packs, take_inner, 0, unroll=packs == 4)
    half[1] = fold()
    send_half(1)

    def comes(kind, v, q):
        dy = 0 if kind == 0 else (1 if v == 0 else -1)
        dx = 0 if kind == 1 else (1 if q == 0 else -1)
        return inside(dy, dx)

    for i, (dy, dx) in enumerate(moves):
        pl.when(inside(-dy, -dx))(lambda i=i: static_copy(i).wait_recv())

    def merge(right, left):
        return jnp.where(iota(right.shape, right.ndim - 1) < 64, right, left)

    def place_static(r0, n, z, zr, zl, sr):
        held[r0 : r0 + n, 0:cols] = z[sr, 256 : 256 + cols]
        held[r0 : r0 + n, cols:fw] = merge(zr[sr, 256:384], zl[sr, 0:128])
        cheld[r0 : r0 + n, 0:ccols] = z[sr, 0:128]
        cheld[r0 : r0 + n, ccols:cw] = merge(zr[sr, 0:128], zl[sr, 128:256])
        clev[r0 : r0 + n, 0:ccols] = z[sr, 128:256]
        clev[r0 : r0 + n, ccols:cw] = merge(zr[sr, 128:256], zl[sr, 256:384])

    place_static(LEAD, rows, zs, zside.at[0], zside.at[1], slice(0, rows))
    place_static(top, 8, zvert.at[0], zcorn.at[0, 0], zcorn.at[0, 1], slice(0, 8))
    place_static(8, 8, zvert.at[1], zcorn.at[1, 0], zcorn.at[1, 1], slice(0, 8))

    @pl.when(tile == 0)
    def _():
        held[LEAD - 1 : LEAD, 0:cols] = depth[0:1, :]
        held[LEAD - 1 : LEAD, cols:fw] = merge(
            zside[0, rows : rows + 1, 256:384], zside[1, rows : rows + 1, 0:128]
        )

    strips = [8 + 8 * i for i in range((rows + 16) // 8)]
    cstrips = [8 + 8 * i for i in range((crows + 16) // 8)]

    def faces(h, k_c, k_r, scale, which):
        width = h.shape[1]
        for b in which:
            here, up = h[b : b + 8, :], h[b - 1 : b + 7, :]
            west = pltpu.roll(here, 1, 1)
            k_c[b : b + 8, :] = jnp.where((here > 0.0) & (west > 0.0), scale * (here + west), 0.0)
            k_r[b : b + 8, :] = jnp.where((here > 0.0) & (up > 0.0), scale * (here + up), 0.0)

    faces(held, kc, kr, 0.5 * 0.5 * 0.5, strips)
    faces(cheld, ckc, ckr, 0.5 * 0.125 * 0.125, cstrips)

    for q in range(2):
        for h, kind, v in kinds:
            dst = hside.at[q] if kind == 0 else hvert.at[v, q, h] if kind == 1 else hcorn.at[v, q]
            @pl.when(jnp.logical_not(comes(kind, v, q)))
            def _(dst=dst):
                dst[...] = jnp.zeros(dst.shape, F32)
            pl.when(comes(kind, v, q))(
                lambda h=h, kind=kind, v=v, q=q: halo_copy(h, 0, kind, v, q).wait_recv()
            )
    for i, (dy, dx) in enumerate(moves):
        pl.when(inside(dy, dx))(lambda i=i: static_copy(i).wait_send())
    core_copy(0).wait_recv()
    core_copy(1).wait_recv()

    def lanes_of(p, h):
        return p * (hw + 128) if h == 0 else 128 + p * 128

    for h in range(2):
        lev[LEAD:top, pl.ds(pl.multiple_of(lanes_of(plane, h), 128), 128)] = half[h, 0:rows, :]
        lev[LEAD:top, pl.ds(pl.multiple_of(lanes_of(other, h), 128), 128)] = hcore[h]
    lev[LEAD:top, cols:fw] = merge(hside[0], hside[1])
    for v, r0 in ((0, top), (1, 8)):
        for q in range(2):
            for h in range(2):
                lev[r0 : r0 + 8, lanes_of(q, h) : lanes_of(q, h) + 128] = hvert[v, q, h]
        lev[r0 : r0 + 8, cols:fw] = merge(hcorn[v, 0], hcorn[v, 1])
    peak_o[...] = lev[LEAD:top, 0:cols]
    total[...] = lev[LEAD:top, :]

    brows = rows // RATIO
    per = crows * RATIO // rows
    nest = brows * tiles
    nested = nest // crows
    ct = tile // per
    cm = lax.rem(tile, per)

    def avg_copy(k, kind):
        if kind == 0:
            src, to = avgs.at[k], ct
            dst = avgr.at[k, pl.ds(pl.multiple_of(LEAD + cm * brows, 8), brows), :]
        elif kind == 1:
            src, to = avgs.at[k, brows - 8 : brows, :], ct + 1
            dst = avgr.at[k, 8:16, :]
        else:
            src, to = avgs.at[k, 0:8, :], ct - 1
            dst = avgr.at[k, LEAD + crows : LEAD + crows + 8, :]
        return pltpu.make_async_remote_copy(
            src_ref=src, dst_ref=dst, send_sem=i_s.at[8 + k if kind == 0 else 2 * kind + k], recv_sem=v_rs.at[k, kind],
            device_id=dev(plane, to, side), device_id_type=MESH,
        )

    def avg_goes(kind):
        if kind == 0:
            return tile > 0
        if kind == 1:
            return jnp.logical_and(cm == per - 1, ct + 1 < nested)
        return jnp.logical_and(cm == 0, ct > 0)

    ways = v_rs.shape[1]

    def avg_send(k):
        for kind in range(ways):
            pl.when(avg_goes(kind))(lambda kind=kind: avg_copy(k, kind).start())

    def avg_wait(k):
        def wait(kind, dst):
            pltpu.make_async_remote_copy(
                src_ref=dst, dst_ref=dst, send_sem=i_s.at[8], recv_sem=v_rs.at[k, kind],
                device_id=dev(plane, tile, side), device_id_type=MESH,
            ).wait_recv()

        pl.when(tile == 0)(lambda: wait(0, avgr.at[k, LEAD + brows : LEAD + per * brows, :]))
        pl.when(tile > 0)(lambda: wait(0, avgr.at[k, LEAD : LEAD + per * brows, :]))
        if ways == 1:
            return
        pl.when(tile > 0)(lambda: wait(1, avgr.at[k, 8:16, :]))
        pl.when(tile < nested - 1)(lambda: wait(2, avgr.at[k, LEAD + crows : LEAD + crows + 8, :]))

    def edge_copy():
        return pltpu.make_async_remote_copy(
            src_ref=edges, dst_ref=edger, send_sem=i_s.at[10], recv_sem=v_rs.at[2, 0],
            device_id=dev(plane, nested, side), device_id_type=MESH,
        )

    ends = nested < tiles
    is_last = tile == tiles - 1

    def push(s_ref, g_c, g_r, k_c, k_r, which):
        for b in which:
            here, up = s_ref[b : b + 8, :], s_ref[b - 1 : b + 7, :]
            g_c[b : b + 8, :] -= k_c[b : b + 8, :] * (here - pltpu.roll(here, 1, 1))
            g_r[b : b + 8, :] -= k_r[b : b + 8, :] * (here - up)

    def spread(g_c, g_r, b):
        east = g_c[b : b + 8, :]
        return (pltpu.roll(east, east.shape[1] - 1, 1) - east) + (
            g_r[b + 1 : b + 9, :] - g_r[b : b + 8, :]
        )

    def means(x):
        high, low = split2(x)
        return jnp.dot(high.astype(BF16), amat[...], preferred_element_type=F32) + jnp.dot(
            low.astype(BF16), amat[...], preferred_element_type=F32
        )

    def block_means(k, x):
        sums = means(x)
        for j in range(cw // 128):
            work[j] = sums[:, j * 128 : (j + 1) * 128]
            avgs[k, :, j * 128 : (j + 1) * 128] = sum(
                work[j, pl.ds(i, brows, stride=RATIO), :] for i in range(RATIO)
            )
        avg_send(k)

        @pl.when(tile == 0)
        def _():
            avgr[k, LEAD : LEAD + brows, :] = avgs[k]

    def stack3(values):
        rows_of = iota((16, values[0].shape[1]), 0)
        out = jnp.zeros(rows_of.shape, F32)
        for i, v in enumerate(values):
            first, rest = split2(v)
            second, third = split2(v - first)
            for j, part in enumerate((first, second, third)):
                out = jnp.where(rows_of == 3 * i + j, part, out)
        return out.astype(BF16)

    def join3(wide, i):
        return wide[3 * i : 3 * i + 1] + wide[3 * i + 1 : 3 * i + 2] + wide[3 * i + 2 : 3 * i + 3]

    wide = jnp.dot(
        stack3([clev[LEAD : LEAD + 1, :], ckc[LEAD : LEAD + 1, :], ckr[LEAD + 1 : LEAD + 2, :]]),
        rmat[...], preferred_element_type=F32,
    )
    kc0, kr1 = join3(wide, 1), join3(wide, 2)
    lane = iota((1, fw), 1)
    odd, upper = lane % 2 == 1, lane % 4 >= 2

    def lane_means(x):
        x = x + jnp.where(odd, pltpu.roll(x, 1, 1), pltpu.roll(x, fw - 1, 1))
        x = x + jnp.where(upper, pltpu.roll(x, 2, 1), pltpu.roll(x, fw - 2, 1))
        return x * (1.0 / (RATIO * RATIO))

    erow = iota((16, fw), 0)

    def step(k, carry, keep=False):
        c0, g0, h1 = carry

        @pl.when(tile == 0)
        def _():
            lev[LEAD - 1 : LEAD, :] = c0

        if ends:
            @pl.when(is_last)
            def _():
                above = jnp.sum(lev[top - 8 : top - 4, :], axis=0, keepdims=True)
                below = jnp.sum(lev[top - 4 : top, :], axis=0, keepdims=True)
                esum[...] = jnp.where(
                    erow == 2 * k, above, jnp.where(erow == 2 * k + 1, below, esum[...])
                )

        mean = lane_means(jnp.sum(lev[LEAD : LEAD + RATIO, :], axis=0, keepdims=True))
        g0 = g0 - kc0 * (c0 - pltpu.roll(c0, RATIO, 1))
        h1 = h1 - kr1 * (mean - c0)
        c0 = c0 - ((pltpu.roll(g0, fw - RATIO, 1) - g0) + h1)
        push(lev, gc, gr, kc, kr, strips)
        for b in strips:
            new = lev[b : b + 8, :] - spread(gc, gr, b)
            lev[b : b + 8, :] = new
            if LEAD <= b < top:
                r = slice(b - LEAD, b - LEAD + 8)
                peak_o[r, :] = jnp.maximum(peak_o[r, :], new[:, 0:cols])
                if keep:
                    total[r, :] += new
        return c0, g0, h1

    zero = jnp.zeros((1, fw), F32)
    carry = lax.fori_loop(
        0, STEPS - 2, functools.partial(step, keep=True), (join3(wide, 0), zero, zero)
    )
    block_means(0, total[...])
    carry = step(STEPS - 2, carry)
    block_means(1, lev[LEAD:top, :])
    carry = step(STEPS - 1, carry)
    if ends:
        @pl.when(is_last)
        def _():
            edges[...] = means(esum[...])
            edge_copy().start()
    surf_o[...] = lev[LEAD:top, 0:cols]

    @pl.when(tile >= nested)
    def _():
        if ends:
            pl.when(tile == nested)(lambda: edge_copy().wait_recv())
        erows = iota((16, cw), 0)
        crow = iota((8, cw), 0)

        def cstep(k, carry):
            def edge(i):
                return jnp.sum(jnp.where(erows == 2 * k + i, edger[...], 0.0), axis=0, keepdims=True)

            @pl.when(tile == nested)
            def _():
                clev[LEAD - 8 : LEAD, :] = jnp.where(crow == 7, edge(0), clev[LEAD - 8 : LEAD, :])
                clev[LEAD : LEAD + 8, :] = jnp.where(crow == 0, edge(1), clev[LEAD : LEAD + 8, :])

            push(clev, cgc, cgr, ckc, ckr, cstrips)
            for b in cstrips:
                clev[b : b + 8, :] -= spread(cgc, cgr, b)
            return carry

        lax.fori_loop(0, STEPS, cstep, 0)
        coarse_o[...] = clev[LEAD : LEAD + crows, 0:ccols]

    @pl.when(tile < nested)
    def _():
        c0, g0, h1 = carry
        narrow = RATIO * jnp.dot(stack3([c0, h1]), amat[...], preferred_element_type=F32)
        avg_wait(0)
        avg_wait(1)
        for b in range(LEAD, LEAD + crows + 8, 8):
            clev[b : b + 8, :] = avgr[0, b - 1 : b + 7, :] + avgr[1, b - 1 : b + 7, :]
        clev[LEAD - 1 : LEAD, :] = avgr[0, LEAD - 2 : LEAD - 1, :] + avgr[1, LEAD - 2 : LEAD - 1, :]
        inner = range(LEAD, LEAD + crows + 8, 8)
        push(clev, cgc, cgr, ckc, ckr, inner)

        @pl.when(tile == 0)
        def _():
            cgr[LEAD + 1 : LEAD + 2, :] = join3(narrow, 1)

        for b in range(LEAD, LEAD + crows, 8):
            new = avgr[1, b - 1 : b + 7, :] - spread(cgc, cgr, b)
            coarse_o[b - LEAD : b - LEAD + 8, :] = new[:, 0:ccols]

        @pl.when(tile == 0)
        def _():
            coarse_o[0:1, :] = join3(narrow, 0)[:, 0:ccols]

    slip_copy.wait_send()
    rest = pl.ds(0, owners - 1)
    for h in range(2):
        pair_copy(send.at[h, rest], recv.at[h, rest], a_ss.at[h], a_rs.at[h, 0], me).wait_send()
    pair_copy(mrecv.at[rest], mrecv.at[rest], m_ss.at[0], m_rs.at[0], me).wait_send()
    for h in range(2):
        core_copy(h).wait_send()
    for s in (1, 0):
        for h, kind, v in kinds:
            pl.when(goes(kind, v, 1))(
                lambda s=s, h=h, kind=kind, v=v: halo_copy(h, s, kind, v, plane).wait_send()
            )
    for k in range(2):
        for kind in range(ways):
            pl.when(avg_goes(kind))(lambda k=k, kind=kind: avg_copy(k, kind).wait_send())
    if ends:
        pl.when(is_last)(lambda: edge_copy().wait_send())


def store(peak, surf, coarse, peak_h, surf_h, coarse_h, sems):
    pairs = [(peak, peak_h), (surf, surf_h), (coarse, coarse_h)]
    copies = [pltpu.make_async_copy(src, dst, sems.at[i]) for i, (src, dst) in enumerate(pairs)]
    for copy in copies:
        copy.start()
    for copy in copies:
        copy.wait()


def shards(dims, green, row_owner, row_index, row_fault, slip, depth, wet, coarse_depth, coarse_start):
    planes, tiles, cols_n, subs_n = dims
    owners = tiles * cols_n * subs_n
    entries, cols = green.shape
    rows = depth.shape[0]
    crows, ccols = coarse_depth.shape
    capacity = max(2, (2 * entries + owners - 1) // owners)
    capp = (capacity + 15) // 16 * 16
    packs = owners // (128 // capp)
    hw = cols // planes
    i32 = lambda *shape: pltpu.VMEM(shape, jnp.int32)
    ways = 3 if tiles * (rows // RATIO) // crows > 1 else 1
    fw, cw = cols + 128, ccols + 128
    high, chigh = rows + 32, crows + 32
    vmem = lambda *shape: pltpu.VMEM(shape, F32)
    dma = pltpu.SemaphoreType.DMA
    keep = lambda x: pltpu.with_memory_space_constraint(x, pltpu.HBM)
    results = pl.pallas_call(
        functools.partial(kernel, dims),
        out_shape=(
            jax.ShapeDtypeStruct((rows, cols), F32),
            jax.ShapeDtypeStruct((rows, cols), F32),
            jax.ShapeDtypeStruct((crows, ccols), F32),
        ),
        in_specs=[pl.BlockSpec(memory_space=pltpu.HBM)] * 9,
        out_specs=(pl.BlockSpec(memory_space=pltpu.VMEM),) * 3,
        scratch_shapes=[
            pltpu.VMEM((entries, hw), BF16), i32(1, entries), i32(1, entries), i32(1, entries),
            vmem(1, slip.shape[0]), vmem(rows, cols), i32(rows, cols),
            pltpu.VMEM((owners * capp, entries), BF16), vmem(owners, entries),
            pltpu.VMEM((2, owners, capp, 128), BF16),
            pltpu.VMEM((2, owners, capp, 128), BF16),
            pltpu.VMEM((packs, 8, 128), BF16), pltpu.VMEM((owners, 8, 128), BF16),
            vmem(8, 128), vmem(8, 128), vmem(4 * rows, 128),
            pltpu.VMEM((packs, 4 * rows, 128), BF16),
            vmem(rows + 8, cols + 512), vmem(2, rows + 8, 384), vmem(2, 8, cols + 256),
            vmem(2, 2, 8, 384),
            vmem(2, 2 * rows, 128), vmem(2, rows, 128), vmem(2, rows, 128), vmem(2, 2, 2, 8, 128),
            vmem(2, 2, 8, 128),
        ]
        + [vmem(high, fw)] * 6
        + [vmem(chigh, cw)] * 6
        + [
            pltpu.VMEM((fw, cw), BF16), pltpu.VMEM((cw, fw), BF16),
            vmem(cw // 128, rows, 128),
            vmem(rows, fw), vmem(2, rows // RATIO, cw), vmem(2, chigh, cw),
            vmem(16, fw), vmem(16, cw), vmem(16, cw),
            dma((12,)), dma((2,)), dma((2, packs)), dma((1,)), dma((packs,)), dma((2,)), dma((8,)), dma((16,)),
            dma((16,)), dma((3, ways)), pltpu.SemaphoreType.REGULAR((tiles + 1,)),
        ],
        compiler_params=pltpu.CompilerParams(
            collective_id=0, has_side_effects=True, vmem_limit_bytes=48 * 1024 * 1024
        ),
    )(
        keep(green), keep(row_owner.reshape(1, entries)), keep(row_index.reshape(1, entries)),
        keep(row_fault.reshape(1, entries)), keep(slip.reshape(1, -1)), keep(depth), keep(wet), keep(coarse_depth), keep(coarse_start),
    )
    return pl.pallas_call(
        store,
        out_shape=tuple(jax.ShapeDtypeStruct(x.shape, F32) for x in results),
        in_specs=[pl.BlockSpec(memory_space=pltpu.VMEM)] * 3,
        out_specs=(pl.BlockSpec(memory_space=pltpu.HBM),) * 3,
        scratch_shapes=[dma((3,))],
        compiler_params=pltpu.CompilerParams(vmem_limit_bytes=1024 * 1024),
    )(*results)


def solution(mesh):
    dims = tuple(mesh.shape[a] for a in ("scen", "tile", "col", "sub"))
    return jax.shard_map(
        functools.partial(shards, dims),
        mesh=mesh,
        in_specs=(
            P(("tile", "col", "sub"), None),
            P(("tile", "col", "sub"), None),
            P(("tile", "col", "sub")),
            P(("tile", "col", "sub")),
            P(("scen", "tile", "col", "sub")),
            P("tile", ("col", "sub")),
            P("tile", ("col", "sub")),
            P("tile", ("col", "sub")),
            P(("scen", "tile"), ("col", "sub")),
        ),
        out_specs=(
            P(("scen", "tile"), ("col", "sub")),
            P(("scen", "tile"), ("col", "sub")),
            P(("scen", "tile"), ("col", "sub")),
        ),
        check_vma=False,
    )
```

```python
import functools
import jax
import jax.numpy as jnp
from jax import lax
from jax.experimental import pallas as pl
from jax.experimental.pallas import tpu as pltpu
from jax.sharding import PartitionSpec as P

RATIO = 4
STEPS = 6
HALO = 8
LEAD = 16
F32 = jnp.float32
BF16 = jnp.bfloat16
MESH = pl.DeviceIdType.MESH


def split2(x):
    high = x.astype(BF16).astype(F32)
    return high, (x - high).astype(BF16).astype(F32)


def iota(shape, dim):
    return lax.broadcasted_iota(jnp.int32, shape, dim)


def kernel(
    dims,
    green_h, owner_h, index_h, fault_h, slip_h, depth_h, wet_h, cdep_h, cstart_h,
    peak_o, surf_o, coarse_o,
    green, owner, index, fault, slip, depth, wet, chosen_r,
    place, send, recv, msend, mrecv, slip_s, slip_r, acc, weights,
    zs, zside, zvert, zcorn,
    half, hcore, hside, hvert, hcorn,
    lev, held, gc, gr, kc, kr,
    clev, cheld, cgc, cgr, ckc, ckr,
    amat, rmat, work, total, avgs, avgr, esum, edges, edger,
    i_s, a_ss, a_rs, m_ss, m_rs, sl_s, z_rs, h_ss, h_rs, v_rs, alive,
):
    planes, tiles, cols_n, subs_n = dims
    sides = cols_n * subs_n
    owners = tiles * sides
    plane = lax.axis_index("scen")
    tile = lax.axis_index("tile")
    side = lax.axis_index("col") * subs_n + lax.axis_index("sub")
    me = tile * sides + side
    rows, cols = depth.shape
    crows, ccols = cdep_h.shape
    entries, hw = green.shape
    capp = send.shape[2]
    pack = 128 // capp
    packs = owners // pack
    fw = cols + 128
    cw = ccols + 128
    top = LEAD + rows

    def dev(p, t, c):
        return {"scen": p, "tile": t, "col": c // subs_n, "sub": c % subs_n}

    def fetch(i):
        edge_lanes = pl.ds(pl.multiple_of(plane * (hw + 128), 128), 128)
        inner_lanes = pl.ds(pl.multiple_of(128 + plane * 128, 128), 128)
        far = 256 + cols
        src, dst = [
            (owner_h, owner), (green_h.at[:, edge_lanes], green.at[:, 0:128]), (index_h, index), (fault_h, fault),
            (slip_h, slip), (depth_h, depth), (wet_h, wet),
            (cdep_h, zs.at[0:rows, 0:ccols]), (cstart_h, zs.at[0:rows, 128 : 128 + ccols]),
            (cdep_h, zs.at[0:rows, far : far + ccols]),
            (cstart_h, zs.at[0:rows, far + 128 : far + 128 + ccols]),
            (green_h.at[:, inner_lanes], green.at[:, 128:256]),
        ][i]
        return pltpu.make_async_copy(src, dst, i_s.at[i])

    barrier = pltpu.get_barrier_semaphore()

    other = planes - 1 - plane

    def hail(sem):
        def start(i, carry):
            pl.semaphore_signal(
                sem, inc=1, device_id=dev(plane, i // sides, lax.rem(i, sides)), device_id_type=MESH
            )
            return carry

        return start

    def hail_other(sem):
        pl.semaphore_signal(sem, inc=1, device_id=dev(other, tile, side), device_id_type=MESH)

    lax.fori_loop(me + 1, owners, hail(barrier), 0)
    pl.when(plane == 0)(lambda: hail_other(barrier))
    for i in (4, 0, 1, 11, 2, 3, 5, 6, 7, 8, 9, 10):
        fetch(i).start()

    slip_copy = pltpu.make_async_remote_copy(
        src_ref=slip_s, dst_ref=slip_r, send_sem=sl_s.at[0], recv_sem=sl_s.at[1],
        device_id=dev(other, tile, side), device_id_type=MESH,
    )
    fetch(4).wait()
    slip_s[...] = jnp.zeros_like(slip_s)
    slip_s[0:1, 0 : slip.shape[1]] = slip[...]
    pl.when(me + plane > 0)(lambda: pl.semaphore_wait(barrier, me + plane))

    @pl.when(plane > 0)
    def _():
        hail_other(alive.at[tiles])
        slip_copy.start()

    lax.fori_loop(0, me, hail(alive.at[tile]), 0)

    fetch(0).wait()
    dest = owner[...]
    hit = iota((owners, entries), 0) == dest
    before = (iota((entries, entries), 0) < iota((entries, entries), 1)).astype(F32).astype(BF16)
    rank = jnp.dot(hit.astype(F32).astype(BF16), before, preferred_element_type=F32)
    place[...] = jnp.where(hit, rank, -1.0)
    group = min(owners, 512 // capp)
    groups = owners // group
    fetch(1).wait()
    fetch(11).wait()
    gh = green[...]
    slots = iota((group, capp, entries), 1).astype(F32)

    def select(g):
        rows_of = place[pl.ds(pl.multiple_of(g * group, group), group), :]
        chosen = jnp.where(rows_of[:, None, :] == slots, 1.0, 0.0)
        chosen = chosen.reshape(group * capp, entries).astype(BF16)
        chosen_r[pl.ds(g * group * capp, group * capp), :] = chosen
        return chosen

    def fill(g, carry):
        picked = jnp.dot(select(g), gh, preferred_element_type=F32).astype(BF16)
        for h in range(2):
            send[h, pl.ds(g * group, group)] = picked[:, h * 128 : (h + 1) * 128].reshape(group, capp, 128)
        return carry

    fill(0, 0) if groups == 1 else lax.fori_loop(0, groups, fill, 0)

    for i in (2, 3, 5, 6, 7, 8, 9, 10):
        fetch(i).wait()
    raw = depth[...]
    zs[0:rows, 256 : 256 + cols] = jnp.where(wet[...] > 0, raw, 0.0)
    zs[rows : rows + 8, 256 : 256 + cols] = jnp.broadcast_to(raw[0:1], (8, cols))
    for off in (0, 256 + cols):
        zs[rows : rows + 8, off : off + 256] = jnp.zeros((8, 256), F32)

    def pair_copy(src, dst, s_sem, r_sem, d):
        return pltpu.make_async_remote_copy(
            src_ref=src, dst_ref=dst, send_sem=s_sem, recv_sem=r_sem,
            device_id=dev(plane, d // sides, lax.rem(d, sides)), device_id_type=MESH,
        )

    def a2a(h, d):
        return pair_copy(send.at[h, d], recv.at[h, me], a_ss.at[h], a_rs.at[h, me // pack], d)

    def a2a_meta(d):
        return pair_copy(msend.at[d], mrecv.at[me], m_ss.at[0], m_rs.at[me // pack], d)

    def a2a_wait(h, g, n):
        got = recv.at[h, pl.ds(g * pack, n)]
        pair_copy(got, got, a_ss.at[h], a_rs.at[h, g], me).wait_recv()

    def meta_wait(g, n):
        got = mrecv.at[pl.ds(g * pack, n)]
        pair_copy(got, got, m_ss.at[0], m_rs.at[g], me).wait_recv()

    middle = tiles // 2
    cut = jnp.where(tile < middle, middle, 0)

    def launch_tile(t, start):
        first = t * sides

        def own(i, carry):
            start(first + lax.rem(side + i, sides)).start()
            return carry

        lax.fori_loop(jnp.where(t == tile, 1, 0), sides, own, 0)

    def launch_across(start):
        lax.fori_loop(
            0, tiles, lambda i, c: (launch_tile(lax.rem(cut + i, tiles), start), c)[1], 0
        )

    def launch_one(d, carry):
        a2a(0, d).start()
        return carry

    def launch_met(t, carry):
        pl.semaphore_wait(alive.at[t], sides)
        launch_tile(t, functools.partial(a2a, 0))
        return carry

    lax.fori_loop(0, me, launch_one, 0)
    @pl.when(plane == 0)
    def _():
        pl.semaphore_wait(alive.at[tiles], 1)
        slip_copy.start()

    pl.when(side < sides - 1)(lambda: pl.semaphore_wait(alive.at[tile], sides - 1 - side))
    lax.fori_loop(me + 1, (tile + 1) * sides, launch_one, 0)
    lax.fori_loop(tile + 1, tiles, launch_met, 0)

    moves = [(0, -1), (0, 1), (-1, 0), (1, 0), (-1, -1), (-1, 1), (1, -1), (1, 1)]

    def static_copy(i):
        dy, dx = moves[i]
        lanes = (
            slice(0, 512 - 128) if dx == -1
            else slice(cols + 128, cols + 512) if dx == 1 else slice(0, 256 + cols)
        )
        sel = slice(0, rows + 8) if dy == 0 else slice(0, 8) if dy == -1 else slice(rows - 8, rows)
        bi = 0 if dy == -1 else 1
        bj = 0 if dx == -1 else 1
        dst = zside.at[bj] if dy == 0 else zvert.at[bi] if dx == 0 else zcorn.at[bi, bj]
        return pltpu.make_async_remote_copy(
            src_ref=zs.at[sel, lanes], dst_ref=dst, send_sem=i_s.at[i], recv_sem=z_rs.at[i],
            device_id=dev(plane, tile + dy, side + dx), device_id_type=MESH,
        )

    def inside(dy, dx):
        ok = True
        for at, by, size in ((tile, dy, tiles), (side, dx, sides)):
            if by == -1:
                ok = jnp.logical_and(ok, at > 0)
            if by == 1:
                ok = jnp.logical_and(ok, at < size - 1)
        return ok

    slip_copy.wait_recv()

    mrow = iota((8, slip.shape[1]), 0)
    own_h, own_l = split2(slip[...])
    oth_h, oth_l = split2(slip_r[0:1, 0 : slip.shape[1]])
    parts = jnp.where(mrow == 1, own_h, 0.0)
    for i, part in ((2, own_l), (3, oth_h), (4, oth_l)):
        parts = jnp.where(mrow == i, part, parts)
    picks = (iota((slip.shape[1], entries), 0) == fault[...]).astype(F32).astype(BF16)
    meta = jnp.dot(parts.astype(BF16), picks, preferred_element_type=F32)
    meta = jnp.where(iota((8, entries), 0) == 0, index[...].astype(F32), meta).astype(BF16)

    lane_of = iota((1, 128), 1)
    within = [(lane_of >= i * capp) & (lane_of < (i + 1) * capp) for i in range(pack)]

    def shifted(x, by):
        by = by % pack
        return pltpu.roll(x, by * capp, 1) if by else x

    def describe(g, carry):
        told = lax.dot_general(
            meta, chosen_r[pl.ds(g * group * capp, group * capp), :], (((1,), (1,)), ((), ())), preferred_element_type=F32
        )
        quantities = [told[0:1], told[1:2] + told[2:3], told[3:4] + told[4:5]]
        for i in range(group // pack):
            parts_of = [q[:, i * 128 : (i + 1) * 128] for q in quantities]
            for j in range(pack):
                record = jnp.zeros((1, 128), F32)
                for q, part in enumerate(parts_of):
                    record = jnp.where(within[q], shifted(part, q - j), record)
                msend[g * group + i * pack + j] = record
        return carry

    describe(0, 0) if groups == 1 else lax.fori_loop(0, groups, describe, 0)

    launch_across(a2a_meta)
    launch_across(functools.partial(a2a, 1))

    fl = iota((fw, cw), 0)
    fmap = jnp.where(fl < cols + 64, fl // RATIO, fl // RATIO + (cw - fw // RATIO))
    amat[...] = jnp.where(fmap == iota((fw, cw), 1), 1.0 / (RATIO * RATIO), 0.0).astype(BF16)
    rl = iota((cw, fw), 1)
    rmap = jnp.where(rl < cols + 64, rl // RATIO, rl // RATIO + (cw - fw // RATIO))
    rmat[...] = jnp.where(rmap == iota((cw, fw), 0), 1.0, 0.0).astype(BF16)
    for ref in (lev, held, gc, gr, clev, cheld, cgc, cgr):
        ref[...] = jnp.zeros_like(ref)

    for bj in range(2):
        dx = 1 if bj == 0 else -1
        @pl.when(jnp.logical_not(inside(0, dx)))
        def _(bj=bj):
            zside[bj] = jnp.zeros(zside.shape[1:], F32)
        for bi in range(2):
            dy = 1 if bi == 0 else -1
            @pl.when(jnp.logical_not(inside(dy, dx)))
            def _(bi=bi, bj=bj):
                zcorn[bi, bj] = jnp.zeros(zcorn.shape[2:], F32)
    for bi in range(2):
        dy = 1 if bi == 0 else -1
        @pl.when(jnp.logical_not(inside(dy, 0)))
        def _(bi=bi):
            zvert[bi] = jnp.zeros(zvert.shape[1:], F32)
    wrow = iota((4 * rows, 128), 0)
    in_tile = lax.rem(wrow, rows).astype(F32)
    recv[0, me] = send[0, me]
    recv[1, me] = send[1, me]
    mrecv[me] = msend[me]

    def product(h, g, weight):
        block = recv[h, pl.ds(g * pack, pack)].reshape(128, 128)
        return jnp.dot(weight, block, preferred_element_type=F32)

    def put(g):
        told = [jnp.zeros((1, 128), F32)] * 3
        for j in range(pack):
            record = mrecv[g * pack + j]
            told = [jnp.where(within[j], shifted(record, j - q), t) for q, t in enumerate(told)]
        (own_h, own_l), (oth_h, oth_l) = split2(told[1]), split2(told[2])
        weight = jnp.where(
            wrow < rows, own_h,
            jnp.where(wrow < 2 * rows, oth_h, jnp.where(wrow < 3 * rows, own_l, oth_l)),
        )
        weight = jnp.where(in_tile == told[0], weight, 0.0).astype(BF16)
        weights[g] = weight
        return product(0, g, weight)

    mine = me // pack

    def take(i, carry):
        g = lax.rem(mine + i, packs)
        a2a_wait(0, g, pack)
        meta_wait(g, pack)
        acc[...] += put(g)
        return carry

    def fold():
        return acc[0 : 2 * rows, :] + acc[2 * rows : 4 * rows, :]

    a2a_wait(0, mine, pack - 1)
    meta_wait(mine, pack - 1)
    acc[...] = put(mine)
    lax.fori_loop(1, packs - 1, take, 0, unroll=packs == 4)
    for i, (dy, dx) in enumerate(moves):
        pl.when(inside(dy, dx))(lambda i=i: static_copy(i).start())

    take(packs - 1, 0)
    half[0] = fold()

    toward = 2 * plane - 1

    def core_copy(h):
        return pltpu.make_async_remote_copy(
            src_ref=half.at[h, rows : 2 * rows, :], dst_ref=hcore.at[h], send_sem=h_ss.at[5],
            recv_sem=h_rs.at[8], device_id=dev(other, tile, side), device_id_type=MESH,
        )

    def halo_copy(h, s, kind, v, q):
        to_plane = plane if s == 0 else other
        dy = 0 if kind == 0 else (-1 if v == 0 else 1)
        r0 = s * rows + (0 if v == 0 else rows - 8)
        if kind == 0:
            src, dst, n, m = half.at[h, s * rows : (s + 1) * rows, :], hside.at[q], 2, 2 + q
        elif kind == 1:
            src, dst, n, m = half.at[h, r0 : r0 + 8, :], hvert.at[v, q, h], v, v
        else:
            src, dst, n, m = half.at[h, r0 : r0 + 8, :], hcorn.at[v, q], 3 + v, 4 + 2 * v + q
        return pltpu.make_async_remote_copy(
            src_ref=src, dst_ref=dst, send_sem=h_ss.at[n], recv_sem=h_rs.at[m],
            device_id=dev(to_plane, tile + dy, side if kind == 1 else side + toward),
            device_id_type=MESH,
        )

    kinds = [(0, 1, 0), (0, 1, 1), (0, 0, 0), (0, 2, 0), (0, 2, 1), (1, 1, 0), (1, 1, 1)]

    def goes(kind, v, sign):
        dy = 0 if kind == 0 else (-1 if v == 0 else 1) * sign
        ok = inside(dy, 0)
        if kind != 1:
            to = side + toward
            ok = jnp.logical_and(ok, jnp.logical_and(to >= 0, to < sides))
        return ok

    def send_half(half_of):
        core_copy(half_of).start()
        for s in (1, 0):
            for h, kind, v in kinds:
                if h == half_of:
                    pl.when(goes(kind, v, 1))(
                        lambda s=s, h=h, kind=kind, v=v: halo_copy(h, s, kind, v, plane).start()
                    )

    send_half(0)

    def take_inner(i, carry):
        g = lax.rem(mine + i, packs)
        a2a_wait(1, g, pack)
        acc[...] += product(1, g, weights[g])
        return carry

    a2a_wait(1, mine, pack - 1)
    acc[...] = product(1, mine, weights[mine])
    lax.fori_loop(1, packs, take_inner, 0, unroll=packs == 4)
    half[1] = fold()
    send_half(1)

    def comes(kind, v, q):
        dy = 0 if kind == 0 else (1 if v == 0 else -1)
        dx = 0 if kind == 1 else (1 if q == 0 else -1)
        return inside(dy, dx)

    for i, (dy, dx) in enumerate(moves):
        pl.when(inside(-dy, -dx))(lambda i=i: static_copy(i).wait_recv())

    def merge(right, left):
        return jnp.where(iota(right.shape, right.ndim - 1) < 64, right, left)

    def place_static(r0, n, z, zr, zl, sr):
        held[r0 : r0 + n, 0:cols] = z[sr, 256 : 256 + cols]
        held[r0 : r0 + n, cols:fw] = merge(zr[sr, 256:384], zl[sr, 0:128])
        cheld[r0 : r0 + n, 0:ccols] = z[sr, 0:128]
        cheld[r0 : r0 + n, ccols:cw] = merge(zr[sr, 0:128], zl[sr, 128:256])
        clev[r0 : r0 + n, 0:ccols] = z[sr, 128:256]
        clev[r0 : r0 + n, ccols:cw] = merge(zr[sr, 128:256], zl[sr, 256:384])

    place_static(LEAD, rows, zs, zside.at[0], zside.at[1], slice(0, rows))
    place_static(top, 8, zvert.at[0], zcorn.at[0, 0], zcorn.at[0, 1], slice(0, 8))
    place_static(8, 8, zvert.at[1], zcorn.at[1, 0], zcorn.at[1, 1], slice(0, 8))

    @pl.when(tile == 0)
    def _():
        held[LEAD - 1 : LEAD, 0:cols] = depth[0:1, :]
        held[LEAD - 1 : LEAD, cols:fw] = merge(
            zside[0, rows : rows + 1, 256:384], zside[1, rows : rows + 1, 0:128]
        )

    strips = [8 + 8 * i for i in range((rows + 16) // 8)]
    cstrips = [8 + 8 * i for i in range((crows + 16) // 8)]

    def faces(h, k_c, k_r, scale, which):
        width = h.shape[1]
        for b in which:
            here, up = h[b : b + 8, :], h[b - 1 : b + 7, :]
            west = pltpu.roll(here, 1, 1)
            k_c[b : b + 8, :] = jnp.where((here > 0.0) & (west > 0.0), scale * (here + west), 0.0)
            k_r[b : b + 8, :] = jnp.where((here > 0.0) & (up > 0.0), scale * (here + up), 0.0)

    faces(held, kc, kr, 0.5 * 0.5 * 0.5, strips)
    faces(cheld, ckc, ckr, 0.5 * 0.125 * 0.125, cstrips)

    def stack3(values):
        rows_of = iota((16, values[0].shape[1]), 0)
        out = jnp.zeros(rows_of.shape, F32)
        for i, v in enumerate(values):
            first, rest = split2(v)
            second, third = split2(v - first)
            for j, part in enumerate((first, second, third)):
                out = jnp.where(rows_of == 3 * i + j, part, out)
        return out.astype(BF16)

    def join3(wide, i):
        return wide[3 * i : 3 * i + 1] + wide[3 * i + 1 : 3 * i + 2] + wide[3 * i + 2 : 3 * i + 3]

    wide = jnp.dot(
        stack3([clev[LEAD : LEAD + 1, :], ckc[LEAD : LEAD + 1, :], ckr[LEAD + 1 : LEAD + 2, :]]),
        rmat[...], preferred_element_type=F32,
    )
    kc0, kr1 = join3(wide, 1), join3(wide, 2)
    def landed(dst, n, m):
        return pltpu.make_async_remote_copy(
            src_ref=dst, dst_ref=dst, send_sem=h_ss.at[n], recv_sem=h_rs.at[m],
            device_id=dev(other, tile, side), device_id_type=MESH,
        )

    arrivals = [(1, v, 0, hvert.at[v], v) for v in range(2)]
    for q in range(2):
        arrivals.append((0, 0, q, hside.at[q], 2 + q))
        arrivals += [(2, v, q, hcorn.at[v, q], 4 + 2 * v + q) for v in range(2)]
    for kind, v, q, dst, m in arrivals:
        @pl.when(jnp.logical_not(comes(kind, v, q)))
        def _(dst=dst):
            dst[...] = jnp.zeros(dst.shape, F32)
        pl.when(comes(kind, v, q))(lambda dst=dst, m=m: landed(dst, 5, m).wait_recv())
    landed(hcore, 5, 8).wait_recv()

    for i, (dy, dx) in enumerate(moves):
        pl.when(inside(dy, dx))(lambda i=i: static_copy(i).wait_send())

    def lanes_of(p, h):
        return p * (hw + 128) if h == 0 else 128 + p * 128

    for h in range(2):
        lev[LEAD:top, pl.ds(pl.multiple_of(lanes_of(plane, h), 128), 128)] = half[h, 0:rows, :]
        lev[LEAD:top, pl.ds(pl.multiple_of(lanes_of(other, h), 128), 128)] = hcore[h]
    lev[LEAD:top, cols:fw] = merge(hside[0], hside[1])
    for v, r0 in ((0, top), (1, 8)):
        for q in range(2):
            for h in range(2):
                lev[r0 : r0 + 8, lanes_of(q, h) : lanes_of(q, h) + 128] = hvert[v, q, h]
        lev[r0 : r0 + 8, cols:fw] = merge(hcorn[v, 0], hcorn[v, 1])
    peak_o[...] = lev[LEAD:top, 0:cols]
    total[...] = lev[LEAD:top, :]

    brows = rows // RATIO
    per = crows * RATIO // rows
    nest = brows * tiles
    nested = nest // crows
    ct = tile // per
    cm = lax.rem(tile, per)

    def avg_copy(k, kind):
        if kind == 0:
            src, to = avgs.at[k], ct
            dst = avgr.at[k, pl.ds(pl.multiple_of(LEAD + cm * brows, 8), brows), :]
        elif kind == 1:
            src, to = avgs.at[k, brows - 8 : brows, :], ct + 1
            dst = avgr.at[k, 8:16, :]
        else:
            src, to = avgs.at[k, 0:8, :], ct - 1
            dst = avgr.at[k, LEAD + crows : LEAD + crows + 8, :]
        return pltpu.make_async_remote_copy(
            src_ref=src, dst_ref=dst, send_sem=i_s.at[8 + k if kind == 0 else 2 * kind + k], recv_sem=v_rs.at[k, kind],
            device_id=dev(plane, to, side), device_id_type=MESH,
        )

    def avg_goes(kind):
        if kind == 0:
            return tile > 0
        if kind == 1:
            return jnp.logical_and(cm == per - 1, ct + 1 < nested)
        return jnp.logical_and(cm == 0, ct > 0)

    ways = v_rs.shape[1]

    def avg_send(k):
        for kind in range(ways):
            pl.when(avg_goes(kind))(lambda kind=kind: avg_copy(k, kind).start())

    def avg_wait(k):
        def wait(kind, dst):
            pltpu.make_async_remote_copy(
                src_ref=dst, dst_ref=dst, send_sem=i_s.at[8], recv_sem=v_rs.at[k, kind],
                device_id=dev(plane, tile, side), device_id_type=MESH,
            ).wait_recv()

        pl.when(tile == 0)(lambda: wait(0, avgr.at[k, LEAD + brows : LEAD + per * brows, :]))
        pl.when(tile > 0)(lambda: wait(0, avgr.at[k, LEAD : LEAD + per * brows, :]))
        if ways == 1:
            return
        pl.when(tile > 0)(lambda: wait(1, avgr.at[k, 8:16, :]))
        pl.when(tile < nested - 1)(lambda: wait(2, avgr.at[k, LEAD + crows : LEAD + crows + 8, :]))

    def edge_copy():
        return pltpu.make_async_remote_copy(
            src_ref=edges, dst_ref=edger, send_sem=i_s.at[10], recv_sem=v_rs.at[2, 0],
            device_id=dev(plane, nested, side), device_id_type=MESH,
        )

    ends = nested < tiles
    is_last = tile == tiles - 1

    def push(s_ref, g_c, g_r, k_c, k_r, which):
        for b in which:
            here, up = s_ref[b : b + 8, :], s_ref[b - 1 : b + 7, :]
            g_c[b : b + 8, :] -= k_c[b : b + 8, :] * (here - pltpu.roll(here, 1, 1))
            g_r[b : b + 8, :] -= k_r[b : b + 8, :] * (here - up)

    def spread(g_c, g_r, b):
        east = g_c[b : b + 8, :]
        return (pltpu.roll(east, east.shape[1] - 1, 1) - east) + (
            g_r[b + 1 : b + 9, :] - g_r[b : b + 8, :]
        )

    def means(x):
        high, low = split2(x)
        return jnp.dot(high.astype(BF16), amat[...], preferred_element_type=F32) + jnp.dot(
            low.astype(BF16), amat[...], preferred_element_type=F32
        )

    def block_means(k, sums):
        for j in range(cw // 128):
            work[j] = sums[:, j * 128 : (j + 1) * 128]
            avgs[k, :, j * 128 : (j + 1) * 128] = sum(
                work[j, pl.ds(i, brows, stride=RATIO), :] for i in range(RATIO)
            )
        avg_send(k)

        @pl.when(tile == 0)
        def _():
            avgr[k, LEAD : LEAD + brows, :] = avgs[k]

    lane = iota((1, fw), 1)
    odd, upper = lane % 2 == 1, lane % 4 >= 2

    def lane_means(x):
        x = x + jnp.where(odd, pltpu.roll(x, 1, 1), pltpu.roll(x, fw - 1, 1))
        x = x + jnp.where(upper, pltpu.roll(x, 2, 1), pltpu.roll(x, fw - 2, 1))
        return x * (1.0 / (RATIO * RATIO))

    erow = iota((16, fw), 0)

    def step(k, carry, keep=False):
        c0, g0, h1 = carry

        lev[LEAD - 1 : LEAD, :] = jnp.where(tile == 0, c0, lev[LEAD - 1 : LEAD, :])
        if ends:
            esum[k] = lev[top - 8 : top, :]
        mean = lane_means(jnp.sum(lev[LEAD : LEAD + RATIO, :], axis=0, keepdims=True))
        g0 = g0 - kc0 * (c0 - pltpu.roll(c0, RATIO, 1))
        h1 = h1 - kr1 * (mean - c0)
        c0 = c0 - ((pltpu.roll(g0, fw - RATIO, 1) - g0) + h1)
        push(lev, gc, gr, kc, kr, strips)
        for b in strips:
            new = lev[b : b + 8, :] - spread(gc, gr, b)
            lev[b : b + 8, :] = new
            if LEAD <= b < top:
                r = slice(b - LEAD, b - LEAD + 8)
                peak_o[r, :] = jnp.maximum(peak_o[r, :], new[:, 0:cols])
                if keep:
                    total[r, :] += new
        return c0, g0, h1

    zero = jnp.zeros((1, fw), F32)
    carry = lax.fori_loop(
        0, STEPS - 2, functools.partial(step, keep=True), (join3(wide, 0), zero, zero)
    )
    sums = means(total[...])
    carry = step(STEPS - 2, carry)
    block_means(0, sums)
    block_means(1, means(lev[LEAD:top, :]))
    carry = step(STEPS - 1, carry)
    if ends:
        @pl.when(is_last)
        def _():
            sums = jnp.zeros(erow.shape, F32)
            for k in range(STEPS):
                above = jnp.sum(esum[k, 0:4, :], axis=0, keepdims=True)
                below = jnp.sum(esum[k, 4:8, :], axis=0, keepdims=True)
                sums = jnp.where(erow == 2 * k, above, jnp.where(erow == 2 * k + 1, below, sums))
            edges[...] = means(sums)
            edge_copy().start()
    surf_o[...] = lev[LEAD:top, 0:cols]

    @pl.when(tile >= nested)
    def _():
        if ends:
            pl.when(tile == nested)(lambda: edge_copy().wait_recv())
        erows = iota((16, cw), 0)
        crow = iota((8, cw), 0)

        def cstep(k, carry):
            def edge(i):
                return jnp.sum(jnp.where(erows == 2 * k + i, edger[...], 0.0), axis=0, keepdims=True)

            @pl.when(tile == nested)
            def _():
                clev[LEAD - 8 : LEAD, :] = jnp.where(crow == 7, edge(0), clev[LEAD - 8 : LEAD, :])
                clev[LEAD : LEAD + 8, :] = jnp.where(crow == 0, edge(1), clev[LEAD : LEAD + 8, :])

            push(clev, cgc, cgr, ckc, ckr, cstrips)
            for b in cstrips:
                clev[b : b + 8, :] -= spread(cgc, cgr, b)
            return carry

        lax.fori_loop(0, STEPS, cstep, 0)
        coarse_o[...] = clev[LEAD : LEAD + crows, 0:ccols]

    @pl.when(tile < nested)
    def _():
        c0, g0, h1 = carry
        narrow = RATIO * jnp.dot(stack3([c0, h1]), amat[...], preferred_element_type=F32)
        avg_wait(0)
        avg_wait(1)
        for b in range(LEAD, LEAD + crows + 8, 8):
            clev[b : b + 8, :] = avgr[0, b - 1 : b + 7, :] + avgr[1, b - 1 : b + 7, :]
        clev[LEAD - 1 : LEAD, :] = avgr[0, LEAD - 2 : LEAD - 1, :] + avgr[1, LEAD - 2 : LEAD - 1, :]
        inner = range(LEAD, LEAD + crows + 8, 8)
        push(clev, cgc, cgr, ckc, ckr, inner)

        @pl.when(tile == 0)
        def _():
            cgr[LEAD + 1 : LEAD + 2, :] = join3(narrow, 1)

        for b in range(LEAD, LEAD + crows, 8):
            new = avgr[1, b - 1 : b + 7, :] - spread(cgc, cgr, b)
            coarse_o[b - LEAD : b - LEAD + 8, :] = new[:, 0:ccols]

        @pl.when(tile == 0)
        def _():
            coarse_o[0:1, :] = join3(narrow, 0)[:, 0:ccols]

    slip_copy.wait_send()
    rest = pl.ds(0, owners - 1)
    for h in range(2):
        pair_copy(send.at[h, rest], recv.at[h, rest], a_ss.at[h], a_rs.at[h, 0], me).wait_send()
    pair_copy(mrecv.at[rest], mrecv.at[rest], m_ss.at[0], m_rs.at[0], me).wait_send()
    landed(hcore, 5, 8).wait_send()
    for kind, v, dst, n in [(1, 0, hvert.at[0], 0), (1, 1, hvert.at[1], 1), (0, 0, hside, 2)] + [
        (2, v, hcorn.at[v], 3 + v) for v in range(2)
    ]:
        pl.when(goes(kind, v, 1))(lambda dst=dst, n=n: landed(dst, n, 8).wait_send())
    for k in range(2):
        for kind in range(ways):
            pl.when(avg_goes(kind))(lambda k=k, kind=kind: avg_copy(k, kind).wait_send())
    if ends:
        pl.when(is_last)(lambda: edge_copy().wait_send())


def store(peak, surf, coarse, peak_h, surf_h, coarse_h, sems):
    pairs = [(peak, peak_h), (surf, surf_h), (coarse, coarse_h)]
    copies = [pltpu.make_async_copy(src, dst, sems.at[i]) for i, (src, dst) in enumerate(pairs)]
    for copy in copies:
        copy.start()
    for copy in copies:
        copy.wait()


def shards(dims, green, row_owner, row_index, row_fault, slip, depth, wet, coarse_depth, coarse_start):
    planes, tiles, cols_n, subs_n = dims
    owners = tiles * cols_n * subs_n
    entries, cols = green.shape
    rows = depth.shape[0]
    crows, ccols = coarse_depth.shape
    capacity = max(2, (2 * entries + owners - 1) // owners)
    capp = (capacity + 15) // 16 * 16
    packs = owners // (128 // capp)
    hw = cols // planes
    i32 = lambda *shape: pltpu.VMEM(shape, jnp.int32)
    ways = 3 if tiles * (rows // RATIO) // crows > 1 else 1
    fw, cw = cols + 128, ccols + 128
    high, chigh = rows + 32, crows + 32
    vmem = lambda *shape: pltpu.VMEM(shape, F32)
    dma = pltpu.SemaphoreType.DMA
    keep = lambda x: pltpu.with_memory_space_constraint(x, pltpu.HBM)
    results = pl.pallas_call(
        functools.partial(kernel, dims),
        out_shape=(
            jax.ShapeDtypeStruct((rows, cols), F32),
            jax.ShapeDtypeStruct((rows, cols), F32),
            jax.ShapeDtypeStruct((crows, ccols), F32),
        ),
        in_specs=[pl.BlockSpec(memory_space=pltpu.HBM)] * 9,
        out_specs=(pl.BlockSpec(memory_space=pltpu.VMEM),) * 3,
        scratch_shapes=[
            pltpu.VMEM((entries, hw), BF16), i32(1, entries), i32(1, entries), i32(1, entries),
            vmem(1, slip.shape[0]), vmem(rows, cols), i32(rows, cols),
            pltpu.VMEM((owners * capp, entries), BF16), vmem(owners, entries),
            pltpu.VMEM((2, owners, capp, 128), BF16),
            pltpu.VMEM((2, owners, capp, 128), BF16),
            vmem(owners, 1, 128), vmem(owners, 1, 128),
            vmem(8, 128), vmem(8, 128), vmem(4 * rows, 128),
            pltpu.VMEM((packs, 4 * rows, 128), BF16),
            vmem(rows + 8, cols + 512), vmem(2, rows + 8, 384), vmem(2, 8, cols + 256),
            vmem(2, 2, 8, 384),
            vmem(2, 2 * rows, 128), vmem(2, rows, 128), vmem(2, rows, 128), vmem(2, 2, 2, 8, 128),
            vmem(2, 2, 8, 128),
        ]
        + [vmem(high, fw)] * 6
        + [vmem(chigh, cw)] * 6
        + [
            pltpu.VMEM((fw, cw), BF16), pltpu.VMEM((cw, fw), BF16),
            vmem(cw // 128, rows, 128),
            vmem(rows, fw), vmem(2, rows // RATIO, cw), vmem(2, chigh, cw),
            vmem(STEPS, 8, fw), vmem(16, cw), vmem(16, cw),
            dma((12,)), dma((2,)), dma((2, packs)), dma((1,)), dma((packs,)), dma((2,)), dma((8,)), dma((6,)),
            dma((9,)), dma((3, ways)), pltpu.SemaphoreType.REGULAR((tiles + 1,)),
        ],
        compiler_params=pltpu.CompilerParams(
            collective_id=0, has_side_effects=True, vmem_limit_bytes=48 * 1024 * 1024
        ),
    )(
        keep(green), keep(row_owner.reshape(1, entries)), keep(row_index.reshape(1, entries)),
        keep(row_fault.reshape(1, entries)), keep(slip.reshape(1, -1)), keep(depth), keep(wet), keep(coarse_depth), keep(coarse_start),
    )
    return pl.pallas_call(
        store,
        out_shape=tuple(jax.ShapeDtypeStruct(x.shape, F32) for x in results),
        in_specs=[pl.BlockSpec(memory_space=pltpu.VMEM)] * 3,
        out_specs=(pl.BlockSpec(memory_space=pltpu.HBM),) * 3,
        scratch_shapes=[dma((3,))],
        compiler_params=pltpu.CompilerParams(vmem_limit_bytes=1024 * 1024),
    )(*results)


def solution(mesh):
    dims = tuple(mesh.shape[a] for a in ("scen", "tile", "col", "sub"))
    return jax.shard_map(
        functools.partial(shards, dims),
        mesh=mesh,
        in_specs=(
            P(("tile", "col", "sub"), None),
            P(("tile", "col", "sub"), None),
            P(("tile", "col", "sub")),
            P(("tile", "col", "sub")),
            P(("scen", "tile", "col", "sub")),
            P("tile", ("col", "sub")),
            P("tile", ("col", "sub")),
            P("tile", ("col", "sub")),
            P(("scen", "tile"), ("col", "sub")),
        ),
        out_specs=(
            P(("scen", "tile"), ("col", "sub")),
            P(("scen", "tile"), ("col", "sub")),
            P(("scen", "tile"), ("col", "sub")),
        ),
        check_vma=False,
    )
```

```python
import functools
import jax
import jax.numpy as jnp
from jax import lax
from jax.experimental import pallas as pl
from jax.experimental.pallas import tpu as pltpu
from jax.sharding import PartitionSpec as P

RATIO = 4
STEPS = 6
HALO = 8
LEAD = 16
F32 = jnp.float32
BF16 = jnp.bfloat16
MESH = pl.DeviceIdType.MESH


def split2(x):
    high = x.astype(BF16).astype(F32)
    return high, (x - high).astype(BF16).astype(F32)


def iota(shape, dim):
    return lax.broadcasted_iota(jnp.int32, shape, dim)


def kernel(
    dims,
    green_h, owner_h, index_h, fault_h, slip_h, depth_h, wet_h, cdep_h, cstart_h,
    peak_o, surf_o, coarse_o,
    green, owner, index, fault, slip, depth, wet, chosen_r,
    place, send, recv, msend, mrecv, slip_s, slip_r, acc, weights,
    zs, zside, zvert, zcorn,
    half, hcore, packed, hside, hvert, hcorn,
    lev, held, gc, gr, kc, kr,
    clev, cheld, cgc, cgr, ckc, ckr,
    amat, rmat, work, total, avgs, avgr, esum, edges, edger,
    i_s, a_ss, a_rs, m_ss, m_rs, sl_s, z_rs, h_ss, h_rs, v_rs, alive,
):
    planes, tiles, cols_n, subs_n = dims
    sides = cols_n * subs_n
    owners = tiles * sides
    plane = lax.axis_index("scen")
    tile = lax.axis_index("tile")
    side = lax.axis_index("col") * subs_n + lax.axis_index("sub")
    me = tile * sides + side
    rows, cols = depth.shape
    crows, ccols = cdep_h.shape
    entries, hw = green.shape
    capp = send.shape[2]
    pack = 128 // capp
    packs = owners // pack
    fw = cols + 128
    cw = ccols + 128
    top = LEAD + rows

    def dev(p, t, c):
        return {"scen": p, "tile": t, "col": c // subs_n, "sub": c % subs_n}

    def fetch(i):
        edge_lanes = pl.ds(pl.multiple_of(plane * (hw + 128), 128), 128)
        inner_lanes = pl.ds(pl.multiple_of(128 + plane * 128, 128), 128)
        far = 256 + cols
        src, dst = [
            (owner_h, owner), (green_h.at[:, edge_lanes], green.at[:, 0:128]), (index_h, index), (fault_h, fault),
            (slip_h, slip), (depth_h, depth), (wet_h, wet),
            (cdep_h, zs.at[0:rows, 0:ccols]), (cstart_h, zs.at[0:rows, 128 : 128 + ccols]),
            (cdep_h, zs.at[0:rows, far : far + ccols]),
            (cstart_h, zs.at[0:rows, far + 128 : far + 128 + ccols]),
            (green_h.at[:, inner_lanes], green.at[:, 128:256]),
        ][i]
        return pltpu.make_async_copy(src, dst, i_s.at[i])

    barrier = pltpu.get_barrier_semaphore()

    other = planes - 1 - plane

    def hail(sem):
        def start(i, carry):
            pl.semaphore_signal(
                sem, inc=1, device_id=dev(plane, i // sides, lax.rem(i, sides)), device_id_type=MESH
            )
            return carry

        return start

    def hail_other(sem):
        pl.semaphore_signal(sem, inc=1, device_id=dev(other, tile, side), device_id_type=MESH)

    lax.fori_loop(me + 1, owners, hail(barrier), 0)
    pl.when(plane == 0)(lambda: hail_other(barrier))
    for i in (4, 0, 1, 11, 2, 3, 5, 6, 7, 8, 9, 10):
        fetch(i).start()

    slip_copy = pltpu.make_async_remote_copy(
        src_ref=slip_s, dst_ref=slip_r, send_sem=sl_s.at[0], recv_sem=sl_s.at[1],
        device_id=dev(other, tile, side), device_id_type=MESH,
    )
    fetch(4).wait()
    slip_s[...] = jnp.zeros_like(slip_s)
    slip_s[0:1, 0 : slip.shape[1]] = slip[...]
    pl.when(me + plane > 0)(lambda: pl.semaphore_wait(barrier, me + plane))

    @pl.when(plane > 0)
    def _():
        hail_other(alive.at[tiles])
        slip_copy.start()

    lax.fori_loop(0, me, hail(alive.at[tile]), 0)

    fetch(0).wait()
    dest = owner[...]
    hit = iota((owners, entries), 0) == dest
    before = (iota((entries, entries), 0) < iota((entries, entries), 1)).astype(F32).astype(BF16)
    rank = jnp.dot(hit.astype(F32).astype(BF16), before, preferred_element_type=F32)
    place[...] = jnp.where(hit, rank, -1.0)
    group = min(owners, 512 // capp)
    groups = owners // group
    fetch(1).wait()
    fetch(11).wait()
    gh = green[...]
    slots = iota((group, capp, entries), 1).astype(F32)

    def select(g):
        rows_of = place[pl.ds(pl.multiple_of(g * group, group), group), :]
        chosen = jnp.where(rows_of[:, None, :] == slots, 1.0, 0.0)
        chosen = chosen.reshape(group * capp, entries).astype(BF16)
        chosen_r[pl.ds(g * group * capp, group * capp), :] = chosen
        return chosen

    def fill(g, carry):
        picked = jnp.dot(select(g), gh, preferred_element_type=F32).astype(BF16)
        for h in range(2):
            send[h, pl.ds(g * group, group)] = picked[:, h * 128 : (h + 1) * 128].reshape(group, capp, 128)
        return carry

    fill(0, 0) if groups == 1 else lax.fori_loop(0, groups, fill, 0)

    for i in (2, 3, 5, 6, 7, 8, 9, 10):
        fetch(i).wait()
    raw = depth[...]
    zs[0:rows, 256 : 256 + cols] = jnp.where(wet[...] > 0, raw, 0.0)
    zs[rows : rows + 8, 256 : 256 + cols] = jnp.broadcast_to(raw[0:1], (8, cols))
    for off in (0, 256 + cols):
        zs[rows : rows + 8, off : off + 256] = jnp.zeros((8, 256), F32)

    def pair_copy(src, dst, s_sem, r_sem, d):
        return pltpu.make_async_remote_copy(
            src_ref=src, dst_ref=dst, send_sem=s_sem, recv_sem=r_sem,
            device_id=dev(plane, d // sides, lax.rem(d, sides)), device_id_type=MESH,
        )

    def a2a(h, d):
        return pair_copy(send.at[h, d], recv.at[h, me], a_ss.at[h], a_rs.at[h, me // pack], d)

    def a2a_meta(d):
        return pair_copy(msend.at[d], mrecv.at[me], m_ss.at[0], m_rs.at[me // pack], d)

    def a2a_wait(h, g, n):
        got = recv.at[h, pl.ds(g * pack, n)]
        pair_copy(got, got, a_ss.at[h], a_rs.at[h, g], me).wait_recv()

    def meta_wait(g, n):
        got = mrecv.at[pl.ds(g * pack, n)]
        pair_copy(got, got, m_ss.at[0], m_rs.at[g], me).wait_recv()

    middle = tiles // 2
    low = tile < middle

    def launch_tile(t, start):
        first = t * sides

        def own(i, carry):
            start(first + lax.rem(side + i, sides)).start()
            return carry

        lax.fori_loop(jnp.where(t == tile, 1, 0), sides, own, 0)

    def launch_across(start):
        lax.fori_loop(
            0, tiles, lambda i, c: (launch_tile(jnp.where(low, tiles - 1 - i, i), start), c)[1], 0
        )

    def launch_one(d, carry):
        a2a(0, d).start()
        return carry

    def launch_met(t, carry):
        pl.semaphore_wait(alive.at[t], sides)
        launch_tile(t, functools.partial(a2a, 0))
        return carry

    lax.fori_loop(0, me, launch_one, 0)
    @pl.when(plane == 0)
    def _():
        pl.semaphore_wait(alive.at[tiles], 1)
        slip_copy.start()

    pl.when(side < sides - 1)(lambda: pl.semaphore_wait(alive.at[tile], sides - 1 - side))
    lax.fori_loop(me + 1, (tile + 1) * sides, launch_one, 0)
    lax.fori_loop(tile + 1, tiles, launch_met, 0)

    moves = [(0, -1), (0, 1), (-1, 0), (1, 0), (-1, -1), (-1, 1), (1, -1), (1, 1)]

    def static_copy(i):
        dy, dx = moves[i]
        lanes = (
            slice(0, 512 - 128) if dx == -1
            else slice(cols + 128, cols + 512) if dx == 1 else slice(0, 256 + cols)
        )
        sel = slice(0, rows + 8) if dy == 0 else slice(0, 8) if dy == -1 else slice(rows - 8, rows)
        bi = 0 if dy == -1 else 1
        bj = 0 if dx == -1 else 1
        dst = zside.at[bj] if dy == 0 else zvert.at[bi] if dx == 0 else zcorn.at[bi, bj]
        return pltpu.make_async_remote_copy(
            src_ref=zs.at[sel, lanes], dst_ref=dst, send_sem=i_s.at[i], recv_sem=z_rs.at[i],
            device_id=dev(plane, tile + dy, side + dx), device_id_type=MESH,
        )

    def inside(dy, dx):
        ok = True
        for at, by, size in ((tile, dy, tiles), (side, dx, sides)):
            if by == -1:
                ok = jnp.logical_and(ok, at > 0)
            if by == 1:
                ok = jnp.logical_and(ok, at < size - 1)
        return ok

    slip_copy.wait_recv()

    mrow = iota((8, slip.shape[1]), 0)
    own_h, own_l = split2(slip[...])
    oth_h, oth_l = split2(slip_r[0:1, 0 : slip.shape[1]])
    parts = jnp.where(mrow == 1, own_h, 0.0)
    for i, part in ((2, own_l), (3, oth_h), (4, oth_l)):
        parts = jnp.where(mrow == i, part, parts)
    picks = (iota((slip.shape[1], entries), 0) == fault[...]).astype(F32).astype(BF16)
    meta = jnp.dot(parts.astype(BF16), picks, preferred_element_type=F32)
    meta = jnp.where(iota((8, entries), 0) == 0, index[...].astype(F32), meta).astype(BF16)

    lane_of = iota((1, 128), 1)
    within = [(lane_of >= i * capp) & (lane_of < (i + 1) * capp) for i in range(pack)]

    def shifted(x, by):
        by = by % pack
        return pltpu.roll(x, by * capp, 1) if by else x

    def describe(g, carry):
        told = lax.dot_general(
            meta, chosen_r[pl.ds(g * group * capp, group * capp), :], (((1,), (1,)), ((), ())), preferred_element_type=F32
        )
        quantities = [told[0:1], told[1:2] + told[2:3], told[3:4] + told[4:5]]
        for i in range(group // pack):
            parts_of = [q[:, i * 128 : (i + 1) * 128] for q in quantities]
            for j in range(pack):
                record = jnp.zeros((1, 128), F32)
                for q, part in enumerate(parts_of):
                    record = jnp.where(within[q], shifted(part, q - j), record)
                msend[g * group + i * pack + j] = record
        return carry

    describe(0, 0) if groups == 1 else lax.fori_loop(0, groups, describe, 0)

    launch_across(a2a_meta)
    launch_across(functools.partial(a2a, 1))

    fl = iota((fw, cw), 0)
    fmap = jnp.where(fl < cols + 64, fl // RATIO, fl // RATIO + (cw - fw // RATIO))
    amat[...] = jnp.where(fmap == iota((fw, cw), 1), 1.0 / (RATIO * RATIO), 0.0).astype(BF16)
    rl = iota((cw, fw), 1)
    rmap = jnp.where(rl < cols + 64, rl // RATIO, rl // RATIO + (cw - fw // RATIO))
    rmat[...] = jnp.where(rmap == iota((cw, fw), 0), 1.0, 0.0).astype(BF16)
    for ref in (lev, held, gc, gr, clev, cheld, cgc, cgr):
        ref[...] = jnp.zeros_like(ref)

    for bj in range(2):
        dx = 1 if bj == 0 else -1
        @pl.when(jnp.logical_not(inside(0, dx)))
        def _(bj=bj):
            zside[bj] = jnp.zeros(zside.shape[1:], F32)
        for bi in range(2):
            dy = 1 if bi == 0 else -1
            @pl.when(jnp.logical_not(inside(dy, dx)))
            def _(bi=bi, bj=bj):
                zcorn[bi, bj] = jnp.zeros(zcorn.shape[2:], F32)
    for bi in range(2):
        dy = 1 if bi == 0 else -1
        @pl.when(jnp.logical_not(inside(dy, 0)))
        def _(bi=bi):
            zvert[bi] = jnp.zeros(zvert.shape[1:], F32)
    wrow = iota((4 * rows, 128), 0)
    in_tile = lax.rem(wrow, rows).astype(F32)
    recv[0, me] = send[0, me]
    recv[1, me] = send[1, me]
    mrecv[me] = msend[me]

    def product(h, g, weight):
        block = recv[h, pl.ds(g * pack, pack)].reshape(128, 128)
        return jnp.dot(weight, block, preferred_element_type=F32)

    def put(g):
        told = [jnp.zeros((1, 128), F32)] * 3
        for j in range(pack):
            record = mrecv[g * pack + j]
            told = [jnp.where(within[j], shifted(record, j - q), t) for q, t in enumerate(told)]
        (own_h, own_l), (oth_h, oth_l) = split2(told[1]), split2(told[2])
        weight = jnp.where(
            wrow < rows, own_h,
            jnp.where(wrow < 2 * rows, oth_h, jnp.where(wrow < 3 * rows, own_l, oth_l)),
        )
        weight = jnp.where(in_tile == told[0], weight, 0.0).astype(BF16)
        weights[g] = weight
        return product(0, g, weight)

    mine = me // pack

    def take(i, carry):
        g = lax.rem(mine + i, packs)
        a2a_wait(0, g, pack)
        meta_wait(g, pack)
        acc[...] += put(g)
        return carry

    def fold():
        return acc[0 : 2 * rows, :] + acc[2 * rows : 4 * rows, :]

    a2a_wait(0, mine, pack - 1)
    meta_wait(mine, pack - 1)
    acc[...] = put(mine)
    lax.fori_loop(1, packs - 1, take, 0, unroll=packs == 4)
    for i, (dy, dx) in enumerate(moves):
        pl.when(inside(dy, dx))(lambda i=i: static_copy(i).start())

    take(packs - 1, 0)
    half[0] = fold()

    toward = 2 * plane - 1

    def core_copy(h):
        return pltpu.make_async_remote_copy(
            src_ref=half.at[h, rows : 2 * rows, :], dst_ref=hcore.at[h], send_sem=h_ss.at[5],
            recv_sem=h_rs.at[8], device_id=dev(other, tile, side), device_id_type=MESH,
        )

    def halo_copy(h, s, kind, v, q):
        to_plane = plane if s == 0 else other
        dy = 0 if kind == 0 else (-1 if v == 0 else 1)
        r0 = s * rows + (0 if v == 0 else rows - 8)
        if kind == 0:
            src, dst, n, m = packed.at[s], hside.at[q], 2, 2 + q
        elif kind == 1:
            src, dst, n, m = half.at[h, r0 : r0 + 8, :], hvert.at[v, q, h], v, v
        else:
            src, dst, n, m = half.at[h, r0 : r0 + 8, :], hcorn.at[v, q], 3 + v, 4 + 2 * v + q
        return pltpu.make_async_remote_copy(
            src_ref=src, dst_ref=dst, send_sem=h_ss.at[n], recv_sem=h_rs.at[m],
            device_id=dev(to_plane, tile + dy, side if kind == 1 else side + toward),
            device_id_type=MESH,
        )

    kinds = [(0, 1, 0), (0, 1, 1), (0, 0, 0), (0, 2, 0), (0, 2, 1), (1, 1, 0), (1, 1, 1)]

    def goes(kind, v, sign):
        dy = 0 if kind == 0 else (-1 if v == 0 else 1) * sign
        ok = inside(dy, 0)
        if kind != 1:
            to = side + toward
            ok = jnp.logical_and(ok, jnp.logical_and(to >= 0, to < sides))
        return ok

    quarter = rows // 4
    qlane = iota((quarter, 128), 1)

    def turn_lanes(x, by):
        by = by % 128
        return pltpu.roll(x, by, 1) if by else x

    def send_half(half_of):
        core_copy(half_of).start()
        if half_of == 0:
            for s in range(2):
                strip = jnp.zeros((quarter, 128), F32)
                for j in range(4):
                    r0 = s * rows + j * quarter
                    x = half[0, r0 : r0 + quarter, :]
                    moved = jnp.where(plane == 0, turn_lanes(x, 32 * j), turn_lanes(x, 32 * j + 32))
                    strip = jnp.where(qlane // 32 == j, moved, strip)
                packed[s] = strip
        for s in (1, 0):
            for h, kind, v in kinds:
                if h == half_of:
                    pl.when(goes(kind, v, 1))(
                        lambda s=s, h=h, kind=kind, v=v: halo_copy(h, s, kind, v, plane).start()
                    )

    send_half(0)

    def take_inner(i, carry):
        g = lax.rem(mine + i, packs)
        a2a_wait(1, g, pack)
        acc[...] += product(1, g, weights[g])
        return carry

    a2a_wait(1, mine, pack - 1)
    acc[...] = product(1, mine, weights[mine])
    lax.fori_loop(1, packs, take_inner, 0, unroll=packs == 4)
    half[1] = fold()
    send_half(1)

    def comes(kind, v, q):
        dy = 0 if kind == 0 else (1 if v == 0 else -1)
        dx = 0 if kind == 1 else (1 if q == 0 else -1)
        return inside(dy, dx)

    for i, (dy, dx) in enumerate(moves):
        pl.when(inside(-dy, -dx))(lambda i=i: static_copy(i).wait_recv())

    def merge(right, left):
        return jnp.where(iota(right.shape, right.ndim - 1) < 64, right, left)

    def place_static(r0, n, z, zr, zl, sr):
        held[r0 : r0 + n, 0:cols] = z[sr, 256 : 256 + cols]
        held[r0 : r0 + n, cols:fw] = merge(zr[sr, 256:384], zl[sr, 0:128])
        cheld[r0 : r0 + n, 0:ccols] = z[sr, 0:128]
        cheld[r0 : r0 + n, ccols:cw] = merge(zr[sr, 0:128], zl[sr, 128:256])
        clev[r0 : r0 + n, 0:ccols] = z[sr, 128:256]
        clev[r0 : r0 + n, ccols:cw] = merge(zr[sr, 128:256], zl[sr, 256:384])

    place_static(LEAD, rows, zs, zside.at[0], zside.at[1], slice(0, rows))
    place_static(top, 8, zvert.at[0], zcorn.at[0, 0], zcorn.at[0, 1], slice(0, 8))
    place_static(8, 8, zvert.at[1], zcorn.at[1, 0], zcorn.at[1, 1], slice(0, 8))

    @pl.when(tile == 0)
    def _():
        held[LEAD - 1 : LEAD, 0:cols] = depth[0:1, :]
        held[LEAD - 1 : LEAD, cols:fw] = merge(
            zside[0, rows : rows + 1, 256:384], zside[1, rows : rows + 1, 0:128]
        )

    strips = [8 + 8 * i for i in range((rows + 16) // 8)]
    cstrips = [8 + 8 * i for i in range((crows + 16) // 8)]

    def faces(h, k_c, k_r, scale, which):
        width = h.shape[1]
        for b in which:
            here, up = h[b : b + 8, :], h[b - 1 : b + 7, :]
            west = pltpu.roll(here, 1, 1)
            k_c[b : b + 8, :] = jnp.where((here > 0.0) & (west > 0.0), scale * (here + west), 0.0)
            k_r[b : b + 8, :] = jnp.where((here > 0.0) & (up > 0.0), scale * (here + up), 0.0)

    faces(held, kc, kr, 0.5 * 0.5 * 0.5, strips)
    faces(cheld, ckc, ckr, 0.5 * 0.125 * 0.125, cstrips)

    def stack3(values):
        rows_of = iota((16, values[0].shape[1]), 0)
        out = jnp.zeros(rows_of.shape, F32)
        for i, v in enumerate(values):
            first, rest = split2(v)
            second, third = split2(v - first)
            for j, part in enumerate((first, second, third)):
                out = jnp.where(rows_of == 3 * i + j, part, out)
        return out.astype(BF16)

    def join3(wide, i):
        return wide[3 * i : 3 * i + 1] + wide[3 * i + 1 : 3 * i + 2] + wide[3 * i + 2 : 3 * i + 3]

    wide = jnp.dot(
        stack3([clev[LEAD : LEAD + 1, :], ckc[LEAD : LEAD + 1, :], ckr[LEAD + 1 : LEAD + 2, :]]),
        rmat[...], preferred_element_type=F32,
    )
    kc0, kr1 = join3(wide, 1), join3(wide, 2)
    def landed(dst, n, m):
        return pltpu.make_async_remote_copy(
            src_ref=dst, dst_ref=dst, send_sem=h_ss.at[n], recv_sem=h_rs.at[m],
            device_id=dev(other, tile, side), device_id_type=MESH,
        )

    arrivals = [(1, v, 0, hvert.at[v], v) for v in range(2)]
    for q in range(2):
        arrivals.append((0, 0, q, hside.at[q], 2 + q))
        arrivals += [(2, v, q, hcorn.at[v, q], 4 + 2 * v + q) for v in range(2)]
    for kind, v, q, dst, m in arrivals:
        @pl.when(jnp.logical_not(comes(kind, v, q)))
        def _(dst=dst):
            dst[...] = jnp.zeros(dst.shape, F32)
        pl.when(comes(kind, v, q))(lambda dst=dst, m=m: landed(dst, 5, m).wait_recv())
    landed(hcore, 5, 8).wait_recv()

    for i, (dy, dx) in enumerate(moves):
        pl.when(inside(dy, dx))(lambda i=i: static_copy(i).wait_send())

    def lanes_of(p, h):
        return p * (hw + 128) if h == 0 else 128 + p * 128

    for h in range(2):
        lev[LEAD:top, pl.ds(pl.multiple_of(lanes_of(plane, h), 128), 128)] = half[h, 0:rows, :]
        lev[LEAD:top, pl.ds(pl.multiple_of(lanes_of(other, h), 128), 128)] = hcore[h]
    for j in range(4):
        right, left = turn_lanes(hside[0], -32 * j), turn_lanes(hside[1], 96 - 32 * j)
        lev[LEAD + j * quarter : LEAD + (j + 1) * quarter, cols:fw] = jnp.where(
            qlane < 32, right, jnp.where(qlane >= 96, left, 0.0)
        )
    for v, r0 in ((0, top), (1, 8)):
        for q in range(2):
            for h in range(2):
                lev[r0 : r0 + 8, lanes_of(q, h) : lanes_of(q, h) + 128] = hvert[v, q, h]
        lev[r0 : r0 + 8, cols:fw] = merge(hcorn[v, 0], hcorn[v, 1])
    peak_o[...] = lev[LEAD:top, 0:cols]
    total[...] = lev[LEAD:top, :]

    brows = rows // RATIO
    per = crows * RATIO // rows
    nest = brows * tiles
    nested = nest // crows
    ct = tile // per
    cm = lax.rem(tile, per)

    def avg_copy(k, kind):
        if kind == 0:
            src, to = avgs.at[k], ct
            dst = avgr.at[k, pl.ds(pl.multiple_of(LEAD + cm * brows, 8), brows), :]
        elif kind == 1:
            src, to = avgs.at[k, brows - 8 : brows, :], ct + 1
            dst = avgr.at[k, 8:16, :]
        else:
            src, to = avgs.at[k, 0:8, :], ct - 1
            dst = avgr.at[k, LEAD + crows : LEAD + crows + 8, :]
        return pltpu.make_async_remote_copy(
            src_ref=src, dst_ref=dst, send_sem=i_s.at[8 + k if kind == 0 else 2 * kind + k], recv_sem=v_rs.at[k, kind],
            device_id=dev(plane, to, side), device_id_type=MESH,
        )

    def avg_goes(kind):
        if kind == 0:
            return tile > 0
        if kind == 1:
            return jnp.logical_and(cm == per - 1, ct + 1 < nested)
        return jnp.logical_and(cm == 0, ct > 0)

    ways = v_rs.shape[1]

    def avg_send(k):
        for kind in range(ways):
            pl.when(avg_goes(kind))(lambda kind=kind: avg_copy(k, kind).start())

    def avg_wait(k):
        def wait(kind, dst):
            pltpu.make_async_remote_copy(
                src_ref=dst, dst_ref=dst, send_sem=i_s.at[8], recv_sem=v_rs.at[k, kind],
                device_id=dev(plane, tile, side), device_id_type=MESH,
            ).wait_recv()

        pl.when(tile == 0)(lambda: wait(0, avgr.at[k, LEAD + brows : LEAD + per * brows, :]))
        pl.when(tile > 0)(lambda: wait(0, avgr.at[k, LEAD : LEAD + per * brows, :]))
        if ways == 1:
            return
        pl.when(tile > 0)(lambda: wait(1, avgr.at[k, 8:16, :]))
        pl.when(tile < nested - 1)(lambda: wait(2, avgr.at[k, LEAD + crows : LEAD + crows + 8, :]))

    def edge_copy():
        return pltpu.make_async_remote_copy(
            src_ref=edges, dst_ref=edger, send_sem=i_s.at[10], recv_sem=v_rs.at[2, 0],
            device_id=dev(plane, nested, side), device_id_type=MESH,
        )

    ends = nested < tiles
    is_last = tile == tiles - 1

    def push(s_ref, g_c, g_r, k_c, k_r, which):
        for b in which:
            here, up = s_ref[b : b + 8, :], s_ref[b - 1 : b + 7, :]
            g_c[b : b + 8, :] -= k_c[b : b + 8, :] * (here - pltpu.roll(here, 1, 1))
            g_r[b : b + 8, :] -= k_r[b : b + 8, :] * (here - up)

    def spread(g_c, g_r, b):
        east = g_c[b : b + 8, :]
        return (pltpu.roll(east, east.shape[1] - 1, 1) - east) + (
            g_r[b + 1 : b + 9, :] - g_r[b : b + 8, :]
        )

    def means(x):
        high, low = split2(x)
        return jnp.dot(high.astype(BF16), amat[...], preferred_element_type=F32) + jnp.dot(
            low.astype(BF16), amat[...], preferred_element_type=F32
        )

    def block_means(k, sums):
        for j in range(cw // 128):
            work[j] = sums[:, j * 128 : (j + 1) * 128]
            avgs[k, :, j * 128 : (j + 1) * 128] = sum(
                work[j, pl.ds(i, brows, stride=RATIO), :] for i in range(RATIO)
            )
        avg_send(k)

        @pl.when(tile == 0)
        def _():
            avgr[k, LEAD : LEAD + brows, :] = avgs[k]

    lane = iota((1, fw), 1)
    odd, upper = lane % 2 == 1, lane % 4 >= 2

    def lane_means(x):
        x = x + jnp.where(odd, pltpu.roll(x, 1, 1), pltpu.roll(x, fw - 1, 1))
        x = x + jnp.where(upper, pltpu.roll(x, 2, 1), pltpu.roll(x, fw - 2, 1))
        return x * (1.0 / (RATIO * RATIO))

    erow = iota((16, fw), 0)

    def step(k, carry, keep=False):
        c0, g0, h1 = carry

        lev[LEAD - 1 : LEAD, :] = jnp.where(tile == 0, c0, lev[LEAD - 1 : LEAD, :])
        if ends:
            esum[k] = lev[top - 8 : top, :]
        mean = lane_means(jnp.sum(lev[LEAD : LEAD + RATIO, :], axis=0, keepdims=True))
        g0 = g0 - kc0 * (c0 - pltpu.roll(c0, RATIO, 1))
        h1 = h1 - kr1 * (mean - c0)
        c0 = c0 - ((pltpu.roll(g0, fw - RATIO, 1) - g0) + h1)
        push(lev, gc, gr, kc, kr, strips)
        for b in strips:
            new = lev[b : b + 8, :] - spread(gc, gr, b)
            lev[b : b + 8, :] = new
            if LEAD <= b < top:
                r = slice(b - LEAD, b - LEAD + 8)
                peak_o[r, :] = jnp.maximum(peak_o[r, :], new[:, 0:cols])
                if keep:
                    total[r, :] += new
        return c0, g0, h1

    zero = jnp.zeros((1, fw), F32)
    carry = lax.fori_loop(
        0, STEPS - 2, functools.partial(step, keep=True), (join3(wide, 0), zero, zero)
    )
    sums = means(total[...])
    carry = step(STEPS - 2, carry)
    block_means(0, sums)
    block_means(1, means(lev[LEAD:top, :]))
    carry = step(STEPS - 1, carry)
    if ends:
        @pl.when(is_last)
        def _():
            sums = jnp.zeros(erow.shape, F32)
            for k in range(STEPS):
                above = jnp.sum(esum[k, 0:4, :], axis=0, keepdims=True)
                below = jnp.sum(esum[k, 4:8, :], axis=0, keepdims=True)
                sums = jnp.where(erow == 2 * k, above, jnp.where(erow == 2 * k + 1, below, sums))
            edges[...] = means(sums)
            edge_copy().start()
    surf_o[...] = lev[LEAD:top, 0:cols]

    @pl.when(tile >= nested)
    def _():
        if ends:
            pl.when(tile == nested)(lambda: edge_copy().wait_recv())
        erows = iota((16, cw), 0)
        crow = iota((8, cw), 0)

        def cstep(k, carry):
            def edge(i):
                return jnp.sum(jnp.where(erows == 2 * k + i, edger[...], 0.0), axis=0, keepdims=True)

            @pl.when(tile == nested)
            def _():
                clev[LEAD - 8 : LEAD, :] = jnp.where(crow == 7, edge(0), clev[LEAD - 8 : LEAD, :])
                clev[LEAD : LEAD + 8, :] = jnp.where(crow == 0, edge(1), clev[LEAD : LEAD + 8, :])

            push(clev, cgc, cgr, ckc, ckr, cstrips)
            for b in cstrips:
                clev[b : b + 8, :] -= spread(cgc, cgr, b)
            return carry

        lax.fori_loop(0, STEPS, cstep, 0)
        coarse_o[...] = clev[LEAD : LEAD + crows, 0:ccols]

    @pl.when(tile < nested)
    def _():
        c0, g0, h1 = carry
        narrow = RATIO * jnp.dot(stack3([c0, h1]), amat[...], preferred_element_type=F32)
        avg_wait(0)
        avg_wait(1)
        for b in range(LEAD, LEAD + crows + 8, 8):
            clev[b : b + 8, :] = avgr[0, b - 1 : b + 7, :] + avgr[1, b - 1 : b + 7, :]
        clev[LEAD - 1 : LEAD, :] = avgr[0, LEAD - 2 : LEAD - 1, :] + avgr[1, LEAD - 2 : LEAD - 1, :]
        inner = range(LEAD, LEAD + crows + 8, 8)
        push(clev, cgc, cgr, ckc, ckr, inner)

        @pl.when(tile == 0)
        def _():
            cgr[LEAD + 1 : LEAD + 2, :] = join3(narrow, 1)

        for b in range(LEAD, LEAD + crows, 8):
            new = avgr[1, b - 1 : b + 7, :] - spread(cgc, cgr, b)
            coarse_o[b - LEAD : b - LEAD + 8, :] = new[:, 0:ccols]

        @pl.when(tile == 0)
        def _():
            coarse_o[0:1, :] = join3(narrow, 0)[:, 0:ccols]

    slip_copy.wait_send()
    rest = pl.ds(0, owners - 1)
    for h in range(2):
        pair_copy(send.at[h, rest], recv.at[h, rest], a_ss.at[h], a_rs.at[h, 0], me).wait_send()
    pair_copy(mrecv.at[rest], mrecv.at[rest], m_ss.at[0], m_rs.at[0], me).wait_send()
    landed(hcore, 5, 8).wait_send()
    for kind, v, dst, n in [(1, 0, hvert.at[0], 0), (1, 1, hvert.at[1], 1), (0, 0, hside, 2)] + [
        (2, v, hcorn.at[v], 3 + v) for v in range(2)
    ]:
        pl.when(goes(kind, v, 1))(lambda dst=dst, n=n: landed(dst, n, 8).wait_send())
    for k in range(2):
        for kind in range(ways):
            pl.when(avg_goes(kind))(lambda k=k, kind=kind: avg_copy(k, kind).wait_send())
    if ends:
        pl.when(is_last)(lambda: edge_copy().wait_send())


def store(peak, surf, coarse, peak_h, surf_h, coarse_h, sems):
    pairs = [(peak, peak_h), (surf, surf_h), (coarse, coarse_h)]
    copies = [pltpu.make_async_copy(src, dst, sems.at[i]) for i, (src, dst) in enumerate(pairs)]
    for copy in copies:
        copy.start()
    for copy in copies:
        copy.wait()


def shards(dims, green, row_owner, row_index, row_fault, slip, depth, wet, coarse_depth, coarse_start):
    planes, tiles, cols_n, subs_n = dims
    owners = tiles * cols_n * subs_n
    entries, cols = green.shape
    rows = depth.shape[0]
    crows, ccols = coarse_depth.shape
    capacity = max(2, (2 * entries + owners - 1) // owners)
    capp = (capacity + 15) // 16 * 16
    packs = owners // (128 // capp)
    hw = cols // planes
    i32 = lambda *shape: pltpu.VMEM(shape, jnp.int32)
    ways = 3 if tiles * (rows // RATIO) // crows > 1 else 1
    fw, cw = cols + 128, ccols + 128
    high, chigh = rows + 32, crows + 32
    vmem = lambda *shape: pltpu.VMEM(shape, F32)
    dma = pltpu.SemaphoreType.DMA
    keep = lambda x: pltpu.with_memory_space_constraint(x, pltpu.HBM)
    results = pl.pallas_call(
        functools.partial(kernel, dims),
        out_shape=(
            jax.ShapeDtypeStruct((rows, cols), F32),
            jax.ShapeDtypeStruct((rows, cols), F32),
            jax.ShapeDtypeStruct((crows, ccols), F32),
        ),
        in_specs=[pl.BlockSpec(memory_space=pltpu.HBM)] * 9,
        out_specs=(pl.BlockSpec(memory_space=pltpu.VMEM),) * 3,
        scratch_shapes=[
            pltpu.VMEM((entries, hw), BF16), i32(1, entries), i32(1, entries), i32(1, entries),
            vmem(1, slip.shape[0]), vmem(rows, cols), i32(rows, cols),
            pltpu.VMEM((owners * capp, entries), BF16), vmem(owners, entries),
            pltpu.VMEM((2, owners, capp, 128), BF16),
            pltpu.VMEM((2, owners, capp, 128), BF16),
            vmem(owners, 1, 128), vmem(owners, 1, 128),
            vmem(8, 128), vmem(8, 128), vmem(4 * rows, 128),
            pltpu.VMEM((packs, 4 * rows, 128), BF16),
            vmem(rows + 8, cols + 512), vmem(2, rows + 8, 384), vmem(2, 8, cols + 256),
            vmem(2, 2, 8, 384),
            vmem(2, 2 * rows, 128), vmem(2, rows, 128), vmem(2, rows // 4, 128), vmem(2, rows // 4, 128), vmem(2, 2, 2, 8, 128),
            vmem(2, 2, 8, 128),
        ]
        + [vmem(high, fw)] * 6
        + [vmem(chigh, cw)] * 6
        + [
            pltpu.VMEM((fw, cw), BF16), pltpu.VMEM((cw, fw), BF16),
            vmem(cw // 128, rows, 128),
            vmem(rows, fw), vmem(2, rows // RATIO, cw), vmem(2, chigh, cw),
            vmem(STEPS, 8, fw), vmem(16, cw), vmem(16, cw),
            dma((12,)), dma((2,)), dma((2, packs)), dma((1,)), dma((packs,)), dma((2,)), dma((8,)), dma((6,)),
            dma((9,)), dma((3, ways)), pltpu.SemaphoreType.REGULAR((tiles + 1,)),
        ],
        compiler_params=pltpu.CompilerParams(
            collective_id=0, has_side_effects=True, vmem_limit_bytes=48 * 1024 * 1024
        ),
    )(
        keep(green), keep(row_owner.reshape(1, entries)), keep(row_index.reshape(1, entries)),
        keep(row_fault.reshape(1, entries)), keep(slip.reshape(1, -1)), keep(depth), keep(wet), keep(coarse_depth), keep(coarse_start),
    )
    return pl.pallas_call(
        store,
        out_shape=tuple(jax.ShapeDtypeStruct(x.shape, F32) for x in results),
        in_specs=[pl.BlockSpec(memory_space=pltpu.VMEM)] * 3,
        out_specs=(pl.BlockSpec(memory_space=pltpu.HBM),) * 3,
        scratch_shapes=[dma((3,))],
        compiler_params=pltpu.CompilerParams(vmem_limit_bytes=1024 * 1024),
    )(*results)


def solution(mesh):
    dims = tuple(mesh.shape[a] for a in ("scen", "tile", "col", "sub"))
    return jax.shard_map(
        functools.partial(shards, dims),
        mesh=mesh,
        in_specs=(
            P(("tile", "col", "sub"), None),
            P(("tile", "col", "sub"), None),
            P(("tile", "col", "sub")),
            P(("tile", "col", "sub")),
            P(("scen", "tile", "col", "sub")),
            P("tile", ("col", "sub")),
            P("tile", ("col", "sub")),
            P("tile", ("col", "sub")),
            P(("scen", "tile"), ("col", "sub")),
        ),
        out_specs=(
            P(("scen", "tile"), ("col", "sub")),
            P(("scen", "tile"), ("col", "sub")),
            P(("scen", "tile"), ("col", "sub")),
        ),
        check_vma=False,
    )
```

```python
import functools
import jax
import jax.numpy as jnp
from jax import lax
from jax.experimental import pallas as pl
from jax.experimental.pallas import tpu as pltpu
from jax.sharding import PartitionSpec as P

RATIO = 4
STEPS = 6
HALO = 8
LEAD = 16
F32 = jnp.float32
BF16 = jnp.bfloat16
MESH = pl.DeviceIdType.MESH


def split2(x):
    high = x.astype(BF16).astype(F32)
    return high, (x - high).astype(BF16).astype(F32)


def iota(shape, dim):
    return lax.broadcasted_iota(jnp.int32, shape, dim)


def kernel(
    dims,
    green_h, owner_h, index_h, fault_h, slip_h, depth_h, wet_h, cdep_h, cstart_h,
    peak_o, surf_o, coarse_o,
    green, owner, index, fault, slip, depth, wet, chosen_r,
    place, send, recv, msend, mrecv, slip_s, slip_r, acc, weights,
    zs, zside, zvert, zcorn,
    half, hcore, packed, hside, hvert, hcorn,
    lev, held, gc, gr, kc, kr,
    clev, cheld, cgc, cgr, ckc, ckr,
    amat, rmat, work, total, avgs, avgr, esum, edges, edger,
    i_s, a_ss, a_rs, m_ss, m_rs, sl_s, z_rs, h_ss, h_rs, v_rs, alive,
):
    planes, tiles, cols_n, subs_n = dims
    sides = cols_n * subs_n
    owners = tiles * sides
    plane = lax.axis_index("scen")
    tile = lax.axis_index("tile")
    side = lax.axis_index("col") * subs_n + lax.axis_index("sub")
    me = tile * sides + side
    rows, cols = depth.shape
    crows, ccols = cdep_h.shape
    entries, hw = green.shape
    capp = send.shape[2]
    pack = 128 // capp
    packs = owners // pack
    fw = cols + 128
    cw = ccols + 128
    top = LEAD + rows

    def dev(p, t, c):
        return {"scen": p, "tile": t, "col": c // subs_n, "sub": c % subs_n}

    def fetch(i):
        edge_lanes = pl.ds(pl.multiple_of(plane * (hw + 128), 128), 128)
        inner_lanes = pl.ds(pl.multiple_of(128 + plane * 128, 128), 128)
        far = 256 + cols
        src, dst = [
            (owner_h, owner), (green_h.at[:, edge_lanes], green.at[:, 0:128]), (index_h, index), (fault_h, fault),
            (slip_h, slip), (depth_h, depth), (wet_h, wet),
            (cdep_h, zs.at[0:rows, 0:ccols]), (cstart_h, zs.at[0:rows, 128 : 128 + ccols]),
            (cdep_h, zs.at[0:rows, far : far + ccols]),
            (cstart_h, zs.at[0:rows, far + 128 : far + 128 + ccols]),
            (green_h.at[:, inner_lanes], green.at[:, 128:256]),
        ][i]
        return pltpu.make_async_copy(src, dst, i_s.at[i])

    barrier = pltpu.get_barrier_semaphore()

    other = planes - 1 - plane

    def hail(sem):
        def start(i, carry):
            pl.semaphore_signal(
                sem, inc=1, device_id=dev(plane, i // sides, lax.rem(i, sides)), device_id_type=MESH
            )
            return carry

        return start

    def hail_other(sem):
        pl.semaphore_signal(sem, inc=1, device_id=dev(other, tile, side), device_id_type=MESH)

    lax.fori_loop(me + 1, owners, hail(barrier), 0)
    pl.when(plane == 0)(lambda: hail_other(barrier))
    for i in (4, 0, 1, 11, 2, 3, 5, 6, 7, 8, 9, 10):
        fetch(i).start()

    slip_copy = pltpu.make_async_remote_copy(
        src_ref=slip_s, dst_ref=slip_r, send_sem=sl_s.at[0], recv_sem=sl_s.at[1],
        device_id=dev(other, tile, side), device_id_type=MESH,
    )
    fetch(4).wait()
    slip_s[...] = jnp.zeros_like(slip_s)
    slip_s[0:1, 0 : slip.shape[1]] = slip[...]
    pl.when(me + plane > 0)(lambda: pl.semaphore_wait(barrier, me + plane))

    @pl.when(plane > 0)
    def _():
        hail_other(alive.at[tiles])
        slip_copy.start()

    lax.fori_loop(0, me, hail(alive.at[tile]), 0)

    fetch(0).wait()
    dest = owner[...]
    hit = iota((owners, entries), 0) == dest
    before = (iota((entries, entries), 0) < iota((entries, entries), 1)).astype(F32).astype(BF16)
    rank = jnp.dot(hit.astype(F32).astype(BF16), before, preferred_element_type=F32)
    place[...] = jnp.where(hit, rank, -1.0)
    group = min(owners, 512 // capp)
    groups = owners // group
    fetch(1).wait()
    fetch(11).wait()
    gh = green[...]
    slots = iota((group, capp, entries), 1).astype(F32)

    def select(g):
        rows_of = place[pl.ds(pl.multiple_of(g * group, group), group), :]
        chosen = jnp.where(rows_of[:, None, :] == slots, 1.0, 0.0)
        chosen = chosen.reshape(group * capp, entries).astype(BF16)
        chosen_r[pl.ds(g * group * capp, group * capp), :] = chosen
        return chosen

    def fill(g, carry):
        picked = jnp.dot(select(g), gh, preferred_element_type=F32).astype(BF16)
        for h in range(2):
            send[h, pl.ds(g * group, group)] = picked[:, h * 128 : (h + 1) * 128].reshape(group, capp, 128)
        return carry

    fill(0, 0) if groups == 1 else lax.fori_loop(0, groups, fill, 0)

    for i in (2, 3, 5, 6, 7, 8, 9, 10):
        fetch(i).wait()
    raw = depth[...]
    zs[0:rows, 256 : 256 + cols] = jnp.where(wet[...] > 0, raw, 0.0)
    zs[rows : rows + 8, 256 : 256 + cols] = jnp.broadcast_to(raw[0:1], (8, cols))
    for off in (0, 256 + cols):
        zs[rows : rows + 8, off : off + 256] = jnp.zeros((8, 256), F32)

    def pair_copy(src, dst, s_sem, r_sem, d):
        return pltpu.make_async_remote_copy(
            src_ref=src, dst_ref=dst, send_sem=s_sem, recv_sem=r_sem,
            device_id=dev(plane, d // sides, lax.rem(d, sides)), device_id_type=MESH,
        )

    def a2a(h, d):
        return pair_copy(send.at[h, d], recv.at[h, me], a_ss.at[h], a_rs.at[h, me // pack], d)

    def a2a_meta(d):
        return pair_copy(msend.at[d], mrecv.at[me], m_ss.at[0], m_rs.at[me // pack], d)

    def a2a_wait(h, g, n):
        got = recv.at[h, pl.ds(g * pack, n)]
        pair_copy(got, got, a_ss.at[h], a_rs.at[h, g], me).wait_recv()

    def meta_wait(g, n):
        got = mrecv.at[pl.ds(g * pack, n)]
        pair_copy(got, got, m_ss.at[0], m_rs.at[g], me).wait_recv()

    middle = tiles // 2
    low = tile < middle
    across = jnp.where(low, tiles - middle, middle)

    def launch_tile(t, start):
        first = t * sides

        def own(i, carry):
            start(first + lax.rem(side + i, sides)).start()
            return carry

        lax.fori_loop(jnp.where(t == tile, 1, 0), sides, own, 0)

    def launch_far(start):
        def far(i, carry):
            launch_tile(jnp.where(low, tiles - 1 - i, i), start)
            return carry

        lax.fori_loop(0, across, far, 0)

    def launch_near(start):
        def near(i, carry):
            t = jnp.where(low, i, middle + i)
            pl.when(t != tile)(lambda: launch_tile(t, start))
            return carry

        lax.fori_loop(0, tiles - across, near, 0)

    def launch_one(d, carry):
        a2a(0, d).start()
        return carry

    def launch_met(t, carry):
        pl.semaphore_wait(alive.at[t], sides)
        launch_tile(t, functools.partial(a2a, 0))
        return carry

    lax.fori_loop(0, me, launch_one, 0)
    @pl.when(plane == 0)
    def _():
        pl.semaphore_wait(alive.at[tiles], 1)
        slip_copy.start()

    pl.when(side < sides - 1)(lambda: pl.semaphore_wait(alive.at[tile], sides - 1 - side))
    lax.fori_loop(me + 1, (tile + 1) * sides, launch_one, 0)
    lax.fori_loop(tile + 1, tiles, launch_met, 0)

    moves = [(0, -1), (0, 1), (-1, 0), (1, 0), (-1, -1), (-1, 1), (1, -1), (1, 1)]

    def static_copy(i):
        dy, dx = moves[i]
        lanes = (
            slice(0, 512 - 128) if dx == -1
            else slice(cols + 128, cols + 512) if dx == 1 else slice(0, 256 + cols)
        )
        sel = slice(0, rows + 8) if dy == 0 else slice(0, 8) if dy == -1 else slice(rows - 8, rows)
        bi = 0 if dy == -1 else 1
        bj = 0 if dx == -1 else 1
        dst = zside.at[bj] if dy == 0 else zvert.at[bi] if dx == 0 else zcorn.at[bi, bj]
        return pltpu.make_async_remote_copy(
            src_ref=zs.at[sel, lanes], dst_ref=dst, send_sem=i_s.at[i], recv_sem=z_rs.at[i],
            device_id=dev(plane, tile + dy, side + dx), device_id_type=MESH,
        )

    def inside(dy, dx):
        ok = True
        for at, by, size in ((tile, dy, tiles), (side, dx, sides)):
            if by == -1:
                ok = jnp.logical_and(ok, at > 0)
            if by == 1:
                ok = jnp.logical_and(ok, at < size - 1)
        return ok

    slip_copy.wait_recv()

    mrow = iota((8, slip.shape[1]), 0)
    own_h, own_l = split2(slip[...])
    oth_h, oth_l = split2(slip_r[0:1, 0 : slip.shape[1]])
    parts = jnp.where(mrow == 1, own_h, 0.0)
    for i, part in ((2, own_l), (3, oth_h), (4, oth_l)):
        parts = jnp.where(mrow == i, part, parts)
    picks = (iota((slip.shape[1], entries), 0) == fault[...]).astype(F32).astype(BF16)
    meta = jnp.dot(parts.astype(BF16), picks, preferred_element_type=F32)
    meta = jnp.where(iota((8, entries), 0) == 0, index[...].astype(F32), meta).astype(BF16)

    lane_of = iota((1, 128), 1)
    within = [(lane_of >= i * capp) & (lane_of < (i + 1) * capp) for i in range(pack)]

    def shifted(x, by):
        by = by % pack
        return pltpu.roll(x, by * capp, 1) if by else x

    def describe(g, carry):
        told = lax.dot_general(
            meta, chosen_r[pl.ds(g * group * capp, group * capp), :], (((1,), (1,)), ((), ())), preferred_element_type=F32
        )
        quantities = [told[0:1], told[1:2] + told[2:3], told[3:4] + told[4:5]]
        for i in range(group // pack):
            parts_of = [q[:, i * 128 : (i + 1) * 128] for q in quantities]
            for j in range(pack):
                record = jnp.zeros((1, 128), F32)
                for q, part in enumerate(parts_of):
                    record = jnp.where(within[q], shifted(part, q - j), record)
                msend[g * group + i * pack + j] = record
        return carry

    describe(0, 0) if groups == 1 else lax.fori_loop(0, groups, describe, 0)

    inner = functools.partial(a2a, 1)
    launch_far(a2a_meta)
    launch_tile(tile, a2a_meta)
    launch_far(inner)
    launch_near(a2a_meta)
    launch_tile(tile, inner)
    launch_near(inner)

    fl = iota((fw, cw), 0)
    fmap = jnp.where(fl < cols + 64, fl // RATIO, fl // RATIO + (cw - fw // RATIO))
    amat[...] = jnp.where(fmap == iota((fw, cw), 1), 1.0 / (RATIO * RATIO), 0.0).astype(BF16)
    rl = iota((cw, fw), 1)
    rmap = jnp.where(rl < cols + 64, rl // RATIO, rl // RATIO + (cw - fw // RATIO))
    rmat[...] = jnp.where(rmap == iota((cw, fw), 0), 1.0, 0.0).astype(BF16)
    for ref in (lev, held, gc, gr, clev, cheld, cgc, cgr):
        ref[...] = jnp.zeros_like(ref)

    for bj in range(2):
        dx = 1 if bj == 0 else -1
        @pl.when(jnp.logical_not(inside(0, dx)))
        def _(bj=bj):
            zside[bj] = jnp.zeros(zside.shape[1:], F32)
        for bi in range(2):
            dy = 1 if bi == 0 else -1
            @pl.when(jnp.logical_not(inside(dy, dx)))
            def _(bi=bi, bj=bj):
                zcorn[bi, bj] = jnp.zeros(zcorn.shape[2:], F32)
    for bi in range(2):
        dy = 1 if bi == 0 else -1
        @pl.when(jnp.logical_not(inside(dy, 0)))
        def _(bi=bi):
            zvert[bi] = jnp.zeros(zvert.shape[1:], F32)
    wrow = iota((4 * rows, 128), 0)
    in_tile = lax.rem(wrow, rows).astype(F32)
    recv[0, me] = send[0, me]
    recv[1, me] = send[1, me]
    mrecv[me] = msend[me]

    def product(h, g, weight):
        block = recv[h, pl.ds(g * pack, pack)].reshape(128, 128)
        return jnp.dot(weight, block, preferred_element_type=F32)

    def put(g):
        told = [jnp.zeros((1, 128), F32)] * 3
        for j in range(pack):
            record = mrecv[g * pack + j]
            told = [jnp.where(within[j], shifted(record, j - q), t) for q, t in enumerate(told)]
        (own_h, own_l), (oth_h, oth_l) = split2(told[1]), split2(told[2])
        weight = jnp.where(
            wrow < rows, own_h,
            jnp.where(wrow < 2 * rows, oth_h, jnp.where(wrow < 3 * rows, own_l, oth_l)),
        )
        weight = jnp.where(in_tile == told[0], weight, 0.0).astype(BF16)
        weights[g] = weight
        return product(0, g, weight)

    mine = me // pack

    def take(i, carry):
        g = lax.rem(mine + i, packs)
        a2a_wait(0, g, pack)
        meta_wait(g, pack)
        acc[...] += put(g)
        return carry

    def fold():
        return acc[0 : 2 * rows, :] + acc[2 * rows : 4 * rows, :]

    a2a_wait(0, mine, pack - 1)
    meta_wait(mine, pack - 1)
    acc[...] = put(mine)
    lax.fori_loop(1, packs - 1, take, 0, unroll=packs == 4)
    for i, (dy, dx) in enumerate(moves):
        pl.when(inside(dy, dx))(lambda i=i: static_copy(i).start())

    take(packs - 1, 0)
    half[0] = fold()

    toward = 2 * plane - 1

    def core_copy(h):
        return pltpu.make_async_remote_copy(
            src_ref=half.at[h, rows : 2 * rows, :], dst_ref=hcore.at[h], send_sem=h_ss.at[5],
            recv_sem=h_rs.at[8], device_id=dev(other, tile, side), device_id_type=MESH,
        )

    def halo_copy(h, s, kind, v, q):
        to_plane = plane if s == 0 else other
        dy = 0 if kind == 0 else (-1 if v == 0 else 1)
        r0 = s * rows + (0 if v == 0 else rows - 8)
        if kind == 0:
            src, dst, n, m = packed.at[s], hside.at[q], 2, 2 + q
        elif kind == 1:
            src, dst, n, m = half.at[h, r0 : r0 + 8, :], hvert.at[v, q, h], v, v
        else:
            src, dst, n, m = half.at[h, r0 : r0 + 8, :], hcorn.at[v, q], 3 + v, 4 + 2 * v + q
        return pltpu.make_async_remote_copy(
            src_ref=src, dst_ref=dst, send_sem=h_ss.at[n], recv_sem=h_rs.at[m],
            device_id=dev(to_plane, tile + dy, side if kind == 1 else side + toward),
            device_id_type=MESH,
        )

    kinds = [(0, 1, 0), (0, 1, 1), (0, 0, 0), (0, 2, 0), (0, 2, 1), (1, 1, 0), (1, 1, 1)]

    def goes(kind, v, sign):
        dy = 0 if kind == 0 else (-1 if v == 0 else 1) * sign
        ok = inside(dy, 0)
        if kind != 1:
            to = side + toward
            ok = jnp.logical_and(ok, jnp.logical_and(to >= 0, to < sides))
        return ok

    quarter = rows // 4
    qlane = iota((quarter, 128), 1)

    def turn_lanes(x, by):
        by = by % 128
        return pltpu.roll(x, by, 1) if by else x

    def send_half(half_of):
        core_copy(half_of).start()
        if half_of == 0:
            for s in range(2):
                strip = jnp.zeros((quarter, 128), F32)
                for j in range(4):
                    r0 = s * rows + j * quarter
                    x = half[0, r0 : r0 + quarter, :]
                    moved = jnp.where(plane == 0, turn_lanes(x, 32 * j), turn_lanes(x, 32 * j + 32))
                    strip = jnp.where(qlane // 32 == j, moved, strip)
                packed[s] = strip
        for s in (1, 0):
            for h, kind, v in kinds:
                if h == half_of:
                    pl.when(goes(kind, v, 1))(
                        lambda s=s, h=h, kind=kind, v=v: halo_copy(h, s, kind, v, plane).start()
                    )

    send_half(0)

    def take_inner(i, carry):
        g = lax.rem(mine + i, packs)
        a2a_wait(1, g, pack)
        acc[...] += product(1, g, weights[g])
        return carry

    a2a_wait(1, mine, pack - 1)
    acc[...] = product(1, mine, weights[mine])
    lax.fori_loop(1, packs, take_inner, 0, unroll=packs == 4)
    half[1] = fold()
    send_half(1)

    def lanes_of(p, h):
        return p * (hw + 128) if h == 0 else 128 + p * 128

    for h in range(2):
        lev[LEAD:top, pl.ds(pl.multiple_of(lanes_of(plane, h), 128), 128)] = half[h, 0:rows, :]

    def comes(kind, v, q):
        dy = 0 if kind == 0 else (1 if v == 0 else -1)
        dx = 0 if kind == 1 else (1 if q == 0 else -1)
        return inside(dy, dx)

    for i, (dy, dx) in enumerate(moves):
        pl.when(inside(-dy, -dx))(lambda i=i: static_copy(i).wait_recv())

    def merge(right, left):
        return jnp.where(iota(right.shape, right.ndim - 1) < 64, right, left)

    def place_static(r0, n, z, zr, zl, sr):
        held[r0 : r0 + n, 0:cols] = z[sr, 256 : 256 + cols]
        held[r0 : r0 + n, cols:fw] = merge(zr[sr, 256:384], zl[sr, 0:128])
        cheld[r0 : r0 + n, 0:ccols] = z[sr, 0:128]
        cheld[r0 : r0 + n, ccols:cw] = merge(zr[sr, 0:128], zl[sr, 128:256])
        clev[r0 : r0 + n, 0:ccols] = z[sr, 128:256]
        clev[r0 : r0 + n, ccols:cw] = merge(zr[sr, 128:256], zl[sr, 256:384])

    place_static(LEAD, rows, zs, zside.at[0], zside.at[1], slice(0, rows))
    place_static(top, 8, zvert.at[0], zcorn.at[0, 0], zcorn.at[0, 1], slice(0, 8))
    place_static(8, 8, zvert.at[1], zcorn.at[1, 0], zcorn.at[1, 1], slice(0, 8))

    @pl.when(tile == 0)
    def _():
        held[LEAD - 1 : LEAD, 0:cols] = depth[0:1, :]
        held[LEAD - 1 : LEAD, cols:fw] = merge(
            zside[0, rows : rows + 1, 256:384], zside[1, rows : rows + 1, 0:128]
        )

    strips = [8 + 8 * i for i in range((rows + 16) // 8)]
    cstrips = [8 + 8 * i for i in range((crows + 16) // 8)]

    def faces(h, k_c, k_r, scale, which):
        width = h.shape[1]
        for b in which:
            here, up = h[b : b + 8, :], h[b - 1 : b + 7, :]
            west = pltpu.roll(here, 1, 1)
            k_c[b : b + 8, :] = jnp.where((here > 0.0) & (west > 0.0), scale * (here + west), 0.0)
            k_r[b : b + 8, :] = jnp.where((here > 0.0) & (up > 0.0), scale * (here + up), 0.0)

    faces(held, kc, kr, 0.5 * 0.5 * 0.5, strips)
    faces(cheld, ckc, ckr, 0.5 * 0.125 * 0.125, cstrips)

    def stack3(values):
        rows_of = iota((16, values[0].shape[1]), 0)
        out = jnp.zeros(rows_of.shape, F32)
        for i, v in enumerate(values):
            first, rest = split2(v)
            second, third = split2(v - first)
            for j, part in enumerate((first, second, third)):
                out = jnp.where(rows_of == 3 * i + j, part, out)
        return out.astype(BF16)

    def join3(wide, i):
        return wide[3 * i : 3 * i + 1] + wide[3 * i + 1 : 3 * i + 2] + wide[3 * i + 2 : 3 * i + 3]

    wide = jnp.dot(
        stack3([clev[LEAD : LEAD + 1, :], ckc[LEAD : LEAD + 1, :], ckr[LEAD + 1 : LEAD + 2, :]]),
        rmat[...], preferred_element_type=F32,
    )
    kc0, kr1 = join3(wide, 1), join3(wide, 2)
    def landed(dst, n, m):
        return pltpu.make_async_remote_copy(
            src_ref=dst, dst_ref=dst, send_sem=h_ss.at[n], recv_sem=h_rs.at[m],
            device_id=dev(other, tile, side), device_id_type=MESH,
        )

    arrivals = [(1, v, 0, hvert.at[v], v) for v in range(2)]
    for q in range(2):
        arrivals.append((0, 0, q, hside.at[q], 2 + q))
        arrivals += [(2, v, q, hcorn.at[v, q], 4 + 2 * v + q) for v in range(2)]
    for kind, v, q, dst, m in arrivals:
        @pl.when(jnp.logical_not(comes(kind, v, q)))
        def _(dst=dst):
            dst[...] = jnp.zeros(dst.shape, F32)
        pl.when(comes(kind, v, q))(lambda dst=dst, m=m: landed(dst, 5, m).wait_recv())
    landed(hcore, 5, 8).wait_recv()

    for i, (dy, dx) in enumerate(moves):
        pl.when(inside(dy, dx))(lambda i=i: static_copy(i).wait_send())

    for h in range(2):
        lev[LEAD:top, pl.ds(pl.multiple_of(lanes_of(other, h), 128), 128)] = hcore[h]
    for j in range(4):
        right, left = turn_lanes(hside[0], -32 * j), turn_lanes(hside[1], 96 - 32 * j)
        lev[LEAD + j * quarter : LEAD + (j + 1) * quarter, cols:fw] = jnp.where(
            qlane < 32, right, jnp.where(qlane >= 96, left, 0.0)
        )
    for v, r0 in ((0, top), (1, 8)):
        for q in range(2):
            for h in range(2):
                lev[r0 : r0 + 8, lanes_of(q, h) : lanes_of(q, h) + 128] = hvert[v, q, h]
        lev[r0 : r0 + 8, cols:fw] = merge(hcorn[v, 0], hcorn[v, 1])

    brows = rows // RATIO
    per = crows * RATIO // rows
    nest = brows * tiles
    nested = nest // crows
    ct = tile // per
    cm = lax.rem(tile, per)

    def avg_copy(k, kind):
        if kind == 0:
            src, to = avgs.at[k], ct
            dst = avgr.at[k, pl.ds(pl.multiple_of(LEAD + cm * brows, 8), brows), :]
        elif kind == 1:
            src, to = avgs.at[k, brows - 8 : brows, :], ct + 1
            dst = avgr.at[k, 8:16, :]
        else:
            src, to = avgs.at[k, 0:8, :], ct - 1
            dst = avgr.at[k, LEAD + crows : LEAD + crows + 8, :]
        return pltpu.make_async_remote_copy(
            src_ref=src, dst_ref=dst, send_sem=i_s.at[8 + k if kind == 0 else 2 * kind + k], recv_sem=v_rs.at[k, kind],
            device_id=dev(plane, to, side), device_id_type=MESH,
        )

    def avg_goes(kind):
        if kind == 0:
            return tile > 0
        if kind == 1:
            return jnp.logical_and(cm == per - 1, ct + 1 < nested)
        return jnp.logical_and(cm == 0, ct > 0)

    ways = v_rs.shape[1]

    def avg_send(k):
        for kind in range(ways):
            pl.when(avg_goes(kind))(lambda kind=kind: avg_copy(k, kind).start())

    def avg_wait(k):
        def wait(kind, dst):
            pltpu.make_async_remote_copy(
                src_ref=dst, dst_ref=dst, send_sem=i_s.at[8], recv_sem=v_rs.at[k, kind],
                device_id=dev(plane, tile, side), device_id_type=MESH,
            ).wait_recv()

        pl.when(tile == 0)(lambda: wait(0, avgr.at[k, LEAD + brows : LEAD + per * brows, :]))
        pl.when(tile > 0)(lambda: wait(0, avgr.at[k, LEAD : LEAD + per * brows, :]))
        if ways == 1:
            return
        pl.when(tile > 0)(lambda: wait(1, avgr.at[k, 8:16, :]))
        pl.when(tile < nested - 1)(lambda: wait(2, avgr.at[k, LEAD + crows : LEAD + crows + 8, :]))

    def edge_copy():
        return pltpu.make_async_remote_copy(
            src_ref=edges, dst_ref=edger, send_sem=i_s.at[10], recv_sem=v_rs.at[2, 0],
            device_id=dev(plane, nested, side), device_id_type=MESH,
        )

    ends = nested < tiles
    is_last = tile == tiles - 1

    def push(s_ref, g_c, g_r, k_c, k_r, which):
        for b in which:
            here, up = s_ref[b : b + 8, :], s_ref[b - 1 : b + 7, :]
            g_c[b : b + 8, :] -= k_c[b : b + 8, :] * (here - pltpu.roll(here, 1, 1))
            g_r[b : b + 8, :] -= k_r[b : b + 8, :] * (here - up)

    def spread(g_c, g_r, b):
        east = g_c[b : b + 8, :]
        return (pltpu.roll(east, east.shape[1] - 1, 1) - east) + (
            g_r[b + 1 : b + 9, :] - g_r[b : b + 8, :]
        )

    def means(x):
        high, low = split2(x)
        return jnp.dot(high.astype(BF16), amat[...], preferred_element_type=F32) + jnp.dot(
            low.astype(BF16), amat[...], preferred_element_type=F32
        )

    def block_means(k, sums):
        for j in range(cw // 128):
            work[j] = sums[:, j * 128 : (j + 1) * 128]
            avgs[k, :, j * 128 : (j + 1) * 128] = sum(
                work[j, pl.ds(i, brows, stride=RATIO), :] for i in range(RATIO)
            )
        avg_send(k)

        @pl.when(tile == 0)
        def _():
            avgr[k, LEAD : LEAD + brows, :] = avgs[k]

    lane = iota((1, fw), 1)
    odd, upper = lane % 2 == 1, lane % 4 >= 2

    def lane_means(x):
        x = x + jnp.where(odd, pltpu.roll(x, 1, 1), pltpu.roll(x, fw - 1, 1))
        x = x + jnp.where(upper, pltpu.roll(x, 2, 1), pltpu.roll(x, fw - 2, 1))
        return x * (1.0 / (RATIO * RATIO))

    erow = iota((16, fw), 0)

    def step(k, carry, keep=False):
        c0, g0, h1 = carry

        lev[LEAD - 1 : LEAD, :] = jnp.where(tile == 0, c0, lev[LEAD - 1 : LEAD, :])
        if ends:
            esum[k] = lev[top - 8 : top, :]
        mean = lane_means(jnp.sum(lev[LEAD : LEAD + RATIO, :], axis=0, keepdims=True))
        g0 = g0 - kc0 * (c0 - pltpu.roll(c0, RATIO, 1))
        h1 = h1 - kr1 * (mean - c0)
        c0 = c0 - ((pltpu.roll(g0, fw - RATIO, 1) - g0) + h1)
        push(lev, gc, gr, kc, kr, strips)
        for b in strips:
            old = lev[b : b + 8, :]
            new = old - spread(gc, gr, b)
            lev[b : b + 8, :] = new
            if LEAD <= b < top:
                r = slice(b - LEAD, b - LEAD + 8)
                if keep:
                    first = k == 0
                    peak_o[r, :] = jnp.maximum(
                        jnp.where(first, old[:, 0:cols], peak_o[r, :]), new[:, 0:cols]
                    )
                    total[r, :] = jnp.where(first, old, total[r, :]) + new
                else:
                    peak_o[r, :] = jnp.maximum(peak_o[r, :], new[:, 0:cols])
        return c0, g0, h1

    zero = jnp.zeros((1, fw), F32)
    carry = lax.fori_loop(
        0, STEPS - 2, functools.partial(step, keep=True), (join3(wide, 0), zero, zero), unroll=True
    )
    sums = means(total[...])
    carry = step(STEPS - 2, carry)
    block_means(0, sums)
    block_means(1, means(lev[LEAD:top, :]))
    carry = step(STEPS - 1, carry)
    if ends:
        @pl.when(is_last)
        def _():
            sums = jnp.zeros(erow.shape, F32)
            for k in range(STEPS):
                above = jnp.sum(esum[k, 0:4, :], axis=0, keepdims=True)
                below = jnp.sum(esum[k, 4:8, :], axis=0, keepdims=True)
                sums = jnp.where(erow == 2 * k, above, jnp.where(erow == 2 * k + 1, below, sums))
            edges[...] = means(sums)
            edge_copy().start()
    surf_o[...] = lev[LEAD:top, 0:cols]

    @pl.when(tile >= nested)
    def _():
        if ends:
            pl.when(tile == nested)(lambda: edge_copy().wait_recv())
        erows = iota((16, cw), 0)
        crow = iota((8, cw), 0)

        def cstep(k, carry):
            def edge(i):
                return jnp.sum(jnp.where(erows == 2 * k + i, edger[...], 0.0), axis=0, keepdims=True)

            @pl.when(tile == nested)
            def _():
                clev[LEAD - 8 : LEAD, :] = jnp.where(crow == 7, edge(0), clev[LEAD - 8 : LEAD, :])
                clev[LEAD : LEAD + 8, :] = jnp.where(crow == 0, edge(1), clev[LEAD : LEAD + 8, :])

            push(clev, cgc, cgr, ckc, ckr, cstrips)
            for b in cstrips:
                clev[b : b + 8, :] -= spread(cgc, cgr, b)
            return carry

        lax.fori_loop(0, STEPS, cstep, 0)
        coarse_o[...] = clev[LEAD : LEAD + crows, 0:ccols]

    @pl.when(tile < nested)
    def _():
        c0, g0, h1 = carry
        narrow = RATIO * jnp.dot(stack3([c0, h1]), amat[...], preferred_element_type=F32)
        avg_wait(0)
        avg_wait(1)
        for b in range(LEAD, LEAD + crows + 8, 8):
            clev[b : b + 8, :] = avgr[0, b - 1 : b + 7, :] + avgr[1, b - 1 : b + 7, :]
        clev[LEAD - 1 : LEAD, :] = avgr[0, LEAD - 2 : LEAD - 1, :] + avgr[1, LEAD - 2 : LEAD - 1, :]
        inner = range(LEAD, LEAD + crows + 8, 8)
        push(clev, cgc, cgr, ckc, ckr, inner)

        @pl.when(tile == 0)
        def _():
            cgr[LEAD + 1 : LEAD + 2, :] = join3(narrow, 1)

        for b in range(LEAD, LEAD + crows, 8):
            new = avgr[1, b - 1 : b + 7, :] - spread(cgc, cgr, b)
            coarse_o[b - LEAD : b - LEAD + 8, :] = new[:, 0:ccols]

        @pl.when(tile == 0)
        def _():
            coarse_o[0:1, :] = join3(narrow, 0)[:, 0:ccols]

    slip_copy.wait_send()
    rest = pl.ds(0, owners - 1)
    for h in range(2):
        pair_copy(send.at[h, rest], recv.at[h, rest], a_ss.at[h], a_rs.at[h, 0], me).wait_send()
    pair_copy(mrecv.at[rest], mrecv.at[rest], m_ss.at[0], m_rs.at[0], me).wait_send()
    landed(hcore, 5, 8).wait_send()
    for kind, v, dst, n in [(1, 0, hvert.at[0], 0), (1, 1, hvert.at[1], 1), (0, 0, hside, 2)] + [
        (2, v, hcorn.at[v], 3 + v) for v in range(2)
    ]:
        pl.when(goes(kind, v, 1))(lambda dst=dst, n=n: landed(dst, n, 8).wait_send())
    for k in range(2):
        for kind in range(ways):
            pl.when(avg_goes(kind))(lambda k=k, kind=kind: avg_copy(k, kind).wait_send())
    if ends:
        pl.when(is_last)(lambda: edge_copy().wait_send())


def store(peak, surf, coarse, peak_h, surf_h, coarse_h, sems):
    pairs = [(peak, peak_h), (surf, surf_h), (coarse, coarse_h)]
    copies = [pltpu.make_async_copy(src, dst, sems.at[i]) for i, (src, dst) in enumerate(pairs)]
    for copy in copies:
        copy.start()
    for copy in copies:
        copy.wait()


def shards(dims, green, row_owner, row_index, row_fault, slip, depth, wet, coarse_depth, coarse_start):
    planes, tiles, cols_n, subs_n = dims
    owners = tiles * cols_n * subs_n
    entries, cols = green.shape
    rows = depth.shape[0]
    crows, ccols = coarse_depth.shape
    capacity = max(2, (2 * entries + owners - 1) // owners)
    capp = (capacity + 15) // 16 * 16
    packs = owners // (128 // capp)
    hw = cols // planes
    i32 = lambda *shape: pltpu.VMEM(shape, jnp.int32)
    ways = 3 if tiles * (rows // RATIO) // crows > 1 else 1
    fw, cw = cols + 128, ccols + 128
    high, chigh = rows + 32, crows + 32
    vmem = lambda *shape: pltpu.VMEM(shape, F32)
    dma = pltpu.SemaphoreType.DMA
    keep = lambda x: pltpu.with_memory_space_constraint(x, pltpu.HBM)
    results = pl.pallas_call(
        functools.partial(kernel, dims),
        out_shape=(
            jax.ShapeDtypeStruct((rows, cols), F32),
            jax.ShapeDtypeStruct((rows, cols), F32),
            jax.ShapeDtypeStruct((crows, ccols), F32),
        ),
        in_specs=[pl.BlockSpec(memory_space=pltpu.HBM)] * 9,
        out_specs=(pl.BlockSpec(memory_space=pltpu.VMEM),) * 3,
        scratch_shapes=[
            pltpu.VMEM((entries, hw), BF16), i32(1, entries), i32(1, entries), i32(1, entries),
            vmem(1, slip.shape[0]), vmem(rows, cols), i32(rows, cols),
            pltpu.VMEM((owners * capp, entries), BF16), vmem(owners, entries),
            pltpu.VMEM((2, owners, capp, 128), BF16),
            pltpu.VMEM((2, owners, capp, 128), BF16),
            vmem(owners, 1, 128), vmem(owners, 1, 128),
            vmem(8, 128), vmem(8, 128), vmem(4 * rows, 128),
            pltpu.VMEM((packs, 4 * rows, 128), BF16),
            vmem(rows + 8, cols + 512), vmem(2, rows + 8, 384), vmem(2, 8, cols + 256),
            vmem(2, 2, 8, 384),
            vmem(2, 2 * rows, 128), vmem(2, rows, 128), vmem(2, rows // 4, 128), vmem(2, rows // 4, 128), vmem(2, 2, 2, 8, 128),
            vmem(2, 2, 8, 128),
        ]
        + [vmem(high, fw)] * 6
        + [vmem(chigh, cw)] * 6
        + [
            pltpu.VMEM((fw, cw), BF16), pltpu.VMEM((cw, fw), BF16),
            vmem(cw // 128, rows, 128),
            vmem(rows, fw), vmem(2, rows // RATIO, cw), vmem(2, chigh, cw),
            vmem(STEPS, 8, fw), vmem(16, cw), vmem(16, cw),
            dma((12,)), dma((2,)), dma((2, packs)), dma((1,)), dma((packs,)), dma((2,)), dma((8,)), dma((6,)),
            dma((9,)), dma((3, ways)), pltpu.SemaphoreType.REGULAR((tiles + 1,)),
        ],
        compiler_params=pltpu.CompilerParams(
            collective_id=0, has_side_effects=True, vmem_limit_bytes=48 * 1024 * 1024
        ),
    )(
        keep(green), keep(row_owner.reshape(1, entries)), keep(row_index.reshape(1, entries)),
        keep(row_fault.reshape(1, entries)), keep(slip.reshape(1, -1)), keep(depth), keep(wet), keep(coarse_depth), keep(coarse_start),
    )
    return pl.pallas_call(
        store,
        out_shape=tuple(jax.ShapeDtypeStruct(x.shape, F32) for x in results),
        in_specs=[pl.BlockSpec(memory_space=pltpu.VMEM)] * 3,
        out_specs=(pl.BlockSpec(memory_space=pltpu.HBM),) * 3,
        scratch_shapes=[dma((3,))],
        compiler_params=pltpu.CompilerParams(vmem_limit_bytes=1024 * 1024),
    )(*results)


def solution(mesh):
    dims = tuple(mesh.shape[a] for a in ("scen", "tile", "col", "sub"))
    return jax.shard_map(
        functools.partial(shards, dims),
        mesh=mesh,
        in_specs=(
            P(("tile", "col", "sub"), None),
            P(("tile", "col", "sub"), None),
            P(("tile", "col", "sub")),
            P(("tile", "col", "sub")),
            P(("scen", "tile", "col", "sub")),
            P("tile", ("col", "sub")),
            P("tile", ("col", "sub")),
            P("tile", ("col", "sub")),
            P(("scen", "tile"), ("col", "sub")),
        ),
        out_specs=(
            P(("scen", "tile"), ("col", "sub")),
            P(("scen", "tile"), ("col", "sub")),
            P(("scen", "tile"), ("col", "sub")),
        ),
        check_vma=False,
    )
```

```python
import functools
import jax
import jax.numpy as jnp
from jax import lax
from jax.experimental import pallas as pl
from jax.experimental.pallas import tpu as pltpu
from jax.sharding import PartitionSpec as P

RATIO = 4
STEPS = 6
HALO = 8
LEAD = 16
F32 = jnp.float32
BF16 = jnp.bfloat16
MESH = pl.DeviceIdType.MESH


def split2(x):
    high = x.astype(BF16).astype(F32)
    return high, (x - high).astype(BF16).astype(F32)


def iota(shape, dim):
    return lax.broadcasted_iota(jnp.int32, shape, dim)


def kernel(
    dims,
    green_h, owner_h, index_h, fault_h, slip_h, depth_h, wet_h, cdep_h, cstart_h,
    peak_o, surf_o, coarse_o,
    green, owner, index, fault, slip, depth, wet, chosen_r,
    place, send, recv, msend, mrecv, slip_s, slip_r, acc, weights,
    zs, zside, zvert, zcorn,
    half, hcore, packed, hside, hvert, hcorn,
    lev, held, gc, gr, kc, kr,
    clev, cheld, cgc, cgr, ckc, ckr,
    amat, rmat, work, total, avgs, avgr, esum, edges, edger,
    i_s, a_ss, a_rs, m_ss, m_rs, sl_s, z_rs, h_ss, h_rs, v_rs, alive,
):
    planes, tiles, cols_n, subs_n = dims
    sides = cols_n * subs_n
    owners = tiles * sides
    plane = lax.axis_index("scen")
    tile = lax.axis_index("tile")
    side = lax.axis_index("col") * subs_n + lax.axis_index("sub")
    me = tile * sides + side
    rows, cols = depth.shape
    crows, ccols = cdep_h.shape
    entries, hw = green.shape
    capp = send.shape[2]
    pack = 128 // capp
    packs = owners // pack
    fw = cols + 128
    cw = ccols + 128
    top = LEAD + rows

    def dev(p, t, c):
        return {"scen": p, "tile": t, "col": c // subs_n, "sub": c % subs_n}

    def fetch(i):
        edge_lanes = pl.ds(pl.multiple_of(plane * (hw + 128), 128), 128)
        inner_lanes = pl.ds(pl.multiple_of(128 + plane * 128, 128), 128)
        far = 256 + cols
        src, dst = [
            (owner_h, owner), (green_h.at[:, edge_lanes], green.at[:, 0:128]), (index_h, index), (fault_h, fault),
            (slip_h, slip), (depth_h, depth), (wet_h, wet),
            (cdep_h, zs.at[0:rows, 0:ccols]), (cstart_h, zs.at[0:rows, 128 : 128 + ccols]),
            (cdep_h, zs.at[0:rows, far : far + ccols]),
            (cstart_h, zs.at[0:rows, far + 128 : far + 128 + ccols]),
            (green_h.at[:, inner_lanes], green.at[:, 128:256]),
        ][i]
        return pltpu.make_async_copy(src, dst, i_s.at[i])

    barrier = pltpu.get_barrier_semaphore()

    other = planes - 1 - plane

    def hail(sem):
        def start(i, carry):
            pl.semaphore_signal(
                sem, inc=1, device_id=dev(plane, i // sides, lax.rem(i, sides)), device_id_type=MESH
            )
            return carry

        return start

    def hail_other(sem):
        pl.semaphore_signal(sem, inc=1, device_id=dev(other, tile, side), device_id_type=MESH)

    lax.fori_loop(me + 1, owners, hail(barrier), 0)
    pl.when(plane == 0)(lambda: hail_other(barrier))
    for i in (4, 0, 1, 11, 2, 3, 5, 6, 7, 8, 9, 10):
        fetch(i).start()

    slip_copy = pltpu.make_async_remote_copy(
        src_ref=slip_s, dst_ref=slip_r, send_sem=sl_s.at[0], recv_sem=sl_s.at[1],
        device_id=dev(other, tile, side), device_id_type=MESH,
    )
    fetch(4).wait()
    slip_s[...] = jnp.zeros_like(slip_s)
    slip_s[0:1, 0 : slip.shape[1]] = slip[...]
    pl.when(me + plane > 0)(lambda: pl.semaphore_wait(barrier, me + plane))

    @pl.when(plane > 0)
    def _():
        hail_other(alive.at[tiles])
        slip_copy.start()

    lax.fori_loop(0, me, hail(alive.at[tile]), 0)

    fetch(0).wait()
    dest = owner[...]
    hit = iota((owners, entries), 0) == dest
    before = (iota((entries, entries), 0) < iota((entries, entries), 1)).astype(F32).astype(BF16)
    rank = jnp.dot(hit.astype(F32).astype(BF16), before, preferred_element_type=F32)
    place[...] = jnp.where(hit, rank, -1.0)
    group = min(owners, 512 // capp)
    groups = owners // group
    fetch(1).wait()
    fetch(11).wait()
    gh = green[...]
    slots = iota((group, capp, entries), 1).astype(F32)

    def select(g):
        rows_of = place[pl.ds(pl.multiple_of(g * group, group), group), :]
        chosen = jnp.where(rows_of[:, None, :] == slots, 1.0, 0.0)
        chosen = chosen.reshape(group * capp, entries).astype(BF16)
        chosen_r[pl.ds(g * group * capp, group * capp), :] = chosen
        return chosen

    def fill(g, carry):
        picked = jnp.dot(select(g), gh, preferred_element_type=F32).astype(BF16)
        for h in range(2):
            send[h, pl.ds(g * group, group)] = picked[:, h * 128 : (h + 1) * 128].reshape(group, capp, 128)
        return carry

    fill(0, 0) if groups == 1 else lax.fori_loop(0, groups, fill, 0)

    for i in (2, 3, 5, 6, 7, 8, 9, 10):
        fetch(i).wait()
    raw = depth[...]
    zs[0:rows, 256 : 256 + cols] = jnp.where(wet[...] > 0, raw, 0.0)
    zs[rows : rows + 8, 256 : 256 + cols] = jnp.broadcast_to(raw[0:1], (8, cols))
    for off in (0, 256 + cols):
        zs[rows : rows + 8, off : off + 256] = jnp.zeros((8, 256), F32)

    def pair_copy(src, dst, s_sem, r_sem, d):
        return pltpu.make_async_remote_copy(
            src_ref=src, dst_ref=dst, send_sem=s_sem, recv_sem=r_sem,
            device_id=dev(plane, d // sides, lax.rem(d, sides)), device_id_type=MESH,
        )

    def a2a(h, d):
        return pair_copy(send.at[h, d], recv.at[h, me], a_ss.at[h], a_rs.at[h, me // pack], d)

    def a2a_meta(d):
        return pair_copy(msend.at[d], mrecv.at[me], m_ss.at[0], m_rs.at[me // pack], d)

    def a2a_wait(h, g, n):
        got = recv.at[h, pl.ds(g * pack, n)]
        pair_copy(got, got, a_ss.at[h], a_rs.at[h, g], me).wait_recv()

    def meta_wait(g, n):
        got = mrecv.at[pl.ds(g * pack, n)]
        pair_copy(got, got, m_ss.at[0], m_rs.at[g], me).wait_recv()

    middle = tiles // 2
    low = tile < middle
    across = jnp.where(low, tiles - middle, middle)

    def launch_tile(t, start):
        first = t * sides

        def own(i, carry):
            start(first + lax.rem(side + i, sides)).start()
            return carry

        lax.fori_loop(jnp.where(t == tile, 1, 0), sides, own, 0)

    def launch_far(start):
        def far(i, carry):
            launch_tile(jnp.where(low, tiles - 1 - i, i), start)
            return carry

        lax.fori_loop(0, across, far, 0)

    def launch_near(start):
        def near(i, carry):
            t = jnp.where(low, i, middle + i)
            pl.when(t != tile)(lambda: launch_tile(t, start))
            return carry

        lax.fori_loop(0, tiles - across, near, 0)

    def launch_one(d, carry):
        a2a(0, d).start()
        return carry

    def launch_met(t, carry):
        pl.semaphore_wait(alive.at[t], sides)
        launch_tile(t, functools.partial(a2a, 0))
        return carry

    lax.fori_loop(0, me, launch_one, 0)
    @pl.when(plane == 0)
    def _():
        pl.semaphore_wait(alive.at[tiles], 1)
        slip_copy.start()

    pl.when(side < sides - 1)(lambda: pl.semaphore_wait(alive.at[tile], sides - 1 - side))
    lax.fori_loop(me + 1, (tile + 1) * sides, launch_one, 0)
    lax.fori_loop(tile + 1, tiles, launch_met, 0)

    moves = [(0, -1), (0, 1), (-1, 0), (1, 0), (-1, -1), (-1, 1), (1, -1), (1, 1)]

    def static_copy(i):
        dy, dx = moves[i]
        lanes = (
            slice(0, 512 - 128) if dx == -1
            else slice(cols + 128, cols + 512) if dx == 1 else slice(0, 256 + cols)
        )
        sel = slice(0, rows + 8) if dy == 0 else slice(0, 8) if dy == -1 else slice(rows - 8, rows)
        bi = 0 if dy == -1 else 1
        bj = 0 if dx == -1 else 1
        dst = zside.at[bj] if dy == 0 else zvert.at[bi] if dx == 0 else zcorn.at[bi, bj]
        return pltpu.make_async_remote_copy(
            src_ref=zs.at[sel, lanes], dst_ref=dst, send_sem=i_s.at[i], recv_sem=z_rs.at[i],
            device_id=dev(plane, tile + dy, side + dx), device_id_type=MESH,
        )

    def inside(dy, dx):
        ok = True
        for at, by, size in ((tile, dy, tiles), (side, dx, sides)):
            if by == -1:
                ok = jnp.logical_and(ok, at > 0)
            if by == 1:
                ok = jnp.logical_and(ok, at < size - 1)
        return ok

    slip_copy.wait_recv()

    mrow = iota((8, slip.shape[1]), 0)
    own_h, own_l = split2(slip[...])
    oth_h, oth_l = split2(slip_r[0:1, 0 : slip.shape[1]])
    parts = jnp.where(mrow == 1, own_h, 0.0)
    for i, part in ((2, own_l), (3, oth_h), (4, oth_l)):
        parts = jnp.where(mrow == i, part, parts)
    picks = (iota((slip.shape[1], entries), 0) == fault[...]).astype(F32).astype(BF16)
    meta = jnp.dot(parts.astype(BF16), picks, preferred_element_type=F32)
    meta = jnp.where(iota((8, entries), 0) == 0, index[...].astype(F32), meta).astype(BF16)

    lane_of = iota((1, 128), 1)
    within = [(lane_of >= i * capp) & (lane_of < (i + 1) * capp) for i in range(pack)]

    def shifted(x, by):
        by = by % pack
        return pltpu.roll(x, by * capp, 1) if by else x

    def describe(g, carry):
        told = lax.dot_general(
            meta, chosen_r[pl.ds(g * group * capp, group * capp), :], (((1,), (1,)), ((), ())), preferred_element_type=F32
        )
        quantities = [told[0:1], told[1:2] + told[2:3], told[3:4] + told[4:5]]
        for i in range(group // pack):
            parts_of = [q[:, i * 128 : (i + 1) * 128] for q in quantities]
            for j in range(pack):
                record = jnp.zeros((1, 128), F32)
                for q, part in enumerate(parts_of):
                    record = jnp.where(within[q], shifted(part, q - j), record)
                msend[g * group + i * pack + j] = record
        return carry

    describe(0, 0) if groups == 1 else lax.fori_loop(0, groups, describe, 0)

    inner = functools.partial(a2a, 1)
    launch_far(a2a_meta)
    launch_tile(tile, a2a_meta)
    launch_far(inner)
    launch_near(a2a_meta)
    launch_tile(tile, inner)
    launch_near(inner)

    fl = iota((fw, cw), 0)
    fmap = jnp.where(fl < cols + 64, fl // RATIO, fl // RATIO + (cw - fw // RATIO))
    amat[...] = jnp.where(fmap == iota((fw, cw), 1), 1.0 / (RATIO * RATIO), 0.0).astype(BF16)
    rl = iota((cw, fw), 1)
    rmap = jnp.where(rl < cols + 64, rl // RATIO, rl // RATIO + (cw - fw // RATIO))
    rmat[...] = jnp.where(rmap == iota((cw, fw), 0), 1.0, 0.0).astype(BF16)
    for ref in (lev, held, gc, gr, clev, cheld, cgc, cgr):
        ref[...] = jnp.zeros_like(ref)

    for bj in range(2):
        dx = 1 if bj == 0 else -1
        @pl.when(jnp.logical_not(inside(0, dx)))
        def _(bj=bj):
            zside[bj] = jnp.zeros(zside.shape[1:], F32)
        for bi in range(2):
            dy = 1 if bi == 0 else -1
            @pl.when(jnp.logical_not(inside(dy, dx)))
            def _(bi=bi, bj=bj):
                zcorn[bi, bj] = jnp.zeros(zcorn.shape[2:], F32)
    for bi in range(2):
        dy = 1 if bi == 0 else -1
        @pl.when(jnp.logical_not(inside(dy, 0)))
        def _(bi=bi):
            zvert[bi] = jnp.zeros(zvert.shape[1:], F32)
    wrow = iota((4 * rows, 128), 0)
    in_tile = lax.rem(wrow, rows).astype(F32)
    recv[0, me] = send[0, me]
    recv[1, me] = send[1, me]
    mrecv[me] = msend[me]

    def product(h, g, weight):
        block = recv[h, pl.ds(g * pack, pack)].reshape(128, 128)
        return jnp.dot(weight, block, preferred_element_type=F32)

    def put(g):
        told = [jnp.zeros((1, 128), F32)] * 3
        for j in range(pack):
            record = mrecv[g * pack + j]
            told = [jnp.where(within[j], shifted(record, j - q), t) for q, t in enumerate(told)]
        (own_h, own_l), (oth_h, oth_l) = split2(told[1]), split2(told[2])
        weight = jnp.where(
            wrow < rows, own_h,
            jnp.where(wrow < 2 * rows, oth_h, jnp.where(wrow < 3 * rows, own_l, oth_l)),
        )
        weight = jnp.where(in_tile == told[0], weight, 0.0).astype(BF16)
        weights[g] = weight
        return product(0, g, weight)

    mine = me // pack

    def take(i, carry):
        g = lax.rem(mine + i, packs)
        a2a_wait(0, g, pack)
        meta_wait(g, pack)
        acc[...] += put(g)
        return carry

    def fold():
        return acc[0 : 2 * rows, :] + acc[2 * rows : 4 * rows, :]

    a2a_wait(0, mine, pack - 1)
    meta_wait(mine, pack - 1)
    acc[...] = put(mine)
    lax.fori_loop(1, packs - 1, take, 0, unroll=packs == 4)
    for i, (dy, dx) in enumerate(moves):
        pl.when(inside(dy, dx))(lambda i=i: static_copy(i).start())

    take(packs - 1, 0)
    half[0] = fold()

    toward = 2 * plane - 1

    def core_copy(h):
        return pltpu.make_async_remote_copy(
            src_ref=half.at[h, rows : 2 * rows, :], dst_ref=hcore.at[h], send_sem=h_ss.at[5],
            recv_sem=h_rs.at[8], device_id=dev(other, tile, side), device_id_type=MESH,
        )

    def halo_copy(h, s, kind, v, q):
        to_plane = plane if s == 0 else other
        dy = 0 if kind == 0 else (-1 if v == 0 else 1)
        r0 = s * rows + (0 if v == 0 else rows - 8)
        if kind == 0:
            src, dst, n, m = packed.at[s], hside.at[q], 2, 2 + q
        elif kind == 1:
            src, dst, n, m = half.at[h, r0 : r0 + 8, :], hvert.at[v, q, h], v, v
        else:
            src, dst, n, m = half.at[h, r0 : r0 + 8, :], hcorn.at[v, q], 3 + v, 4 + 2 * v + q
        return pltpu.make_async_remote_copy(
            src_ref=src, dst_ref=dst, send_sem=h_ss.at[n], recv_sem=h_rs.at[m],
            device_id=dev(to_plane, tile + dy, side if kind == 1 else side + toward),
            device_id_type=MESH,
        )

    kinds = [(0, 1, 0), (0, 1, 1), (0, 0, 0), (0, 2, 0), (0, 2, 1), (1, 1, 0), (1, 1, 1)]

    def goes(kind, v, sign):
        dy = 0 if kind == 0 else (-1 if v == 0 else 1) * sign
        ok = inside(dy, 0)
        if kind != 1:
            to = side + toward
            ok = jnp.logical_and(ok, jnp.logical_and(to >= 0, to < sides))
        return ok

    quarter = rows // 4
    qlane = iota((quarter, 128), 1)

    def turn_lanes(x, by):
        by = by % 128
        return pltpu.roll(x, by, 1) if by else x

    def send_half(half_of):
        core_copy(half_of).start()
        if half_of == 0:
            for s in range(2):
                strip = jnp.zeros((quarter, 128), F32)
                for j in range(4):
                    r0 = s * rows + j * quarter
                    x = half[0, r0 : r0 + quarter, :]
                    moved = jnp.where(plane == 0, turn_lanes(x, 32 * j), turn_lanes(x, 32 * j + 32))
                    strip = jnp.where(qlane // 32 == j, moved, strip)
                packed[s] = strip
        for s in (1, 0):
            for h, kind, v in kinds:
                if h == half_of:
                    pl.when(goes(kind, v, 1))(
                        lambda s=s, h=h, kind=kind, v=v: halo_copy(h, s, kind, v, plane).start()
                    )

    send_half(0)

    def take_inner(i, carry):
        g = lax.rem(mine + i, packs)
        a2a_wait(1, g, pack)
        acc[...] += product(1, g, weights[g])
        return carry

    a2a_wait(1, mine, pack - 1)
    acc[...] = product(1, mine, weights[mine])
    lax.fori_loop(1, packs, take_inner, 0, unroll=packs == 4)
    half[1] = fold()
    send_half(1)

    def lanes_of(p, h):
        return p * (hw + 128) if h == 0 else 128 + p * 128

    for h in range(2):
        lev[LEAD:top, pl.ds(pl.multiple_of(lanes_of(plane, h), 128), 128)] = half[h, 0:rows, :]

    def comes(kind, v, q):
        dy = 0 if kind == 0 else (1 if v == 0 else -1)
        dx = 0 if kind == 1 else (1 if q == 0 else -1)
        return inside(dy, dx)

    for i, (dy, dx) in enumerate(moves):
        pl.when(inside(-dy, -dx))(lambda i=i: static_copy(i).wait_recv())

    def merge(right, left):
        return jnp.where(iota(right.shape, right.ndim - 1) < 64, right, left)

    def place_static(r0, n, z, zr, zl, sr):
        held[r0 : r0 + n, 0:cols] = z[sr, 256 : 256 + cols]
        held[r0 : r0 + n, cols:fw] = merge(zr[sr, 256:384], zl[sr, 0:128])
        cheld[r0 : r0 + n, 0:ccols] = z[sr, 0:128]
        cheld[r0 : r0 + n, ccols:cw] = merge(zr[sr, 0:128], zl[sr, 128:256])
        clev[r0 : r0 + n, 0:ccols] = z[sr, 128:256]
        clev[r0 : r0 + n, ccols:cw] = merge(zr[sr, 128:256], zl[sr, 256:384])

    place_static(LEAD, rows, zs, zside.at[0], zside.at[1], slice(0, rows))
    place_static(top, 8, zvert.at[0], zcorn.at[0, 0], zcorn.at[0, 1], slice(0, 8))
    place_static(8, 8, zvert.at[1], zcorn.at[1, 0], zcorn.at[1, 1], slice(0, 8))

    @pl.when(tile == 0)
    def _():
        held[LEAD - 1 : LEAD, 0:cols] = depth[0:1, :]
        held[LEAD - 1 : LEAD, cols:fw] = merge(
            zside[0, rows : rows + 1, 256:384], zside[1, rows : rows + 1, 0:128]
        )

    strips = [8 + 8 * i for i in range((rows + 16) // 8)]
    cstrips = [8 + 8 * i for i in range((crows + 16) // 8)]

    def faces(h, k_c, k_r, scale, which):
        width = h.shape[1]
        for b in which:
            here, up = h[b : b + 8, :], h[b - 1 : b + 7, :]
            west = pltpu.roll(here, 1, 1)
            k_c[b : b + 8, :] = jnp.where((here > 0.0) & (west > 0.0), scale * (here + west), 0.0)
            k_r[b : b + 8, :] = jnp.where((here > 0.0) & (up > 0.0), scale * (here + up), 0.0)

    faces(held, kc, kr, 0.5 * 0.5 * 0.5, strips)
    faces(cheld, ckc, ckr, 0.5 * 0.125 * 0.125, cstrips)

    def stack3(values):
        rows_of = iota((16, values[0].shape[1]), 0)
        out = jnp.zeros(rows_of.shape, F32)
        for i, v in enumerate(values):
            first, rest = split2(v)
            second, third = split2(v - first)
            for j, part in enumerate((first, second, third)):
                out = jnp.where(rows_of == 3 * i + j, part, out)
        return out.astype(BF16)

    def join3(wide, i):
        return wide[3 * i : 3 * i + 1] + wide[3 * i + 1 : 3 * i + 2] + wide[3 * i + 2 : 3 * i + 3]

    wide = jnp.dot(
        stack3([clev[LEAD : LEAD + 1, :], ckc[LEAD : LEAD + 1, :], ckr[LEAD + 1 : LEAD + 2, :]]),
        rmat[...], preferred_element_type=F32,
    )
    kc0, kr1 = join3(wide, 1), join3(wide, 2)
    def landed(dst, n, m):
        return pltpu.make_async_remote_copy(
            src_ref=dst, dst_ref=dst, send_sem=h_ss.at[n], recv_sem=h_rs.at[m],
            device_id=dev(other, tile, side), device_id_type=MESH,
        )

    arrivals = [(1, v, 0, hvert.at[v], v) for v in range(2)]
    for q in range(2):
        arrivals.append((0, 0, q, hside.at[q], 2 + q))
        arrivals += [(2, v, q, hcorn.at[v, q], 4 + 2 * v + q) for v in range(2)]
    for kind, v, q, dst, m in arrivals:
        @pl.when(jnp.logical_not(comes(kind, v, q)))
        def _(dst=dst):
            dst[...] = jnp.zeros(dst.shape, F32)
        pl.when(comes(kind, v, q))(lambda dst=dst, m=m: landed(dst, 5, m).wait_recv())
    landed(hcore, 5, 8).wait_recv()

    for i, (dy, dx) in enumerate(moves):
        pl.when(inside(dy, dx))(lambda i=i: static_copy(i).wait_send())

    for h in range(2):
        lev[LEAD:top, pl.ds(pl.multiple_of(lanes_of(other, h), 128), 128)] = hcore[h]
    for j in range(4):
        right, left = turn_lanes(hside[0], -32 * j), turn_lanes(hside[1], 96 - 32 * j)
        lev[LEAD + j * quarter : LEAD + (j + 1) * quarter, cols:fw] = jnp.where(
            qlane < 32, right, jnp.where(qlane >= 96, left, 0.0)
        )
    for v, r0 in ((0, top), (1, 8)):
        for q in range(2):
            for h in range(2):
                lev[r0 : r0 + 8, lanes_of(q, h) : lanes_of(q, h) + 128] = hvert[v, q, h]
        lev[r0 : r0 + 8, cols:fw] = merge(hcorn[v, 0], hcorn[v, 1])

    brows = rows // RATIO
    per = crows * RATIO // rows
    nest = brows * tiles
    nested = nest // crows
    ct = tile // per
    cm = lax.rem(tile, per)

    def avg_copy(k, kind):
        if kind == 0:
            src, to = avgs.at[k], ct
            dst = avgr.at[k, pl.ds(pl.multiple_of(LEAD + cm * brows, 8), brows), :]
        elif kind == 1:
            src, to = avgs.at[k, brows - 8 : brows, :], ct + 1
            dst = avgr.at[k, 8:16, :]
        else:
            src, to = avgs.at[k, 0:8, :], ct - 1
            dst = avgr.at[k, LEAD + crows : LEAD + crows + 8, :]
        return pltpu.make_async_remote_copy(
            src_ref=src, dst_ref=dst, send_sem=i_s.at[8 + k if kind == 0 else 2 * kind + k], recv_sem=v_rs.at[k, kind],
            device_id=dev(plane, to, side), device_id_type=MESH,
        )

    def avg_goes(kind):
        if kind == 0:
            return tile > 0
        if kind == 1:
            return jnp.logical_and(cm == per - 1, ct + 1 < nested)
        return jnp.logical_and(cm == 0, ct > 0)

    ways = v_rs.shape[1]

    def avg_send(k):
        for kind in range(ways):
            pl.when(avg_goes(kind))(lambda kind=kind: avg_copy(k, kind).start())

    def avg_wait(k):
        def wait(kind, dst):
            pltpu.make_async_remote_copy(
                src_ref=dst, dst_ref=dst, send_sem=i_s.at[8], recv_sem=v_rs.at[k, kind],
                device_id=dev(plane, tile, side), device_id_type=MESH,
            ).wait_recv()

        pl.when(tile == 0)(lambda: wait(0, avgr.at[k, LEAD + brows : LEAD + per * brows, :]))
        pl.when(tile > 0)(lambda: wait(0, avgr.at[k, LEAD : LEAD + per * brows, :]))
        if ways == 1:
            return
        pl.when(tile > 0)(lambda: wait(1, avgr.at[k, 8:16, :]))
        pl.when(tile < nested - 1)(lambda: wait(2, avgr.at[k, LEAD + crows : LEAD + crows + 8, :]))

    def edge_copy():
        return pltpu.make_async_remote_copy(
            src_ref=edges, dst_ref=edger, send_sem=i_s.at[10], recv_sem=v_rs.at[2, 0],
            device_id=dev(plane, nested, side), device_id_type=MESH,
        )

    ends = nested < tiles
    is_last = tile == tiles - 1

    def push(s_ref, g_c, g_r, k_c, k_r, which):
        for b in which:
            here, up = s_ref[b : b + 8, :], s_ref[b - 1 : b + 7, :]
            g_c[b : b + 8, :] -= k_c[b : b + 8, :] * (here - pltpu.roll(here, 1, 1))
            g_r[b : b + 8, :] -= k_r[b : b + 8, :] * (here - up)

    def spread(g_c, g_r, b):
        east = g_c[b : b + 8, :]
        return (pltpu.roll(east, east.shape[1] - 1, 1) - east) + (
            g_r[b + 1 : b + 9, :] - g_r[b : b + 8, :]
        )

    def means(x):
        parts = jnp.concatenate(split2(x), axis=0).astype(BF16)
        sums = jnp.dot(parts, amat[...], preferred_element_type=F32)
        return sums[0 : x.shape[0]] + sums[x.shape[0] :]

    def block_means(k, sums):
        for j in range(cw // 128):
            work[j] = sums[:, j * 128 : (j + 1) * 128]
            avgs[k, :, j * 128 : (j + 1) * 128] = sum(
                work[j, pl.ds(i, brows, stride=RATIO), :] for i in range(RATIO)
            )
        avg_send(k)

        @pl.when(tile == 0)
        def _():
            avgr[k, LEAD : LEAD + brows, :] = avgs[k]

    lane = iota((1, fw), 1)
    odd, upper = lane % 2 == 1, lane % 4 >= 2

    def lane_means(x):
        x = x + jnp.where(odd, pltpu.roll(x, 1, 1), pltpu.roll(x, fw - 1, 1))
        x = x + jnp.where(upper, pltpu.roll(x, 2, 1), pltpu.roll(x, fw - 2, 1))
        return x * (1.0 / (RATIO * RATIO))

    erow = iota((16, fw), 0)

    def step(k, carry, keep=False):
        c0, g0, h1 = carry

        lev[LEAD - 1 : LEAD, :] = jnp.where(tile == 0, c0, lev[LEAD - 1 : LEAD, :])
        if ends:
            esum[k] = lev[top - 8 : top, :]
        mean = lane_means(jnp.sum(lev[LEAD : LEAD + RATIO, :], axis=0, keepdims=True))
        g0 = g0 - kc0 * (c0 - pltpu.roll(c0, RATIO, 1))
        h1 = h1 - kr1 * (mean - c0)
        c0 = c0 - ((pltpu.roll(g0, fw - RATIO, 1) - g0) + h1)
        push(lev, gc, gr, kc, kr, strips)
        for b in strips:
            old = lev[b : b + 8, :]
            new = old - spread(gc, gr, b)
            lev[b : b + 8, :] = new
            if LEAD <= b < top:
                r = slice(b - LEAD, b - LEAD + 8)
                if keep:
                    first = k == 0
                    peak_o[r, :] = jnp.maximum(
                        jnp.where(first, old[:, 0:cols], peak_o[r, :]), new[:, 0:cols]
                    )
                    total[r, :] = jnp.where(first, old, total[r, :]) + new
                else:
                    peak_o[r, :] = jnp.maximum(peak_o[r, :], new[:, 0:cols])
        return c0, g0, h1

    zero = jnp.zeros((1, fw), F32)
    carry = lax.fori_loop(
        0, STEPS - 2, functools.partial(step, keep=True), (join3(wide, 0), zero, zero), unroll=True
    )
    sums = means(total[...])
    carry = step(STEPS - 2, carry)
    block_means(0, sums)
    block_means(1, means(lev[LEAD:top, :]))
    carry = step(STEPS - 1, carry)
    if ends:
        @pl.when(is_last)
        def _():
            sums = jnp.zeros(erow.shape, F32)
            for k in range(STEPS):
                above = jnp.sum(esum[k, 0:4, :], axis=0, keepdims=True)
                below = jnp.sum(esum[k, 4:8, :], axis=0, keepdims=True)
                sums = jnp.where(erow == 2 * k, above, jnp.where(erow == 2 * k + 1, below, sums))
            edges[...] = means(sums)
            edge_copy().start()
    surf_o[...] = lev[LEAD:top, 0:cols]

    @pl.when(tile >= nested)
    def _():
        if ends:
            pl.when(tile == nested)(lambda: edge_copy().wait_recv())
        erows = iota((16, cw), 0)
        crow = iota((8, cw), 0)

        def cstep(k, carry):
            def edge(i):
                return jnp.sum(jnp.where(erows == 2 * k + i, edger[...], 0.0), axis=0, keepdims=True)

            @pl.when(tile == nested)
            def _():
                clev[LEAD - 8 : LEAD, :] = jnp.where(crow == 7, edge(0), clev[LEAD - 8 : LEAD, :])
                clev[LEAD : LEAD + 8, :] = jnp.where(crow == 0, edge(1), clev[LEAD : LEAD + 8, :])

            push(clev, cgc, cgr, ckc, ckr, cstrips)
            for b in cstrips:
                clev[b : b + 8, :] -= spread(cgc, cgr, b)
            return carry

        lax.fori_loop(0, STEPS, cstep, 0)
        coarse_o[...] = clev[LEAD : LEAD + crows, 0:ccols]

    @pl.when(tile < nested)
    def _():
        c0, g0, h1 = carry
        narrow = RATIO * jnp.dot(stack3([c0, h1]), amat[...], preferred_element_type=F32)
        avg_wait(0)
        avg_wait(1)
        for b in range(LEAD, LEAD + crows + 8, 8):
            clev[b : b + 8, :] = avgr[0, b - 1 : b + 7, :] + avgr[1, b - 1 : b + 7, :]
        clev[LEAD - 1 : LEAD, :] = avgr[0, LEAD - 2 : LEAD - 1, :] + avgr[1, LEAD - 2 : LEAD - 1, :]
        inner = range(LEAD, LEAD + crows + 8, 8)
        push(clev, cgc, cgr, ckc, ckr, inner)

        @pl.when(tile == 0)
        def _():
            cgr[LEAD + 1 : LEAD + 2, :] = join3(narrow, 1)

        for b in range(LEAD, LEAD + crows, 8):
            new = avgr[1, b - 1 : b + 7, :] - spread(cgc, cgr, b)
            coarse_o[b - LEAD : b - LEAD + 8, :] = new[:, 0:ccols]

        @pl.when(tile == 0)
        def _():
            coarse_o[0:1, :] = join3(narrow, 0)[:, 0:ccols]

    slip_copy.wait_send()
    rest = pl.ds(0, owners - 1)
    for h in range(2):
        pair_copy(send.at[h, rest], recv.at[h, rest], a_ss.at[h], a_rs.at[h, 0], me).wait_send()
    pair_copy(mrecv.at[rest], mrecv.at[rest], m_ss.at[0], m_rs.at[0], me).wait_send()
    landed(hcore, 5, 8).wait_send()
    for kind, v, dst, n in [(1, 0, hvert.at[0], 0), (1, 1, hvert.at[1], 1), (0, 0, hside, 2)] + [
        (2, v, hcorn.at[v], 3 + v) for v in range(2)
    ]:
        pl.when(goes(kind, v, 1))(lambda dst=dst, n=n: landed(dst, n, 8).wait_send())
    for k in range(2):
        for kind in range(ways):
            pl.when(avg_goes(kind))(lambda k=k, kind=kind: avg_copy(k, kind).wait_send())
    if ends:
        pl.when(is_last)(lambda: edge_copy().wait_send())


def store(peak, surf, coarse, peak_h, surf_h, coarse_h, sems):
    pairs = [(peak, peak_h), (surf, surf_h), (coarse, coarse_h)]
    copies = [pltpu.make_async_copy(src, dst, sems.at[i]) for i, (src, dst) in enumerate(pairs)]
    for copy in copies:
        copy.start()
    for copy in copies:
        copy.wait()


def shards(dims, green, row_owner, row_index, row_fault, slip, depth, wet, coarse_depth, coarse_start):
    planes, tiles, cols_n, subs_n = dims
    owners = tiles * cols_n * subs_n
    entries, cols = green.shape
    rows = depth.shape[0]
    crows, ccols = coarse_depth.shape
    capacity = max(2, (2 * entries + owners - 1) // owners)
    capp = (capacity + 15) // 16 * 16
    packs = owners // (128 // capp)
    hw = cols // planes
    i32 = lambda *shape: pltpu.VMEM(shape, jnp.int32)
    ways = 3 if tiles * (rows // RATIO) // crows > 1 else 1
    fw, cw = cols + 128, ccols + 128
    high, chigh = rows + 32, crows + 32
    vmem = lambda *shape: pltpu.VMEM(shape, F32)
    dma = pltpu.SemaphoreType.DMA
    keep = lambda x: pltpu.with_memory_space_constraint(x, pltpu.HBM)
    results = pl.pallas_call(
        functools.partial(kernel, dims),
        out_shape=(
            jax.ShapeDtypeStruct((rows, cols), F32),
            jax.ShapeDtypeStruct((rows, cols), F32),
            jax.ShapeDtypeStruct((crows, ccols), F32),
        ),
        in_specs=[pl.BlockSpec(memory_space=pltpu.HBM)] * 9,
        out_specs=(pl.BlockSpec(memory_space=pltpu.VMEM),) * 3,
        scratch_shapes=[
            pltpu.VMEM((entries, hw), BF16), i32(1, entries), i32(1, entries), i32(1, entries),
            vmem(1, slip.shape[0]), vmem(rows, cols), i32(rows, cols),
            pltpu.VMEM((owners * capp, entries), BF16), vmem(owners, entries),
            pltpu.VMEM((2, owners, capp, 128), BF16),
            pltpu.VMEM((2, owners, capp, 128), BF16),
            vmem(owners, 1, 128), vmem(owners, 1, 128),
            vmem(8, 128), vmem(8, 128), vmem(4 * rows, 128),
            pltpu.VMEM((packs, 4 * rows, 128), BF16),
            vmem(rows + 8, cols + 512), vmem(2, rows + 8, 384), vmem(2, 8, cols + 256),
            vmem(2, 2, 8, 384),
            vmem(2, 2 * rows, 128), vmem(2, rows, 128), vmem(2, rows // 4, 128), vmem(2, rows // 4, 128), vmem(2, 2, 2, 8, 128),
            vmem(2, 2, 8, 128),
        ]
        + [vmem(high, fw)] * 6
        + [vmem(chigh, cw)] * 6
        + [
            pltpu.VMEM((fw, cw), BF16), pltpu.VMEM((cw, fw), BF16),
            vmem(cw // 128, rows, 128),
            vmem(rows, fw), vmem(2, rows // RATIO, cw), vmem(2, chigh, cw),
            vmem(STEPS, 8, fw), vmem(16, cw), vmem(16, cw),
            dma((12,)), dma((2,)), dma((2, packs)), dma((1,)), dma((packs,)), dma((2,)), dma((8,)), dma((6,)),
            dma((9,)), dma((3, ways)), pltpu.SemaphoreType.REGULAR((tiles + 1,)),
        ],
        compiler_params=pltpu.CompilerParams(
            collective_id=0, has_side_effects=True, vmem_limit_bytes=48 * 1024 * 1024
        ),
    )(
        keep(green), keep(row_owner.reshape(1, entries)), keep(row_index.reshape(1, entries)),
        keep(row_fault.reshape(1, entries)), keep(slip.reshape(1, -1)), keep(depth), keep(wet), keep(coarse_depth), keep(coarse_start),
    )
    return pl.pallas_call(
        store,
        out_shape=tuple(jax.ShapeDtypeStruct(x.shape, F32) for x in results),
        in_specs=[pl.BlockSpec(memory_space=pltpu.VMEM)] * 3,
        out_specs=(pl.BlockSpec(memory_space=pltpu.HBM),) * 3,
        scratch_shapes=[dma((3,))],
        compiler_params=pltpu.CompilerParams(vmem_limit_bytes=1024 * 1024),
    )(*results)


def solution(mesh):
    dims = tuple(mesh.shape[a] for a in ("scen", "tile", "col", "sub"))
    return jax.shard_map(
        functools.partial(shards, dims),
        mesh=mesh,
        in_specs=(
            P(("tile", "col", "sub"), None),
            P(("tile", "col", "sub"), None),
            P(("tile", "col", "sub")),
            P(("tile", "col", "sub")),
            P(("scen", "tile", "col", "sub")),
            P("tile", ("col", "sub")),
            P("tile", ("col", "sub")),
            P("tile", ("col", "sub")),
            P(("scen", "tile"), ("col", "sub")),
        ),
        out_specs=(
            P(("scen", "tile"), ("col", "sub")),
            P(("scen", "tile"), ("col", "sub")),
            P(("scen", "tile"), ("col", "sub")),
        ),
        check_vma=False,
    )
```

```python
import functools
import jax
import jax.numpy as jnp
from jax import lax
from jax.experimental import pallas as pl
from jax.experimental.pallas import tpu as pltpu
from jax.sharding import PartitionSpec as P

RATIO = 4
STEPS = 6
HALO = 8
LEAD = 16
F32 = jnp.float32
BF16 = jnp.bfloat16
MESH = pl.DeviceIdType.MESH


def split2(x):
    high = x.astype(BF16).astype(F32)
    return high, (x - high).astype(BF16).astype(F32)


def iota(shape, dim):
    return lax.broadcasted_iota(jnp.int32, shape, dim)


def kernel(
    dims,
    green_h, owner_h, index_h, fault_h, slip_h, depth_h, wet_h, cdep_h, cstart_h,
    peak_o, surf_o, coarse_o,
    green, owner, index, fault, slip, depth, wet, chosen_r,
    place, send, recv, msend, mrecv, slip_s, slip_r, acc, weights,
    zs, zedge, zside, zvert, zcorn,
    half, hcore, packed, hside, hvert, hcorn,
    lev, held, gc, gr, kc, kr,
    clev, cheld, cgc, cgr, ckc, ckr,
    amat, rmat, work, total, avgs, avgr, esum, edges, edger,
    i_s, a_ss, a_rs, m_ss, m_rs, sl_s, z_rs, h_ss, h_rs, v_rs, alive,
):
    planes, tiles, cols_n, subs_n = dims
    sides = cols_n * subs_n
    owners = tiles * sides
    plane = lax.axis_index("scen")
    tile = lax.axis_index("tile")
    side = lax.axis_index("col") * subs_n + lax.axis_index("sub")
    me = tile * sides + side
    rows, cols = depth.shape
    crows, ccols = cdep_h.shape
    entries, hw = green.shape
    capp = send.shape[2]
    pack = 128 // capp
    packs = owners // pack
    fw = cols + 128
    cw = ccols + 128
    top = LEAD + rows

    def dev(p, t, c):
        return {"scen": p, "tile": t, "col": c // subs_n, "sub": c % subs_n}

    def turn_lanes(x, by):
        by = by % 128
        return pltpu.roll(x, by, 1) if by else x

    def thirds(parts):
        lanes = iota(parts[0].shape, 1)
        out = jnp.zeros(parts[0].shape, F32)
        for q, part in enumerate(parts):
            out = jnp.where(lanes // 32 == q, part, out)
        return out

    def both_sides(right, left, q):
        lanes = iota(right.shape, 1)
        left = jnp.where(lanes >= 96, turn_lanes(left, 96 - 32 * q), 0.0)
        return jnp.where(lanes < 32, turn_lanes(right, -32 * q), left)

    def fetch(i):
        edge_lanes = pl.ds(pl.multiple_of(plane * (hw + 128), 128), 128)
        inner_lanes = pl.ds(pl.multiple_of(128 + plane * 128, 128), 128)
        src, dst = [
            (owner_h, owner), (green_h.at[:, edge_lanes], green.at[:, 0:128]), (index_h, index), (fault_h, fault),
            (slip_h, slip), (depth_h, depth), (wet_h, wet),
            (cdep_h, zs.at[0:rows, 0:ccols]), (cstart_h, zs.at[0:rows, 128 : 128 + ccols]),
            (green_h.at[:, inner_lanes], green.at[:, 128:256]),
        ][i]
        return pltpu.make_async_copy(src, dst, i_s.at[i])

    barrier = pltpu.get_barrier_semaphore()

    other = planes - 1 - plane

    def hail(sem):
        def start(i, carry):
            pl.semaphore_signal(
                sem, inc=1, device_id=dev(plane, i // sides, lax.rem(i, sides)), device_id_type=MESH
            )
            return carry

        return start

    def hail_other(sem):
        pl.semaphore_signal(sem, inc=1, device_id=dev(other, tile, side), device_id_type=MESH)

    lax.fori_loop(me + 1, owners, hail(barrier), 0)
    pl.when(plane == 0)(lambda: hail_other(barrier))
    for i in (4, 0, 1, 9, 2, 3, 5, 6, 7, 8):
        fetch(i).start()

    slip_copy = pltpu.make_async_remote_copy(
        src_ref=slip_s, dst_ref=slip_r, send_sem=sl_s.at[0], recv_sem=sl_s.at[1],
        device_id=dev(other, tile, side), device_id_type=MESH,
    )
    fetch(4).wait()
    slip_s[...] = jnp.zeros_like(slip_s)
    slip_s[0:1, 0 : slip.shape[1]] = slip[...]
    pl.when(me + plane > 0)(lambda: pl.semaphore_wait(barrier, me + plane))

    @pl.when(plane > 0)
    def _():
        hail_other(alive.at[tiles])
        slip_copy.start()

    lax.fori_loop(0, me, hail(alive.at[tile]), 0)

    fetch(0).wait()
    dest = owner[...]
    hit = iota((owners, entries), 0) == dest
    before = (iota((entries, entries), 0) < iota((entries, entries), 1)).astype(F32).astype(BF16)
    rank = jnp.dot(hit.astype(F32).astype(BF16), before, preferred_element_type=F32)
    place[...] = jnp.where(hit, rank, -1.0)
    group = min(owners, 512 // capp)
    groups = owners // group
    fetch(1).wait()
    fetch(9).wait()
    gh = green[...]
    slots = iota((group, capp, entries), 1).astype(F32)

    def select(g):
        rows_of = place[pl.ds(pl.multiple_of(g * group, group), group), :]
        chosen = jnp.where(rows_of[:, None, :] == slots, 1.0, 0.0)
        chosen = chosen.reshape(group * capp, entries).astype(BF16)
        chosen_r[pl.ds(g * group * capp, group * capp), :] = chosen
        return chosen

    def fill(g, carry):
        picked = jnp.dot(select(g), gh, preferred_element_type=F32).astype(BF16)
        for h in range(2):
            send[h, pl.ds(g * group, group)] = picked[:, h * 128 : (h + 1) * 128].reshape(group, capp, 128)
        return carry

    fill(0, 0) if groups == 1 else lax.fori_loop(0, groups, fill, 0)

    for i in (2, 3, 5, 6, 7, 8):
        fetch(i).wait()
    raw = depth[...]
    zs[0:rows, 256 : 256 + cols] = jnp.where(wet[...] > 0, raw, 0.0)
    zs[rows : rows + 8, 256 : 256 + cols] = jnp.broadcast_to(raw[0:1], (8, cols))
    zs[rows : rows + 8, 0:256] = jnp.zeros((8, 256), F32)
    for bj, off, first in ((0, 0, 256), (1, 96, 128 + cols)):
        blocks_of = (zs[:, first : first + 128], zs[:, 0:128], zs[:, 128:256])
        zedge[bj] = thirds([turn_lanes(x, 32 * q - off) for q, x in enumerate(blocks_of)])

    def pair_copy(src, dst, s_sem, r_sem, d):
        return pltpu.make_async_remote_copy(
            src_ref=src, dst_ref=dst, send_sem=s_sem, recv_sem=r_sem,
            device_id=dev(plane, d // sides, lax.rem(d, sides)), device_id_type=MESH,
        )

    def a2a(h, d):
        return pair_copy(send.at[h, d], recv.at[h, me], a_ss.at[h], a_rs.at[h, me // pack], d)

    def a2a_meta(d):
        return pair_copy(msend.at[d], mrecv.at[me], m_ss.at[0], m_rs.at[me // pack], d)

    def a2a_wait(h, g, n):
        got = recv.at[h, pl.ds(g * pack, n)]
        pair_copy(got, got, a_ss.at[h], a_rs.at[h, g], me).wait_recv()

    def meta_wait(g, n):
        got = mrecv.at[pl.ds(g * pack, n)]
        pair_copy(got, got, m_ss.at[0], m_rs.at[g], me).wait_recv()

    middle = tiles // 2
    low = tile < middle
    across = jnp.where(low, tiles - middle, middle)

    def launch_tile(t, start):
        first = t * sides

        def own(i, carry):
            start(first + lax.rem(side + i, sides)).start()
            return carry

        lax.fori_loop(jnp.where(t == tile, 1, 0), sides, own, 0)

    def launch_far(start):
        def far(i, carry):
            launch_tile(jnp.where(low, tiles - 1 - i, i), start)
            return carry

        lax.fori_loop(0, across, far, 0)

    def launch_near(start):
        def near(i, carry):
            t = jnp.where(low, i, middle + i)
            pl.when(t != tile)(lambda: launch_tile(t, start))
            return carry

        lax.fori_loop(0, tiles - across, near, 0)

    def launch_one(d, carry):
        a2a(0, d).start()
        return carry

    def launch_met(t, carry):
        pl.semaphore_wait(alive.at[t], sides)
        launch_tile(t, functools.partial(a2a, 0))
        return carry

    lax.fori_loop(0, me, launch_one, 0)
    @pl.when(plane == 0)
    def _():
        pl.semaphore_wait(alive.at[tiles], 1)
        slip_copy.start()

    pl.when(side < sides - 1)(lambda: pl.semaphore_wait(alive.at[tile], sides - 1 - side))
    lax.fori_loop(me + 1, (tile + 1) * sides, launch_one, 0)
    lax.fori_loop(tile + 1, tiles, launch_met, 0)

    moves = [(0, -1), (0, 1), (-1, 0), (1, 0), (-1, -1), (-1, 1), (1, -1), (1, 1)]

    def static_copy(i):
        dy, dx = moves[i]
        sel = slice(0, rows + 8) if dy == 0 else slice(0, 8) if dy == -1 else slice(rows - 8, rows)
        bi = 0 if dy == -1 else 1
        bj = 0 if dx == -1 else 1
        dst = zside.at[bj] if dy == 0 else zvert.at[bi] if dx == 0 else zcorn.at[bi, bj]
        return pltpu.make_async_remote_copy(
            src_ref=zedge.at[bj, sel, :] if dx else zs.at[sel, :], dst_ref=dst, send_sem=i_s.at[i], recv_sem=z_rs.at[i],
            device_id=dev(plane, tile + dy, side + dx), device_id_type=MESH,
        )

    def inside(dy, dx):
        ok = True
        for at, by, size in ((tile, dy, tiles), (side, dx, sides)):
            if by == -1:
                ok = jnp.logical_and(ok, at > 0)
            if by == 1:
                ok = jnp.logical_and(ok, at < size - 1)
        return ok

    slip_copy.wait_recv()

    mrow = iota((8, slip.shape[1]), 0)
    own_h, own_l = split2(slip[...])
    oth_h, oth_l = split2(slip_r[0:1, 0 : slip.shape[1]])
    parts = jnp.where(mrow == 1, own_h, 0.0)
    for i, part in ((2, own_l), (3, oth_h), (4, oth_l)):
        parts = jnp.where(mrow == i, part, parts)
    picks = (iota((slip.shape[1], entries), 0) == fault[...]).astype(F32).astype(BF16)
    meta = jnp.dot(parts.astype(BF16), picks, preferred_element_type=F32)
    meta = jnp.where(iota((8, entries), 0) == 0, index[...].astype(F32), meta).astype(BF16)

    lane_of = iota((1, 128), 1)
    within = [(lane_of >= i * capp) & (lane_of < (i + 1) * capp) for i in range(pack)]

    def shifted(x, by):
        by = by % pack
        return pltpu.roll(x, by * capp, 1) if by else x

    def describe(g, carry):
        told = lax.dot_general(
            meta, chosen_r[pl.ds(g * group * capp, group * capp), :], (((1,), (1,)), ((), ())), preferred_element_type=F32
        )
        quantities = [told[0:1], told[1:2] + told[2:3], told[3:4] + told[4:5]]
        for i in range(group // pack):
            parts_of = [q[:, i * 128 : (i + 1) * 128] for q in quantities]
            for j in range(pack):
                record = jnp.zeros((1, 128), F32)
                for q, part in enumerate(parts_of):
                    record = jnp.where(within[q], shifted(part, q - j), record)
                msend[g * group + i * pack + j] = record
        return carry

    describe(0, 0) if groups == 1 else lax.fori_loop(0, groups, describe, 0)

    inner = functools.partial(a2a, 1)
    launch_far(a2a_meta)
    launch_tile(tile, a2a_meta)
    launch_far(inner)
    launch_near(a2a_meta)
    launch_tile(tile, inner)
    launch_near(inner)

    fl = iota((fw, cw), 0)
    fmap = jnp.where(fl < cols + 64, fl // RATIO, fl // RATIO + (cw - fw // RATIO))
    amat[...] = jnp.where(fmap == iota((fw, cw), 1), 1.0 / (RATIO * RATIO), 0.0).astype(BF16)
    rl = iota((cw, fw), 1)
    rmap = jnp.where(rl < cols + 64, rl // RATIO, rl // RATIO + (cw - fw // RATIO))
    rmat[...] = jnp.where(rmap == iota((cw, fw), 0), 1.0, 0.0).astype(BF16)
    for ref in (lev, held, gc, gr, clev, cheld, cgc, cgr):
        ref[...] = jnp.zeros_like(ref)

    for bj in range(2):
        dx = 1 if bj == 0 else -1
        @pl.when(jnp.logical_not(inside(0, dx)))
        def _(bj=bj):
            zside[bj] = jnp.zeros(zside.shape[1:], F32)
        for bi in range(2):
            dy = 1 if bi == 0 else -1
            @pl.when(jnp.logical_not(inside(dy, dx)))
            def _(bi=bi, bj=bj):
                zcorn[bi, bj] = jnp.zeros(zcorn.shape[2:], F32)
    for bi in range(2):
        dy = 1 if bi == 0 else -1
        @pl.when(jnp.logical_not(inside(dy, 0)))
        def _(bi=bi):
            zvert[bi] = jnp.zeros(zvert.shape[1:], F32)
    wrow = iota((4 * rows, 128), 0)
    in_tile = lax.rem(wrow, rows).astype(F32)
    recv[0, me] = send[0, me]
    recv[1, me] = send[1, me]
    mrecv[me] = msend[me]

    def product(h, g, weight):
        block = recv[h, pl.ds(g * pack, pack)].reshape(128, 128)
        return jnp.dot(weight, block, preferred_element_type=F32)

    def put(g):
        told = [jnp.zeros((1, 128), F32)] * 3
        for j in range(pack):
            record = mrecv[g * pack + j]
            told = [jnp.where(within[j], shifted(record, j - q), t) for q, t in enumerate(told)]
        (own_h, own_l), (oth_h, oth_l) = split2(told[1]), split2(told[2])
        weight = jnp.where(
            wrow < rows, own_h,
            jnp.where(wrow < 2 * rows, oth_h, jnp.where(wrow < 3 * rows, own_l, oth_l)),
        )
        weight = jnp.where(in_tile == told[0], weight, 0.0).astype(BF16)
        weights[g] = weight
        return product(0, g, weight)

    mine = me // pack

    def take(i, carry):
        g = lax.rem(mine + i, packs)
        a2a_wait(0, g, pack)
        meta_wait(g, pack)
        acc[...] += put(g)
        return carry

    def fold():
        return acc[0 : 2 * rows, :] + acc[2 * rows : 4 * rows, :]

    a2a_wait(0, mine, pack - 1)
    meta_wait(mine, pack - 1)
    acc[...] = put(mine)
    lax.fori_loop(1, packs - 1, take, 0, unroll=packs == 4)
    for i, (dy, dx) in enumerate(moves):
        pl.when(inside(dy, dx))(lambda i=i: static_copy(i).start())

    take(packs - 1, 0)
    half[0] = fold()

    toward = 2 * plane - 1

    def core_copy(h):
        return pltpu.make_async_remote_copy(
            src_ref=half.at[h, rows : 2 * rows, :], dst_ref=hcore.at[h], send_sem=h_ss.at[5],
            recv_sem=h_rs.at[8], device_id=dev(other, tile, side), device_id_type=MESH,
        )

    def halo_copy(h, s, kind, v, q):
        to_plane = plane if s == 0 else other
        dy = 0 if kind == 0 else (-1 if v == 0 else 1)
        r0 = s * rows + (0 if v == 0 else rows - 8)
        if kind == 0:
            src, dst, n, m = packed.at[s], hside.at[q], 2, 2 + q
        elif kind == 1:
            src, dst, n, m = half.at[h, r0 : r0 + 8, :], hvert.at[v, q, h], v, v
        else:
            src, dst, n, m = half.at[h, r0 : r0 + 8, :], hcorn.at[v, q], 3 + v, 4 + 2 * v + q
        return pltpu.make_async_remote_copy(
            src_ref=src, dst_ref=dst, send_sem=h_ss.at[n], recv_sem=h_rs.at[m],
            device_id=dev(to_plane, tile + dy, side if kind == 1 else side + toward),
            device_id_type=MESH,
        )

    kinds = [(0, 1, 0), (0, 1, 1), (0, 0, 0), (0, 2, 0), (0, 2, 1), (1, 1, 0), (1, 1, 1)]

    def goes(kind, v, sign):
        dy = 0 if kind == 0 else (-1 if v == 0 else 1) * sign
        ok = inside(dy, 0)
        if kind != 1:
            to = side + toward
            ok = jnp.logical_and(ok, jnp.logical_and(to >= 0, to < sides))
        return ok

    quarter = rows // 4
    qlane = iota((quarter, 128), 1)

    def send_half(half_of):
        core_copy(half_of).start()
        if half_of == 0:
            for s in range(2):
                strip = jnp.zeros((quarter, 128), F32)
                for j in range(4):
                    r0 = s * rows + j * quarter
                    x = half[0, r0 : r0 + quarter, :]
                    moved = jnp.where(plane == 0, turn_lanes(x, 32 * j), turn_lanes(x, 32 * j + 32))
                    strip = jnp.where(qlane // 32 == j, moved, strip)
                packed[s] = strip
        for s in (1, 0):
            for h, kind, v in kinds:
                if h == half_of:
                    pl.when(goes(kind, v, 1))(
                        lambda s=s, h=h, kind=kind, v=v: halo_copy(h, s, kind, v, plane).start()
                    )

    send_half(0)

    def take_inner(i, carry):
        g = lax.rem(mine + i, packs)
        a2a_wait(1, g, pack)
        acc[...] += product(1, g, weights[g])
        return carry

    a2a_wait(1, mine, pack - 1)
    acc[...] = product(1, mine, weights[mine])
    lax.fori_loop(1, packs, take_inner, 0, unroll=packs == 4)
    half[1] = fold()
    send_half(1)

    def lanes_of(p, h):
        return p * (hw + 128) if h == 0 else 128 + p * 128

    for h in range(2):
        lev[LEAD:top, pl.ds(pl.multiple_of(lanes_of(plane, h), 128), 128)] = half[h, 0:rows, :]

    def comes(kind, v, q):
        dy = 0 if kind == 0 else (1 if v == 0 else -1)
        dx = 0 if kind == 1 else (1 if q == 0 else -1)
        return inside(dy, dx)

    for i, (dy, dx) in enumerate(moves):
        pl.when(inside(-dy, -dx))(lambda i=i: static_copy(i).wait_recv())

    def merge(right, left):
        return jnp.where(iota(right.shape, right.ndim - 1) < 64, right, left)

    def place_static(r0, n, z, zr, zl, sr):
        right, left = zr[sr, :], zl[sr, :]
        held[r0 : r0 + n, 0:cols] = z[sr, 256 : 256 + cols]
        held[r0 : r0 + n, cols:fw] = both_sides(right, left, 0)
        cheld[r0 : r0 + n, 0:ccols] = z[sr, 0:128]
        cheld[r0 : r0 + n, ccols:cw] = both_sides(right, left, 1)
        clev[r0 : r0 + n, 0:ccols] = z[sr, 128:256]
        clev[r0 : r0 + n, ccols:cw] = both_sides(right, left, 2)

    place_static(LEAD, rows, zs, zside.at[0], zside.at[1], slice(0, rows))
    place_static(top, 8, zvert.at[0], zcorn.at[0, 0], zcorn.at[0, 1], slice(0, 8))
    place_static(8, 8, zvert.at[1], zcorn.at[1, 0], zcorn.at[1, 1], slice(0, 8))

    @pl.when(tile == 0)
    def _():
        held[LEAD - 1 : LEAD, 0:cols] = depth[0:1, :]
        held[LEAD - 1 : LEAD, cols:fw] = both_sides(
            zside[0, rows : rows + 1, :], zside[1, rows : rows + 1, :], 0
        )

    strips = [8 + 8 * i for i in range((rows + 16) // 8)]
    cstrips = [8 + 8 * i for i in range((crows + 16) // 8)]

    def faces(h, k_c, k_r, scale, which):
        width = h.shape[1]
        for b in which:
            here, up = h[b : b + 8, :], h[b - 1 : b + 7, :]
            west = pltpu.roll(here, 1, 1)
            k_c[b : b + 8, :] = jnp.where((here > 0.0) & (west > 0.0), scale * (here + west), 0.0)
            k_r[b : b + 8, :] = jnp.where((here > 0.0) & (up > 0.0), scale * (here + up), 0.0)

    faces(held, kc, kr, 0.5 * 0.5 * 0.5, strips)
    faces(cheld, ckc, ckr, 0.5 * 0.125 * 0.125, cstrips)

    def stack3(values):
        rows_of = iota((16, values[0].shape[1]), 0)
        out = jnp.zeros(rows_of.shape, F32)
        for i, v in enumerate(values):
            first, rest = split2(v)
            second, third = split2(v - first)
            for j, part in enumerate((first, second, third)):
                out = jnp.where(rows_of == 3 * i + j, part, out)
        return out.astype(BF16)

    def join3(wide, i):
        return wide[3 * i : 3 * i + 1] + wide[3 * i + 1 : 3 * i + 2] + wide[3 * i + 2 : 3 * i + 3]

    wide = jnp.dot(
        stack3([clev[LEAD : LEAD + 1, :], ckc[LEAD : LEAD + 1, :], ckr[LEAD + 1 : LEAD + 2, :]]),
        rmat[...], preferred_element_type=F32,
    )
    kc0, kr1 = join3(wide, 1), join3(wide, 2)
    def landed(dst, n, m):
        return pltpu.make_async_remote_copy(
            src_ref=dst, dst_ref=dst, send_sem=h_ss.at[n], recv_sem=h_rs.at[m],
            device_id=dev(other, tile, side), device_id_type=MESH,
        )

    arrivals = [(1, v, 0, hvert.at[v], v) for v in range(2)]
    for q in range(2):
        arrivals.append((0, 0, q, hside.at[q], 2 + q))
        arrivals += [(2, v, q, hcorn.at[v, q], 4 + 2 * v + q) for v in range(2)]
    for kind, v, q, dst, m in arrivals:
        @pl.when(jnp.logical_not(comes(kind, v, q)))
        def _(dst=dst):
            dst[...] = jnp.zeros(dst.shape, F32)
        pl.when(comes(kind, v, q))(lambda dst=dst, m=m: landed(dst, 5, m).wait_recv())
    landed(hcore, 5, 8).wait_recv()

    for i, (dy, dx) in enumerate(moves):
        pl.when(inside(dy, dx))(lambda i=i: static_copy(i).wait_send())

    for h in range(2):
        lev[LEAD:top, pl.ds(pl.multiple_of(lanes_of(other, h), 128), 128)] = hcore[h]
    for j in range(4):
        right, left = turn_lanes(hside[0], -32 * j), turn_lanes(hside[1], 96 - 32 * j)
        lev[LEAD + j * quarter : LEAD + (j + 1) * quarter, cols:fw] = jnp.where(
            qlane < 32, right, jnp.where(qlane >= 96, left, 0.0)
        )
    for v, r0 in ((0, top), (1, 8)):
        for q in range(2):
            for h in range(2):
                lev[r0 : r0 + 8, lanes_of(q, h) : lanes_of(q, h) + 128] = hvert[v, q, h]
        lev[r0 : r0 + 8, cols:fw] = merge(hcorn[v, 0], hcorn[v, 1])

    brows = rows // RATIO
    per = crows * RATIO // rows
    nest = brows * tiles
    nested = nest // crows
    ct = tile // per
    cm = lax.rem(tile, per)

    def avg_copy(k, kind):
        if kind == 0:
            src, to = avgs.at[k], ct
            dst = avgr.at[k, pl.ds(pl.multiple_of(LEAD + cm * brows, 8), brows), :]
        elif kind == 1:
            src, to = avgs.at[k, brows - 8 : brows, :], ct + 1
            dst = avgr.at[k, 8:16, :]
        else:
            src, to = avgs.at[k, 0:8, :], ct - 1
            dst = avgr.at[k, LEAD + crows : LEAD + crows + 8, :]
        return pltpu.make_async_remote_copy(
            src_ref=src, dst_ref=dst, send_sem=i_s.at[8 + k if kind == 0 else 2 * kind + k], recv_sem=v_rs.at[k, kind],
            device_id=dev(plane, to, side), device_id_type=MESH,
        )

    def avg_goes(kind):
        if kind == 0:
            return tile > 0
        if kind == 1:
            return jnp.logical_and(cm == per - 1, ct + 1 < nested)
        return jnp.logical_and(cm == 0, ct > 0)

    ways = v_rs.shape[1]

    def avg_send(k):
        for kind in range(ways):
            pl.when(avg_goes(kind))(lambda kind=kind: avg_copy(k, kind).start())

    def avg_wait(k):
        def wait(kind, dst):
            pltpu.make_async_remote_copy(
                src_ref=dst, dst_ref=dst, send_sem=i_s.at[8], recv_sem=v_rs.at[k, kind],
                device_id=dev(plane, tile, side), device_id_type=MESH,
            ).wait_recv()

        pl.when(tile == 0)(lambda: wait(0, avgr.at[k, LEAD + brows : LEAD + per * brows, :]))
        pl.when(tile > 0)(lambda: wait(0, avgr.at[k, LEAD : LEAD + per * brows, :]))
        if ways == 1:
            return
        pl.when(tile > 0)(lambda: wait(1, avgr.at[k, 8:16, :]))
        pl.when(tile < nested - 1)(lambda: wait(2, avgr.at[k, LEAD + crows : LEAD + crows + 8, :]))

    def edge_copy():
        return pltpu.make_async_remote_copy(
            src_ref=edges, dst_ref=edger, send_sem=i_s.at[10], recv_sem=v_rs.at[2, 0],
            device_id=dev(plane, nested, side), device_id_type=MESH,
        )

    ends = nested < tiles
    is_last = tile == tiles - 1

    def push(s_ref, g_c, g_r, k_c, k_r, which):
        for b in which:
            here, up = s_ref[b : b + 8, :], s_ref[b - 1 : b + 7, :]
            g_c[b : b + 8, :] -= k_c[b : b + 8, :] * (here - pltpu.roll(here, 1, 1))
            g_r[b : b + 8, :] -= k_r[b : b + 8, :] * (here - up)

    def spread(g_c, g_r, b):
        east = g_c[b : b + 8, :]
        return (pltpu.roll(east, east.shape[1] - 1, 1) - east) + (
            g_r[b + 1 : b + 9, :] - g_r[b : b + 8, :]
        )

    def means(x):
        parts = jnp.concatenate(split2(x), axis=0).astype(BF16)
        sums = jnp.dot(parts, amat[...], preferred_element_type=F32)
        return sums[0 : x.shape[0]] + sums[x.shape[0] :]

    def block_means(k, sums):
        for j in range(cw // 128):
            work[j] = sums[:, j * 128 : (j + 1) * 128]
            avgs[k, :, j * 128 : (j + 1) * 128] = sum(
                work[j, pl.ds(i, brows, stride=RATIO), :] for i in range(RATIO)
            )
        avg_send(k)

        @pl.when(tile == 0)
        def _():
            avgr[k, LEAD : LEAD + brows, :] = avgs[k]

    lane = iota((1, fw), 1)
    odd, upper = lane % 2 == 1, lane % 4 >= 2

    def lane_means(x):
        x = x + jnp.where(odd, pltpu.roll(x, 1, 1), pltpu.roll(x, fw - 1, 1))
        x = x + jnp.where(upper, pltpu.roll(x, 2, 1), pltpu.roll(x, fw - 2, 1))
        return x * (1.0 / (RATIO * RATIO))

    erow = iota((16, fw), 0)

    def step(k, carry, keep=False):
        c0, g0, h1 = carry

        lev[LEAD - 1 : LEAD, :] = jnp.where(tile == 0, c0, lev[LEAD - 1 : LEAD, :])
        if ends:
            esum[k] = lev[top - 8 : top, :]
        mean = lane_means(jnp.sum(lev[LEAD : LEAD + RATIO, :], axis=0, keepdims=True))
        g0 = g0 - kc0 * (c0 - pltpu.roll(c0, RATIO, 1))
        h1 = h1 - kr1 * (mean - c0)
        c0 = c0 - ((pltpu.roll(g0, fw - RATIO, 1) - g0) + h1)
        push(lev, gc, gr, kc, kr, strips)
        for b in strips:
            old = lev[b : b + 8, :]
            new = old - spread(gc, gr, b)
            lev[b : b + 8, :] = new
            if LEAD <= b < top:
                r = slice(b - LEAD, b - LEAD + 8)
                if keep:
                    first = k == 0
                    peak_o[r, :] = jnp.maximum(
                        jnp.where(first, old[:, 0:cols], peak_o[r, :]), new[:, 0:cols]
                    )
                    total[r, :] = jnp.where(first, old, total[r, :]) + new
                else:
                    peak_o[r, :] = jnp.maximum(peak_o[r, :], new[:, 0:cols])
        return c0, g0, h1

    zero = jnp.zeros((1, fw), F32)
    carry = lax.fori_loop(
        0, STEPS - 2, functools.partial(step, keep=True), (join3(wide, 0), zero, zero), unroll=True
    )
    sums = means(total[...])
    carry = step(STEPS - 2, carry)
    block_means(0, sums)
    block_means(1, means(lev[LEAD:top, :]))
    carry = step(STEPS - 1, carry)
    if ends:
        @pl.when(is_last)
        def _():
            sums = jnp.zeros(erow.shape, F32)
            for k in range(STEPS):
                above = jnp.sum(esum[k, 0:4, :], axis=0, keepdims=True)
                below = jnp.sum(esum[k, 4:8, :], axis=0, keepdims=True)
                sums = jnp.where(erow == 2 * k, above, jnp.where(erow == 2 * k + 1, below, sums))
            edges[...] = means(sums)
            edge_copy().start()
    surf_o[...] = lev[LEAD:top, 0:cols]

    @pl.when(tile >= nested)
    def _():
        if ends:
            pl.when(tile == nested)(lambda: edge_copy().wait_recv())
        erows = iota((16, cw), 0)
        crow = iota((8, cw), 0)

        def cstep(k, carry):
            def edge(i):
                return jnp.sum(jnp.where(erows == 2 * k + i, edger[...], 0.0), axis=0, keepdims=True)

            @pl.when(tile == nested)
            def _():
                clev[LEAD - 8 : LEAD, :] = jnp.where(crow == 7, edge(0), clev[LEAD - 8 : LEAD, :])
                clev[LEAD : LEAD + 8, :] = jnp.where(crow == 0, edge(1), clev[LEAD : LEAD + 8, :])

            push(clev, cgc, cgr, ckc, ckr, cstrips)
            for b in cstrips:
                clev[b : b + 8, :] -= spread(cgc, cgr, b)
            return carry

        lax.fori_loop(0, STEPS, cstep, 0)
        coarse_o[...] = clev[LEAD : LEAD + crows, 0:ccols]

    @pl.when(tile < nested)
    def _():
        c0, g0, h1 = carry
        narrow = RATIO * jnp.dot(stack3([c0, h1]), amat[...], preferred_element_type=F32)
        avg_wait(0)
        avg_wait(1)
        for b in range(LEAD, LEAD + crows + 8, 8):
            clev[b : b + 8, :] = avgr[0, b - 1 : b + 7, :] + avgr[1, b - 1 : b + 7, :]
        clev[LEAD - 1 : LEAD, :] = avgr[0, LEAD - 2 : LEAD - 1, :] + avgr[1, LEAD - 2 : LEAD - 1, :]
        inner = range(LEAD, LEAD + crows + 8, 8)
        push(clev, cgc, cgr, ckc, ckr, inner)

        @pl.when(tile == 0)
        def _():
            cgr[LEAD + 1 : LEAD + 2, :] = join3(narrow, 1)

        for b in range(LEAD, LEAD + crows, 8):
            new = avgr[1, b - 1 : b + 7, :] - spread(cgc, cgr, b)
            coarse_o[b - LEAD : b - LEAD + 8, :] = new[:, 0:ccols]

        @pl.when(tile == 0)
        def _():
            coarse_o[0:1, :] = join3(narrow, 0)[:, 0:ccols]

    slip_copy.wait_send()
    rest = pl.ds(0, owners - 1)
    for h in range(2):
        pair_copy(send.at[h, rest], recv.at[h, rest], a_ss.at[h], a_rs.at[h, 0], me).wait_send()
    pair_copy(mrecv.at[rest], mrecv.at[rest], m_ss.at[0], m_rs.at[0], me).wait_send()
    landed(hcore, 5, 8).wait_send()
    for kind, v, dst, n in [(1, 0, hvert.at[0], 0), (1, 1, hvert.at[1], 1), (0, 0, hside, 2)] + [
        (2, v, hcorn.at[v], 3 + v) for v in range(2)
    ]:
        pl.when(goes(kind, v, 1))(lambda dst=dst, n=n: landed(dst, n, 8).wait_send())
    for k in range(2):
        for kind in range(ways):
            pl.when(avg_goes(kind))(lambda k=k, kind=kind: avg_copy(k, kind).wait_send())
    if ends:
        pl.when(is_last)(lambda: edge_copy().wait_send())


def store(peak, surf, coarse, peak_h, surf_h, coarse_h, sems):
    pairs = [(peak, peak_h), (surf, surf_h), (coarse, coarse_h)]
    copies = [pltpu.make_async_copy(src, dst, sems.at[i]) for i, (src, dst) in enumerate(pairs)]
    for copy in copies:
        copy.start()
    for copy in copies:
        copy.wait()


def shards(dims, green, row_owner, row_index, row_fault, slip, depth, wet, coarse_depth, coarse_start):
    planes, tiles, cols_n, subs_n = dims
    owners = tiles * cols_n * subs_n
    entries, cols = green.shape
    rows = depth.shape[0]
    crows, ccols = coarse_depth.shape
    capacity = max(2, (2 * entries + owners - 1) // owners)
    capp = (capacity + 15) // 16 * 16
    packs = owners // (128 // capp)
    hw = cols // planes
    i32 = lambda *shape: pltpu.VMEM(shape, jnp.int32)
    ways = 3 if tiles * (rows // RATIO) // crows > 1 else 1
    fw, cw = cols + 128, ccols + 128
    high, chigh = rows + 32, crows + 32
    vmem = lambda *shape: pltpu.VMEM(shape, F32)
    dma = pltpu.SemaphoreType.DMA
    keep = lambda x: pltpu.with_memory_space_constraint(x, pltpu.HBM)
    results = pl.pallas_call(
        functools.partial(kernel, dims),
        out_shape=(
            jax.ShapeDtypeStruct((rows, cols), F32),
            jax.ShapeDtypeStruct((rows, cols), F32),
            jax.ShapeDtypeStruct((crows, ccols), F32),
        ),
        in_specs=[pl.BlockSpec(memory_space=pltpu.HBM)] * 9,
        out_specs=(pl.BlockSpec(memory_space=pltpu.VMEM),) * 3,
        scratch_shapes=[
            pltpu.VMEM((entries, hw), BF16), i32(1, entries), i32(1, entries), i32(1, entries),
            vmem(1, slip.shape[0]), vmem(rows, cols), i32(rows, cols),
            pltpu.VMEM((owners * capp, entries), BF16), vmem(owners, entries),
            pltpu.VMEM((2, owners, capp, 128), BF16),
            pltpu.VMEM((2, owners, capp, 128), BF16),
            vmem(owners, 1, 128), vmem(owners, 1, 128),
            vmem(8, 128), vmem(8, 128), vmem(4 * rows, 128),
            pltpu.VMEM((packs, 4 * rows, 128), BF16),
            vmem(rows + 8, cols + 256), vmem(2, rows + 8, 128), vmem(2, rows + 8, 128), vmem(2, 8, cols + 256),
            vmem(2, 2, 8, 128),
            vmem(2, 2 * rows, 128), vmem(2, rows, 128), vmem(2, rows // 4, 128), vmem(2, rows // 4, 128), vmem(2, 2, 2, 8, 128),
            vmem(2, 2, 8, 128),
        ]
        + [vmem(high, fw)] * 6
        + [vmem(chigh, cw)] * 6
        + [
            pltpu.VMEM((fw, cw), BF16), pltpu.VMEM((cw, fw), BF16),
            vmem(cw // 128, rows, 128),
            vmem(rows, fw), vmem(2, rows // RATIO, cw), vmem(2, chigh, cw),
            vmem(STEPS, 8, fw), vmem(16, cw), vmem(16, cw),
            dma((11,)), dma((2,)), dma((2, packs)), dma((1,)), dma((packs,)), dma((2,)), dma((8,)), dma((6,)),
            dma((9,)), dma((3, ways)), pltpu.SemaphoreType.REGULAR((tiles + 1,)),
        ],
        compiler_params=pltpu.CompilerParams(
            collective_id=0, has_side_effects=True, vmem_limit_bytes=48 * 1024 * 1024
        ),
    )(
        keep(green), keep(row_owner.reshape(1, entries)), keep(row_index.reshape(1, entries)),
        keep(row_fault.reshape(1, entries)), keep(slip.reshape(1, -1)), keep(depth), keep(wet), keep(coarse_depth), keep(coarse_start),
    )
    return pl.pallas_call(
        store,
        out_shape=tuple(jax.ShapeDtypeStruct(x.shape, F32) for x in results),
        in_specs=[pl.BlockSpec(memory_space=pltpu.VMEM)] * 3,
        out_specs=(pl.BlockSpec(memory_space=pltpu.HBM),) * 3,
        scratch_shapes=[dma((3,))],
        compiler_params=pltpu.CompilerParams(vmem_limit_bytes=1024 * 1024),
    )(*results)


def solution(mesh):
    dims = tuple(mesh.shape[a] for a in ("scen", "tile", "col", "sub"))
    return jax.shard_map(
        functools.partial(shards, dims),
        mesh=mesh,
        in_specs=(
            P(("tile", "col", "sub"), None),
            P(("tile", "col", "sub"), None),
            P(("tile", "col", "sub")),
            P(("tile", "col", "sub")),
            P(("scen", "tile", "col", "sub")),
            P("tile", ("col", "sub")),
            P("tile", ("col", "sub")),
            P("tile", ("col", "sub")),
            P(("scen", "tile"), ("col", "sub")),
        ),
        out_specs=(
            P(("scen", "tile"), ("col", "sub")),
            P(("scen", "tile"), ("col", "sub")),
            P(("scen", "tile"), ("col", "sub")),
        ),
        check_vma=False,
    )
```
